32 devices in a mesh: az: 16 (over z, y, x), rad: 2 (over core).
Axes of the slice: x: 2, y: 2, z: 4, core: 2. Of those that a mesh axis runs over, the one named last changes fastest.
Arguments:
- state: float32 [5, 2, 512, 256], P(None, None, 'az', 'rad'), as said below
- shifts: int32 [256], P('rad'), may hold values from 4 to 96, as said below
Outputs:
- state_out: float32 [5, 2, 512, 256], P(None, None, 'az', 'rad')
The draws below stay inside these ranges and needn't reach their ends.
Inputs may be any that keep to these rules, and one draw needn't show every extreme that they name: `state`: density lies between 0.3 and 3, each velocity component (momentum over density) between -1 and 1, and energy exceeds the kinetic energy by at least 0.8 times density. `shifts`: both 4 and 96 occur.
All inputs are finite; a program needn't handle non-finite values.
Results may differ from the reference program's by a relative error of at most 0.0003.
Values sent between devices are 32-bit elements; how exact they have to be, the bound alone decides.
A program may use at most 64 MiB of HBM per device.

```python
import jax
import jax.numpy as jnp
from jax import lax

ZL = 2
STEPS = 2
SMIN = 4
SMAX = 96
NPHI = 512
NR = 256


def draw_state(key, part):
    shape = (ZL, NPHI, NR)
    key_density = jax.random.fold_in(key, 1)
    key_speed = jax.random.fold_in(key, 2)
    key_heat = jax.random.fold_in(key, 3)
    density = jnp.exp(jax.random.uniform(key_density, shape, jnp.float32, jnp.log(0.5), jnp.log(2.0)))
    speeds = jax.random.uniform(key_speed, (3,) + shape, jnp.float32, -1.0, 1.0)
    heat = jax.random.uniform(key_heat, shape, jnp.float32, 1.0, 2.0)
    momenta = density[None] * speeds
    energy = density * (heat + 0.5 * jnp.sum(speeds * speeds, axis=0))
    return jnp.concatenate([density[None], momenta, energy[None]], axis=0)


def draw_shifts(key, part):
    base = jax.random.randint(jax.random.fold_in(key, 11), (NR,), SMIN, SMAX + 1, dtype=jnp.int32)
    places = jax.random.permutation(jax.random.fold_in(key, 12), NR)[:6]
    planted = jnp.array([SMIN, 23, 42, 61, 80, SMAX], dtype=jnp.int32)
    return base.at[places].set(planted)


def setup_inputs(seed: int = 0) -> dict:
    key_of = jax.random.split(jax.random.key(seed), 3)
    state = draw_state(jax.random.fold_in(key_of[2], 71), 0)
    shifts = draw_shifts(jax.random.fold_in(key_of[2], 71), 0)
    return {"state": state, "shifts": shifts}


GAMMA_GAS = 1.4
COURANT_RADIAL = 0.15
COURANT_AZIMUTH = 0.15
VISCOSITY_COEF = 1.0


def cut(array, start, stop, axis):
    return lax.slice_in_dim(array, start, stop, axis=axis)


def van_leer(left_diff, right_diff):
    product = left_diff * right_diff
    positive = product > 0
    safe_sum = jnp.where(positive, left_diff + right_diff, 1.0)
    return jnp.where(positive, 2.0 * product / safe_sum, 0.0)


def transport(strip, axis, component, courant):
    length = strip.shape[axis] - 4
    velocity = strip[component:component + 1] / strip[0:1]
    diffs = cut(strip, 1, length + 4, axis) - cut(strip, 0, length + 3, axis)
    slopes = van_leer(cut(diffs, 0, length + 2, axis), cut(diffs, 1, length + 3, axis))
    left_state = cut(strip, 1, length + 2, axis) + 0.5 * cut(slopes, 0, length + 1, axis)
    right_state = cut(strip, 2, length + 3, axis) - 0.5 * cut(slopes, 1, length + 2, axis)
    face_speed = 0.5 * (cut(velocity, 1, length + 2, axis) + cut(velocity, 2, length + 3, axis))
    flux = jnp.maximum(face_speed, 0.0) * left_state + jnp.minimum(face_speed, 0.0) * right_state
    return -courant * (cut(flux, 1, length + 1, axis) - cut(flux, 0, length, axis))


def pressure_push(strip, axis, component, courant):
    length = strip.shape[axis] - 4
    density = strip[0:1]
    momenta = strip[1:4]
    speed = strip[component:component + 1] / density
    pressure = (GAMMA_GAS - 1.0) * (strip[4:5] - 0.5 * jnp.sum(momenta * momenta, axis=0, keepdims=True) / density)
    compress = jnp.minimum(cut(speed, 2, length + 4, axis) - cut(speed, 0, length + 2, axis), 0.0)
    total = cut(pressure, 1, length + 3, axis) + VISCOSITY_COEF * cut(density, 1, length + 3, axis) * compress * compress
    work = total * cut(speed, 1, length + 3, axis)
    gradient = 0.5 * (cut(total, 2, length + 2, axis) - cut(total, 0, length, axis))
    work_div = 0.5 * (cut(work, 2, length + 2, axis) - cut(work, 0, length, axis))
    zeros = jnp.zeros_like(gradient)
    pieces = [zeros, zeros, zeros, zeros, -courant * work_div]
    pieces[component] = -courant * gradient
    return jnp.concatenate(pieces, axis=0)


def hydro(state, az_strip, rad_strip):
    return state + transport(az_strip, 2, 2, COURANT_AZIMUTH) + transport(rad_strip, 3, 1, COURANT_RADIAL)


def viscous(state, az_strip, rad_strip):
    return state + pressure_push(az_strip, 2, 2, COURANT_AZIMUTH) + pressure_push(rad_strip, 3, 1, COURANT_RADIAL)


def strips(state):
    az_strip = jnp.pad(state, ((0, 0), (0, 0), (2, 2), (0, 0)), mode="wrap")
    rad_strip = jnp.pad(state, ((0, 0), (0, 0), (0, 0), (2, 2)), mode="edge")
    return az_strip, rad_strip


def rotate(state, shifts):
    total = state.shape[2]
    index = (jnp.arange(total, dtype=jnp.int32)[:, None] - shifts[None, :].astype(jnp.int32)) % total
    index = jnp.broadcast_to(index.astype(jnp.int32), state.shape)
    return jnp.take_along_axis(state, index, axis=2)


def reference(state, shifts):
    for step in range(STEPS):
        az_strip, rad_strip = strips(state)
        state = hydro(state, az_strip, rad_strip)
        state = rotate(state, shifts)
        az_strip, rad_strip = strips(state)
        state = viscous(state, az_strip, rad_strip)
    return state
```

```python
import functools

import jax
import jax.numpy as jnp
from jax import lax
from jax.experimental import pallas as pl
from jax.experimental.pallas import tpu as pltpu
from jax.sharding import PartitionSpec as P

STEPS = 2
SMIN = 4
SMAX = 96
EDGE = 4
TILE = 8

GAMMA_GAS = 1.4
COURANT_RADIAL = 0.15
COURANT_AZIMUTH = 0.15
VISCOSITY_COEF = 1.0


def up(x, axis):
    return pltpu.roll(x, x.shape[axis] - 1, axis)


def down(x, axis):
    return pltpu.roll(x, 1, axis)


def face_speeds(velocity, axis, courant):
    face = (0.5 * courant) * (velocity + up(velocity, axis))
    return jnp.maximum(face, 0.0), jnp.minimum(face, 0.0)


def advect(field, speeds, axis):
    low = field - down(field, axis)
    high = up(low, axis)
    product = low * high
    positive = product > 0
    half = jnp.where(positive, product / jnp.where(positive, low + high, 1.0), 0.0)
    flux = speeds[0] * (field + half) + speeds[1] * up(field - half, axis)
    return flux - down(flux, axis)


def push(pressure, density, speed, axis, courant):
    compress = jnp.minimum(up(speed, axis) - down(speed, axis), 0.0)
    total = pressure + VISCOSITY_COEF * density * compress * compress
    work = total * speed
    scale = -0.5 * courant
    return scale * (up(total, axis) - down(total, axis)), scale * (up(work, axis) - down(work, axis))


def shifted(window, shift_left, rows, longest):
    bits = longest.bit_length()
    x = window
    for bit in reversed(range(bits)):
        stride = 1 << bit
        left = stride - 1
        if stride >= TILE:
            keep = -(-(rows + left) // TILE) * TILE
            chosen = min(keep, x.shape[0] - stride)
            mask = (jnp.broadcast_to(shift_left, (chosen, shift_left.shape[1])) & stride) != 0
            y = jnp.where(mask, x[stride : stride + chosen], x[:chosen])
            x = y if chosen == keep else jnp.concatenate([y, x[chosen:keep]], axis=0)
        else:
            mask = (jnp.broadcast_to(shift_left, x.shape) & stride) != 0
            x = jnp.where(mask, pltpu.roll(x, x.shape[0] - stride, 0), x)
    return x[:rows]


def kernel(n_az, n_rad, x_in, shifts, out, *scratch):
    (x, load_sem, A, W0, W1, O0, O1, L0, R0, L1, R1, L2, R2, state_send, state_recv, gather_send, gather_recv,
     side_send, side_recv) = scratch
    fields, depth, width, lanes = x.shape
    behind = SMAX + EDGE
    whole = behind // width
    tail = behind % width
    tail_rows = -(-tail // TILE) * TILE
    group = whole + 1
    base = group * width
    first_row = width - tail_rows
    me = lax.axis_index("az")
    place = lax.rem(me, group)
    position = lax.axis_index("rad")

    def az(by):
        return {"az": lax.rem(me + by + n_az, n_az)}

    def member(by):
        return {"az": me - place + lax.rem(place + by + group, group)}

    def rad(by):
        return {"rad": position + by}

    barrier = pltpu.get_barrier_semaphore()
    MESH = pl.DeviceIdType.MESH
    load = pltpu.make_async_copy(x_in, x, load_sem)
    load.start()
    for by in (1, -1, -group):
        pl.semaphore_signal(barrier, inc=1, device_id=az(by), device_id_type=MESH)
    for h in range(1, group):
        pl.semaphore_signal(barrier, inc=1, device_id=member(h), device_id_type=MESH)

    has_left = position > 0
    has_right = position < n_rad - 1

    @pl.when(has_left)
    def _():
        pl.semaphore_signal(barrier, inc=1, device_id=rad(-1), device_id_type=MESH)

    @pl.when(has_right)
    def _():
        pl.semaphore_signal(barrier, inc=1, device_id=rad(1), device_id_type=MESH)

    load.wait()
    A[:, :, TILE : TILE + width, :] = x[...]
    beside_me = (position + n_rad - 1) // n_rad + (2 * n_rad - 2 - position) // n_rad
    pl.semaphore_wait(barrier, group + 2 + beside_me)

    def remote(src, dst, send, recv, where):
        return pltpu.make_async_remote_copy(
            src_ref=src, dst_ref=dst, send_sem=send, recv_sem=recv, device_id=where, device_id_type=MESH
        )

    def ring_copies(z):
        return [
            remote(x.at[:, z, width - TILE : width], A.at[:, z, 0:TILE],
                   state_send.at[0, z], state_recv.at[0, z], az(1)),
            remote(x.at[:, z, 0:TILE], A.at[:, z, TILE + width : 2 * TILE + width],
                   state_send.at[1, z], state_recv.at[1, z], az(-1)),
        ]

    def side_copies(phase, src, left_dst, right_dst, z):
        to_right = remote(src.at[:, z], left_dst.at[:, z], side_send.at[phase, 0, z],
                          side_recv.at[phase, 0, z], rad(1))
        to_left = remote(src.at[:, z], right_dst.at[:, z], side_send.at[phase, 1, z],
                         side_recv.at[phase, 1, z], rad(-1))
        return to_right, to_left

    def start_side(*args):
        to_right, to_left = side_copies(*args)

        @pl.when(has_right)
        def _():
            to_right.start()

        @pl.when(has_left)
        def _():
            to_left.start()

    def await_side(*args):
        to_right, to_left = side_copies(*args)

        @pl.when(has_left)
        def _():
            to_right.wait_recv()

        @pl.when(has_right)
        def _():
            to_left.wait_recv()

    def end_side(*args):
        to_right, to_left = side_copies(*args)

        @pl.when(has_right)
        def _():
            to_right.wait_send()

        @pl.when(has_left)
        def _():
            to_left.wait_send()

    windows = (W0, W1)
    rotated = (O0, O1)
    sides = ((x, L0, R0), (O0, L1, R1), (O1, L2, R2))

    def gather_copies(step, f, z):
        W = windows[step]
        own, back = W.at[f, z, base : base + width], W.at[f, z, 0:width]
        sems = lambda h: (gather_send.at[step, h, f, z], gather_recv.at[step, h, f, z])
        onward = remote(own, back, *sems(0), az(group))
        inside = []
        for h in range(1, group):
            dst = W.at[f, z, base - h * width : base - (h - 1) * width]
            inside.append([remote(src, dst, *sems(h), member(h)) for src in (own, back)])
        return onward, inside

    def send_own(step, f, z):
        onward, inside = gather_copies(step, f, z)
        onward.start()
        for h in range(1, group):

            @pl.when(place + h < group)
            def _():
                inside[h - 1][0].start()

    def pass_on(step, f, z):
        onward, inside = gather_copies(step, f, z)
        onward.wait_recv()
        for h in range(1, group):

            @pl.when(place + h >= group)
            def _():
                inside[h - 1][1].start()

    def edges(own, left, right):
        rows = own.shape[0]
        lane = lax.broadcasted_iota(jnp.int32, (rows, lanes), 1)
        at = jnp.full((rows, lanes), position, jnp.int32)
        left = jnp.where(at == 0, jnp.broadcast_to(own[:, 0:1], own.shape), left)
        right = jnp.where(at == n_rad - 1, jnp.broadcast_to(own[:, lanes - 1 : lanes], own.shape), right)
        return jnp.where(lane < lanes // 2, right, left)

    def wide(own, beside):
        return jnp.concatenate([own, beside], axis=1)

    def hydro(step, z, strip, beside):
        rows = slice(TILE, TILE + width)
        tall = [strip(f) for f in range(fields)]
        az_speeds = face_speeds(tall[2] / tall[0], 0, COURANT_AZIMUTH)
        broad = [wide(tall[f][rows], beside(f, tall[f][rows])) for f in range(fields)]
        rad_speeds = face_speeds(broad[1] / broad[0], 1, COURANT_RADIAL)
        for f in range(fields):
            along = advect(tall[f], az_speeds, 0)[rows]
            across = advect(broad[f], rad_speeds, 1)[:, :lanes]
            windows[step][f, z, base : base + width, :] = tall[f][rows] - along - across
            send_own(step, f, z)

    def viscous(z, state, extended):
        rho, mr, mp, mz, energy = state
        own = slice(None) if extended else slice(0, lanes)
        inverse = 1.0 / rho
        pressure = (GAMMA_GAS - 1.0) * (energy - 0.5 * (mr * mr + mp * mp + mz * mz) * inverse)
        az_m, az_e = push(pressure[:, own], rho[:, own], (mp * inverse)[:, own], 0, COURANT_AZIMUTH)
        rad_m, rad_e = push(pressure, rho, mr * inverse, 1, COURANT_RADIAL)
        return [
            rho[:, own],
            mr[:, own] + rad_m[:, own],
            mp[:, own] + az_m,
            mz[:, own],
            energy[:, own] + az_e + rad_e[:, own],
        ]

    count = width + 2 * EDGE

    for z in range(depth):
        for copy in ring_copies(z):
            copy.start()
    for z in range(depth):
        start_side(0, *sides[0], z)
    for z in range(depth):
        for copy in ring_copies(z):
            copy.wait_recv()
        await_side(0, *sides[0], z)
        hydro(0, z, lambda f: A[f, z], lambda f, own: edges(own, L0[f, z], R0[f, z]))

    for step in range(STEPS):
        for z in range(depth):
            for f in range(fields):
                pass_on(step, f, z)
        O, L, R = sides[step + 1]
        for z in range(depth):
            for f in range(fields):
                for copies in gather_copies(step, f, z)[1]:
                    copies[0].wait_recv()
                start = base - first_row - EDGE
                O[f, z] = shifted(windows[step][f, z, first_row:], start - shifts[...], count, start - SMIN)
            start_side(step + 1, O, L, R, z)
        for z in range(depth):
            await_side(step + 1, O, L, R, z)
            state = [wide(O[f, z], edges(O[f, z], L[f, z], R[f, z])) for f in range(fields)]
            if step == STEPS - 1:
                new = viscous(z, state, False)
                for f in range(fields):
                    out[f, z] = new[f][EDGE : EDGE + width]
            else:
                new = viscous(z, state, True)
                A_rows = slice(TILE - EDGE, TILE - EDGE + count)
                for f in range(fields):
                    A[f, z, A_rows, :] = new[f][:, :lanes]
                hydro(
                    step + 1,
                    z,
                    lambda f: A[f, z],
                    lambda f, own: edges(own, *[new[f][EDGE : EDGE + width, lanes:]] * 2),
                )

    for z in range(depth):
        for copy in ring_copies(z):
            copy.wait_send()
        for phase in range(STEPS + 1):
            end_side(phase, *sides[phase], z)
        for step in range(STEPS):
            for f in range(fields):
                onward, inside = gather_copies(step, f, z)
                onward.wait_send()
                for copies in inside:
                    copies[0].wait_send()


def body(mesh, state, shifts):
    n_az, n_rad = mesh.shape["az"], mesh.shape["rad"]
    fields, depth, width, lanes = state.shape
    behind = SMAX + EDGE
    group = behind // width + 1
    window = (group + 1) * width
    count = width + 2 * EDGE
    vmem = lambda rows: pltpu.VMEM((fields, depth, rows, lanes), jnp.float32)
    dma = pltpu.SemaphoreType.DMA
    return pl.pallas_call(
        functools.partial(kernel, n_az, n_rad),
        out_shape=pltpu.VMEM(state.shape, state.dtype),
        in_specs=[pl.BlockSpec(memory_space=pl.ANY), pl.BlockSpec(memory_space=pltpu.VMEM)],
        out_specs=pl.BlockSpec(memory_space=pltpu.VMEM),
        scratch_shapes=[
            vmem(width),
            dma(()),
            vmem(width + 2 * TILE),
            vmem(window),
            vmem(window),
            vmem(count),
            vmem(count),
            vmem(width),
            vmem(width),
            vmem(count),
            vmem(count),
            vmem(count),
            vmem(count),
            dma((2, depth)),
            dma((2, depth)),
            dma((STEPS, group, fields, depth)),
            dma((STEPS, group, fields, depth)),
            dma((STEPS + 1, 2, depth)),
            dma((STEPS + 1, 2, depth)),
        ],
        compiler_params=pltpu.CompilerParams(collective_id=0, has_side_effects=True),
    )(state, shifts.reshape(1, -1))


GROUPS = 4


def lane_rows(x, shift):
    return pltpu.roll(x, shift % x.shape[1], 1)


def regroup(parts, lane):
    size = parts[0].shape[1] // GROUPS
    low = (lane & (2 * size)) == 0
    even = (lane & size) == 0
    a = [None] * GROUPS
    for g in range(2):
        p, q = parts[g], parts[g + 2]
        a[g] = jnp.where(low, p, lane_rows(q, 2 * size))
        a[g + 2] = jnp.where(low, lane_rows(p, 2 * size), q)
    out = []
    for g in (0, 2):
        p, q = a[g], a[g + 1]
        out.append(jnp.where(even, p, lane_rows(q, size)))
        out.append(jnp.where(even, lane_rows(p, -size), q))
    return out


def fold(x, lane, row):
    half = x.shape[1] // 2
    stay = (lane < half) == (row < TILE // 2)
    return jnp.where(stay, x, lane_rows(pltpu.roll(x, TILE // 2, 0), half))


def advect_all(state):
    rho, mr, mp = state[0], state[1], state[2]
    inverse = 1.0 / rho
    az_speeds = face_speeds(mp * inverse, 1, COURANT_AZIMUTH)
    rad_speeds = face_speeds(mr * inverse, 0, COURANT_RADIAL)

    def step(field):
        return field - advect(field, az_speeds, 1) - advect(field, rad_speeds, 0)

    return step


def push_all(state):
    rho, mr, mp, mz, energy = state
    inverse = 1.0 / rho
    pressure = (GAMMA_GAS - 1.0) * (energy - 0.5 * (mr * mr + mp * mp + mz * mz) * inverse)
    az_m, az_e = push(pressure, rho, mp * inverse, 1, COURANT_AZIMUTH)
    rad_m, rad_e = push(pressure, rho, mr * inverse, 0, COURANT_RADIAL)
    return mr + rad_m, mp + az_m, energy + az_e + rad_e


def turned_kernel(n_az, n_rad, x_in, shifts, out, *scratch):
    (x, T4, EP, EV, W4, WE, other, SC, PA, PB, PE, RA, RB, RE, load_sem, shift_sem, swap_sem, own_send, own_recv,
     side_send, side_recv, last_send, last_recv, pass_send, pass_recv, back_send, back_recv) = scratch
    fields, depth, width, lanes = x.shape
    blocks = n_az // (depth * n_rad)
    tiles = lanes // TILE
    rows = 4 * TILE
    MESH = pl.DeviceIdType.MESH
    me = lax.axis_index("az")
    core = lax.axis_index("rad")
    half = lax.rem(me, n_rad)
    layer = lax.rem(me // n_rad, depth)
    block = me // (n_rad * depth)
    place = (half * blocks + block) * 2 + core
    partner = {"rad": 1 - core}
    here = half == core

    def remote(src, dst, send, recv, where):
        return pltpu.make_async_remote_copy(
            src_ref=src, dst_ref=dst, send_sem=send, recv_sem=recv, device_id=where, device_id_type=MESH
        )

    loads = [pltpu.make_async_copy(x_in.at[:, l], x.at[:, l], load_sem.at[l]) for l in range(depth)]
    for load in loads:
        load.start()
    barrier = pltpu.get_barrier_semaphore()
    for k in range(1, n_az):
        pl.semaphore_signal(
            barrier, inc=1, device_id={"az": lax.rem(me + k, n_az), "rad": half}, device_id_type=MESH
        )
    pl.semaphore_signal(barrier, inc=1, device_id=partner, device_id_type=MESH)

    lane = lax.broadcasted_iota(jnp.int32, (TILE, lanes), 1)
    row = lax.broadcasted_iota(jnp.int32, (TILE, lanes), 0)
    group = lane // width

    for l in range(depth):
        loads[l].wait()
        T4[l, 1 : tiles + 1] = x[0:4, l].reshape(4 * width, lanes).T.reshape(tiles, TILE, lanes)
    energy = x[4].reshape(depth * width, lanes)
    turned = jnp.concatenate([energy] * (lanes // (depth * width)), axis=0).T.reshape(tiles, TILE, lanes)
    for l in range(depth):
        for m in range(tiles // GROUPS):
            packed = turned[GROUPS * m] if l == 0 else lane_rows(turned[GROUPS * m], -width * l)
            for g in range(1, GROUPS):
                packed = jnp.where(group == g, lane_rows(turned[GROUPS * m + g], width * (g - l)), packed)
            EP[l, 1 + m] = packed

    def pad(l, to, tile_from, energy_from):
        T4[l, to[0]] = T4[l, tile_from]
        EP[l, to[1]] = EP[l, energy_from]

    @pl.when(core == 0)
    def _():
        for l in range(depth):
            pad(l, (0, 0), 1, 1)

    @pl.when(core == 1)
    def _():
        for l in range(depth):
            pad(l, (tiles + 1, blocks + 1), tiles, blocks)

    def energy_window(l, s, c):
        own = EP[l, 1 + s]
        if c == 0:
            EV[l, s, c] = lane_rows(jnp.where(group == GROUPS - 1, EP[l, s], own), width)
        else:
            EV[l, s, c] = lane_rows(jnp.where(group == 0, EP[l, s + 2], own), -width)

    late = ((0, 0), (blocks - 1, 1))
    for l in range(depth):
        for s in range(blocks):
            for c in range(2):
                if (s, c) not in late:
                    energy_window(l, s, c)

    senders = jnp.where(here, 2 * (n_az // n_rad - 1) + 1, 2 * (n_az // n_rad) + 1)
    pl.semaphore_wait(barrier, senders)

    swap_shift = remote(shifts, other, shift_sem.at[0], shift_sem.at[1], partner)
    swap_shift.start()

    def swaps(l, up):
        src = (tiles, blocks) if up else (1, 1)
        dst = (0, 0) if up else (tiles + 1, blocks + 1)
        return [
            remote(T4.at[l, src[0]], T4.at[l, dst[0]], swap_sem.at[0, l], swap_sem.at[1, l], partner),
            remote(EP.at[l, src[1]], EP.at[l, dst[1]], swap_sem.at[2, l], swap_sem.at[3, l], partner),
        ]

    @pl.when(core == 0)
    def _():
        for l in range(depth):
            for copy in swaps(l, True):
                copy.start()

    @pl.when(core == 1)
    def _():
        for l in range(depth):
            for copy in swaps(l, False):
                copy.start()

    targets = [(ks, kl, kc) for ks in (2, 1, 3, 0) for kl in (1, 0) for kc in (1, 0)]

    def target(ks, kl, kc):
        s = lax.rem(block + ks, blocks)
        l = lax.rem(layer + kl, depth)
        c = lax.rem(core + kc, 2)
        return s, l, c, {"az": (s * depth + l) * n_rad + core, "rad": c}

    def send(kind, index):
        ks, kl, kc = targets[index]
        s, l, c, where = target(ks, kl, kc)
        if kind == "own":
            src, dst = T4.at[l, pl.ds(GROUPS * s + 1 + 2 * c, 2)], W4.at[me, pl.ds(1, 2)]
            sems = own_send.at[index], own_recv.at[me]
        elif kind == "side":
            src, dst = T4.at[l, GROUPS * s + 5 * c], W4.at[me, 3 * c]
            sems = side_send.at[index], side_recv.at[me]
        else:
            src, dst = EV.at[l, s, c], WE.at[me]
            sems = last_send.at[index], last_recv.at[me]
        across = remote(src, dst, *sems, where)
        if (ks, kl, kc) != (0, 0, 0):
            return across, None
        return across, pltpu.make_async_copy(src, dst, sems[1])

    def start(kind):
        for index in range(len(targets)):
            across, within = send(kind, index)
            if within is None:
                across.start()
            else:

                @pl.when(here)
                def _():
                    within.start()

                @pl.when(jnp.logical_not(here))
                def _():
                    across.start()

    def end(kind):
        for index in range(len(targets)):
            across, within = send(kind, index)
            if within is None:
                across.wait_send()
            else:

                @pl.when(jnp.logical_not(here))
                def _():
                    across.wait_send()

    start("own")
    for l in range(depth):
        for copy in swaps(l, True):
            copy.wait_recv()
    start("side")
    for l in range(depth):
        for s, c in late:
            energy_window(l, s, c)
    start("last")

    swap_shift.wait_recv()
    first = jnp.full((1, lanes), core, jnp.int32) == 0
    mine, theirs = shifts[...], other[...]
    for c in range(2):
        part = jnp.where(first, mine if c == 0 else theirs, theirs if c == 0 else mine)
        table = jnp.broadcast_to(part.astype(jnp.float32), (lanes, lanes)).T.astype(jnp.int32)
        SC[TILE + c * lanes : TILE + (c + 1) * lanes] = table
    SC[0:TILE] = jnp.zeros((TILE, lanes), jnp.int32)
    SC[TILE + 2 * lanes :] = jnp.zeros((TILE, lanes), jnp.int32)
    amount = SC[pl.ds(pl.multiple_of(place * 2 * TILE, TILE), rows)]

    def passes(i):
        return remote(W4.at[i, 2 - core], W4.at[i, 3 * core], pass_send.at[i], pass_recv.at[i], partner)

    def arrived(dst, recv):
        return pltpu.make_async_copy(dst, dst, recv)

    for k in range(n_az):
        i = lax.rem(me + k, n_az)
        arrived(W4.at[i, pl.ds(1, 2)], own_recv.at[i]).wait()
        passes(i).start()

    wide_lane = lax.broadcasted_iota(jnp.int32, (rows, lanes), 1)
    source = (wide_lane - amount) & (lanes - 1)
    inside = wide_lane >= amount

    def rotate(field):
        chunks = [field[:, v * lanes : (v + 1) * lanes] for v in range(GROUPS)]
        turned = [jnp.take_along_axis(chunk, source, axis=1) for chunk in chunks]
        return jnp.concatenate(
            [jnp.where(inside, turned[v], turned[v - 1]) for v in range(GROUPS)], axis=1
        )

    total = GROUPS * lanes
    at = jnp.full((TILE, total), place, jnp.int32)
    lowest = at == 0
    highest = at == 2 * blocks * n_rad - 1

    def edged(field):
        low = jnp.broadcast_to(field[TILE : TILE + 1], (TILE, total))
        high = jnp.broadcast_to(field[3 * TILE - 1 : 3 * TILE], (TILE, total))
        return jnp.concatenate(
            [
                jnp.where(lowest, low, field[:TILE]),
                field[TILE : 3 * TILE],
                jnp.where(highest, high, field[3 * TILE :]),
            ],
            axis=0,
        )

    for k in range(n_az):
        i = lax.rem(me + k, n_az)
        arrived(W4.at[i, 3 * core], side_recv.at[i]).wait()
    for i in range(n_az):
        passes(i).wait_recv()

    columns = []
    for v in range(GROUPS):
        parts = [W4[GROUPS * v + b].reshape(rows, lanes) for b in range(GROUPS)]
        columns.append(regroup(parts, wide_lane))
    state = [edged(jnp.concatenate([columns[v][f] for v in range(GROUPS)], axis=1)) for f in range(4)]
    step = advect_all(state)
    state = [edged(rotate(step(field))) for field in state]

    for k in range(n_az):
        i = lax.rem(me + k, n_az)
        arrived(WE.at[i], last_recv.at[i]).wait()
    columns = [regroup([WE[GROUPS * v + b] for b in range(GROUPS)], lane) for v in range(GROUPS)]
    field = jnp.concatenate(
        [jnp.concatenate([columns[v][w] for v in range(GROUPS)], axis=1) for w in range(4)], axis=0
    )
    state.append(edged(rotate(step(edged(field)))))

    mr, mp, en = push_all(state)
    state = [edged(field) for field in (state[0], mr, mp, state[3], en)]
    step = advect_all(state)

    def back(kind, k):
        i = lax.rem(me + k, n_az)
        P, R = ((PA, RA), (PB, RB), (PE, RE))[kind]
        src, dst = P.at[i], R.at[layer, block, core]
        sems = back_send.at[kind, k], back_recv.at[kind, (layer * blocks + block) * 2 + core]
        across = remote(src, dst, *sems, {"az": i, "rad": half})
        return across, None if k else pltpu.make_async_copy(src, dst, sems[1])

    def start_back(kind):
        for k in [*range(1, n_az), 0]:
            across, within = back(kind, k)
            if within is None:
                across.start()
            else:

                @pl.when(here)
                def _():
                    within.start()

                @pl.when(jnp.logical_not(here))
                def _():
                    across.start()

    def pack(P, fields2):
        for v in range(GROUPS):
            cut = slice(v * lanes, (v + 1) * lanes)
            parts = [f[(1 + t) * TILE : (2 + t) * TILE, cut] for f in fields2 for t in range(2)]
            for b, part in enumerate(regroup(parts, lane)):
                P[GROUPS * v + b] = part

    rho, mz = (edged(rotate(step(state[f]))) for f in (0, 3))
    pack(PA, (rho, mz))
    start_back(0)
    mr, mp, en = (edged(rotate(step(state[f]))) for f in (1, 2, 4))
    mr, mp, en = push_all((rho, mr, mp, mz, en))
    pack(PB, (mr, mp))
    start_back(1)
    for v in range(GROUPS // 2):
        cuts = [slice(u * lanes, (u + 1) * lanes) for u in (v, v + GROUPS // 2)]
        parts = [en[(1 + t) * TILE : (2 + t) * TILE, cut] for cut in cuts for t in range(2)]
        for b, part in enumerate(regroup(parts, lane)):
            folded = fold(part, lane, row)
            PE[GROUPS * v + b] = folded[: TILE // 2]
            PE[GROUPS * (v + GROUPS // 2) + b] = folded[TILE // 2 :]
    start_back(2)

    def returned(kind, l, s, c):
        R = (RA, RB, RE)[kind]
        return arrived(R.at[l, s, c], back_recv.at[kind, (l * blocks + s) * 2 + c])

    everyone = [(l, s, c) for l in range(depth) for s in range(blocks) for c in range(2)]
    for kind in range(2):
        for l, s, c in everyone:
            returned(kind, l, s, c).wait()
    for l in range(depth):
        pieces = []
        for s in range(blocks):
            for c in range(2):
                A, B = RA[l, s, c], RB[l, s, c]
                for t in range(2):
                    a = lane_rows(A, width if t == 0 else -width)
                    b = lane_rows(B, width if t == 0 else -width)
                    if t == 0:
                        p, q, r, u = A, b, B, a
                    else:
                        p, q, r, u = a, B, b, A
                    pieces.append(
                        jnp.where(group < 2, jnp.where(group == 0, p, q), jnp.where(group == 2, r, u))
                    )
        block_out = jnp.concatenate(pieces, axis=0).T
        for f in range(4):
            out[f, l] = block_out[f * width : (f + 1) * width]
    for l, s, c in everyone:
        returned(2, l, s, c).wait()
    pieces = []
    for s in range(blocks):
        both = [fold(jnp.concatenate([RE[l, s, 0], RE[l, s, 1]], axis=0), lane, row) for l in range(depth)]
        for g in range(GROUPS):
            piece = lane_rows(both[0], -width * g)
            for l in range(1, depth):
                piece = jnp.where(group == l, lane_rows(both[l], width * (l - g)), piece)
            pieces.append(piece)
    block_out = jnp.concatenate(pieces, axis=0).T
    for l in range(depth):
        out[4, l] = block_out[l * width : (l + 1) * width]

    swap_shift.wait_send()
    for l in range(depth):
        for copy in swaps(l, True):
            copy.wait_send()
    for kind in ("own", "side", "last"):
        end(kind)
    for i in range(n_az):
        passes(i).wait_send()
    for kind in range(3):
        for k in range(n_az):
            across, within = back(kind, k)
            if within is None:
                across.wait_send()
            else:

                @pl.when(jnp.logical_not(here))
                def _():
                    across.wait_send()


def turned_body(mesh, state, shifts):
    n_az, n_rad = mesh.shape["az"], mesh.shape["rad"]
    fields, depth, width, lanes = state.shape
    blocks = n_az // (depth * n_rad)
    tiles = lanes // TILE
    vmem = lambda *shape: pltpu.VMEM(shape, jnp.float32)
    dma = pltpu.SemaphoreType.DMA
    tile = (TILE, lanes)
    return pl.pallas_call(
        functools.partial(turned_kernel, n_az, n_rad),
        out_shape=pltpu.VMEM(state.shape, state.dtype),
        in_specs=[pl.BlockSpec(memory_space=pl.ANY), pl.BlockSpec(memory_space=pltpu.VMEM)],
        out_specs=pl.BlockSpec(memory_space=pltpu.VMEM),
        scratch_shapes=[
            vmem(fields, depth, width, lanes),
            vmem(depth, tiles + 2, *tile),
            vmem(depth, blocks + 2, *tile),
            vmem(depth, blocks, 2, *tile),
            vmem(n_az, 4, *tile),
            vmem(n_az, *tile),
            pltpu.VMEM((1, lanes), jnp.int32),
            pltpu.VMEM((2 * lanes + 2 * TILE, lanes), jnp.int32),
            vmem(n_az, *tile),
            vmem(n_az, *tile),
            vmem(n_az, TILE // 2, lanes),
            vmem(depth, blocks, 2, *tile),
            vmem(depth, blocks, 2, *tile),
            vmem(depth, blocks, 2, TILE // 2, lanes),
            dma((depth,)),
            dma((2,)),
            dma((4, depth)),
            dma((n_az,)),
            dma((n_az,)),
            dma((n_az,)),
            dma((n_az,)),
            dma((n_az,)),
            dma((n_az,)),
            dma((n_az,)),
            dma((n_az,)),
            dma((3, n_az)),
            dma((3, n_az)),
        ],
        compiler_params=pltpu.CompilerParams(collective_id=0, has_side_effects=True),
    )(state, shifts.reshape(1, -1))


def turns(mesh, state):
    n_az, n_rad = mesh.shape["az"], mesh.shape["rad"]
    fields, depth, width, lanes = state.shape
    tiles = lanes // TILE
    return (
        n_rad == 2
        and fields == GROUPS + 1
        and width * GROUPS == lanes
        and n_az == GROUPS * GROUPS
        and n_az % (depth * n_rad) == 0
        and tiles == GROUPS * (n_az // (depth * n_rad))
        and depth * width <= lanes
        and SMAX <= lanes
    )


def choose(mesh, state, shifts):
    return (turned_body if turns(mesh, state) else body)(mesh, state, shifts)


def solution(mesh):
    in_specs = (P(None, None, "az", "rad"), P("rad"))
    out_specs = P(None, None, "az", "rad")
    return jax.shard_map(
        functools.partial(choose, mesh), mesh=mesh, in_specs=in_specs, out_specs=out_specs, check_vma=False
    )
```

```python
import functools

import jax
import jax.numpy as jnp
from jax import lax
from jax.experimental import pallas as pl
from jax.experimental.pallas import tpu as pltpu
from jax.sharding import PartitionSpec as P

STEPS = 2
SMIN = 4
SMAX = 96
EDGE = 4
TILE = 8

GAMMA_GAS = 1.4
COURANT_RADIAL = 0.15
COURANT_AZIMUTH = 0.15
VISCOSITY_COEF = 1.0


def up(x, axis):
    return pltpu.roll(x, x.shape[axis] - 1, axis)


def down(x, axis):
    return pltpu.roll(x, 1, axis)


def face_speeds(velocity, axis, courant):
    face = (0.5 * courant) * (velocity + up(velocity, axis))
    return jnp.maximum(face, 0.0), jnp.minimum(face, 0.0)


def advect(field, speeds, axis):
    low = field - down(field, axis)
    high = up(low, axis)
    product = low * high
    positive = product > 0
    half = jnp.where(positive, product / jnp.where(positive, low + high, 1.0), 0.0)
    flux = speeds[0] * (field + half) + speeds[1] * up(field - half, axis)
    return flux - down(flux, axis)


def push(pressure, density, speed, axis, courant):
    compress = jnp.minimum(up(speed, axis) - down(speed, axis), 0.0)
    total = pressure + VISCOSITY_COEF * density * compress * compress
    work = total * speed
    scale = -0.5 * courant
    return scale * (up(total, axis) - down(total, axis)), scale * (up(work, axis) - down(work, axis))


def shifted(window, shift_left, rows, longest):
    bits = longest.bit_length()
    x = window
    for bit in reversed(range(bits)):
        stride = 1 << bit
        left = stride - 1
        if stride >= TILE:
            keep = -(-(rows + left) // TILE) * TILE
            chosen = min(keep, x.shape[0] - stride)
            mask = (jnp.broadcast_to(shift_left, (chosen, shift_left.shape[1])) & stride) != 0
            y = jnp.where(mask, x[stride : stride + chosen], x[:chosen])
            x = y if chosen == keep else jnp.concatenate([y, x[chosen:keep]], axis=0)
        else:
            mask = (jnp.broadcast_to(shift_left, x.shape) & stride) != 0
            x = jnp.where(mask, pltpu.roll(x, x.shape[0] - stride, 0), x)
    return x[:rows]


def kernel(n_az, n_rad, x_in, shifts, out, *scratch):
    (x, load_sem, A, W0, W1, O0, O1, L0, R0, L1, R1, L2, R2, state_send, state_recv, gather_send, gather_recv,
     side_send, side_recv) = scratch
    fields, depth, width, lanes = x.shape
    behind = SMAX + EDGE
    whole = behind // width
    tail = behind % width
    tail_rows = -(-tail // TILE) * TILE
    group = whole + 1
    base = group * width
    first_row = width - tail_rows
    me = lax.axis_index("az")
    place = lax.rem(me, group)
    position = lax.axis_index("rad")

    def az(by):
        return {"az": lax.rem(me + by + n_az, n_az)}

    def member(by):
        return {"az": me - place + lax.rem(place + by + group, group)}

    def rad(by):
        return {"rad": position + by}

    barrier = pltpu.get_barrier_semaphore()
    MESH = pl.DeviceIdType.MESH
    load = pltpu.make_async_copy(x_in, x, load_sem)
    load.start()
    for by in (1, -1, -group):
        pl.semaphore_signal(barrier, inc=1, device_id=az(by), device_id_type=MESH)
    for h in range(1, group):
        pl.semaphore_signal(barrier, inc=1, device_id=member(h), device_id_type=MESH)

    has_left = position > 0
    has_right = position < n_rad - 1

    @pl.when(has_left)
    def _():
        pl.semaphore_signal(barrier, inc=1, device_id=rad(-1), device_id_type=MESH)

    @pl.when(has_right)
    def _():
        pl.semaphore_signal(barrier, inc=1, device_id=rad(1), device_id_type=MESH)

    load.wait()
    A[:, :, TILE : TILE + width, :] = x[...]
    beside_me = (position + n_rad - 1) // n_rad + (2 * n_rad - 2 - position) // n_rad
    pl.semaphore_wait(barrier, group + 2 + beside_me)

    def remote(src, dst, send, recv, where):
        return pltpu.make_async_remote_copy(
            src_ref=src, dst_ref=dst, send_sem=send, recv_sem=recv, device_id=where, device_id_type=MESH
        )

    def ring_copies(z):
        return [
            remote(x.at[:, z, width - TILE : width], A.at[:, z, 0:TILE],
                   state_send.at[0, z], state_recv.at[0, z], az(1)),
            remote(x.at[:, z, 0:TILE], A.at[:, z, TILE + width : 2 * TILE + width],
                   state_send.at[1, z], state_recv.at[1, z], az(-1)),
        ]

    def side_copies(phase, src, left_dst, right_dst, z):
        to_right = remote(src.at[:, z], left_dst.at[:, z], side_send.at[phase, 0, z],
                          side_recv.at[phase, 0, z], rad(1))
        to_left = remote(src.at[:, z], right_dst.at[:, z], side_send.at[phase, 1, z],
                         side_recv.at[phase, 1, z], rad(-1))
        return to_right, to_left

    def start_side(*args):
        to_right, to_left = side_copies(*args)

        @pl.when(has_right)
        def _():
            to_right.start()

        @pl.when(has_left)
        def _():
            to_left.start()

    def await_side(*args):
        to_right, to_left = side_copies(*args)

        @pl.when(has_left)
        def _():
            to_right.wait_recv()

        @pl.when(has_right)
        def _():
            to_left.wait_recv()

    def end_side(*args):
        to_right, to_left = side_copies(*args)

        @pl.when(has_right)
        def _():
            to_right.wait_send()

        @pl.when(has_left)
        def _():
            to_left.wait_send()

    windows = (W0, W1)
    rotated = (O0, O1)
    sides = ((x, L0, R0), (O0, L1, R1), (O1, L2, R2))

    def gather_copies(step, f, z):
        W = windows[step]
        own, back = W.at[f, z, base : base + width], W.at[f, z, 0:width]
        sems = lambda h: (gather_send.at[step, h, f, z], gather_recv.at[step, h, f, z])
        onward = remote(own, back, *sems(0), az(group))
        inside = []
        for h in range(1, group):
            dst = W.at[f, z, base - h * width : base - (h - 1) * width]
            inside.append([remote(src, dst, *sems(h), member(h)) for src in (own, back)])
        return onward, inside

    def send_own(step, f, z):
        onward, inside = gather_copies(step, f, z)
        onward.start()
        for h in range(1, group):

            @pl.when(place + h < group)
            def _():
                inside[h - 1][0].start()

    def pass_on(step, f, z):
        onward, inside = gather_copies(step, f, z)
        onward.wait_recv()
        for h in range(1, group):

            @pl.when(place + h >= group)
            def _():
                inside[h - 1][1].start()

    def edges(own, left, right):
        rows = own.shape[0]
        lane = lax.broadcasted_iota(jnp.int32, (rows, lanes), 1)
        at = jnp.full((rows, lanes), position, jnp.int32)
        left = jnp.where(at == 0, jnp.broadcast_to(own[:, 0:1], own.shape), left)
        right = jnp.where(at == n_rad - 1, jnp.broadcast_to(own[:, lanes - 1 : lanes], own.shape), right)
        return jnp.where(lane < lanes // 2, right, left)

    def wide(own, beside):
        return jnp.concatenate([own, beside], axis=1)

    def hydro(step, z, strip, beside):
        rows = slice(TILE, TILE + width)
        tall = [strip(f) for f in range(fields)]
        az_speeds = face_speeds(tall[2] / tall[0], 0, COURANT_AZIMUTH)
        broad = [wide(tall[f][rows], beside(f, tall[f][rows])) for f in range(fields)]
        rad_speeds = face_speeds(broad[1] / broad[0], 1, COURANT_RADIAL)
        for f in range(fields):
            along = advect(tall[f], az_speeds, 0)[rows]
            across = advect(broad[f], rad_speeds, 1)[:, :lanes]
            windows[step][f, z, base : base + width, :] = tall[f][rows] - along - across
            send_own(step, f, z)

    def viscous(z, state, extended):
        rho, mr, mp, mz, energy = state
        own = slice(None) if extended else slice(0, lanes)
        inverse = 1.0 / rho
        pressure = (GAMMA_GAS - 1.0) * (energy - 0.5 * (mr * mr + mp * mp + mz * mz) * inverse)
        az_m, az_e = push(pressure[:, own], rho[:, own], (mp * inverse)[:, own], 0, COURANT_AZIMUTH)
        rad_m, rad_e = push(pressure, rho, mr * inverse, 1, COURANT_RADIAL)
        return [
            rho[:, own],
            mr[:, own] + rad_m[:, own],
            mp[:, own] + az_m,
            mz[:, own],
            energy[:, own] + az_e + rad_e[:, own],
        ]

    count = width + 2 * EDGE

    for z in range(depth):
        for copy in ring_copies(z):
            copy.start()
    for z in range(depth):
        start_side(0, *sides[0], z)
    for z in range(depth):
        for copy in ring_copies(z):
            copy.wait_recv()
        await_side(0, *sides[0], z)
        hydro(0, z, lambda f: A[f, z], lambda f, own: edges(own, L0[f, z], R0[f, z]))

    for step in range(STEPS):
        for z in range(depth):
            for f in range(fields):
                pass_on(step, f, z)
        O, L, R = sides[step + 1]
        for z in range(depth):
            for f in range(fields):
                for copies in gather_copies(step, f, z)[1]:
                    copies[0].wait_recv()
                start = base - first_row - EDGE
                O[f, z] = shifted(windows[step][f, z, first_row:], start - shifts[...], count, start - SMIN)
            start_side(step + 1, O, L, R, z)
        for z in range(depth):
            await_side(step + 1, O, L, R, z)
            state = [wide(O[f, z], edges(O[f, z], L[f, z], R[f, z])) for f in range(fields)]
            if step == STEPS - 1:
                new = viscous(z, state, False)
                for f in range(fields):
                    out[f, z] = new[f][EDGE : EDGE + width]
            else:
                new = viscous(z, state, True)
                A_rows = slice(TILE - EDGE, TILE - EDGE + count)
                for f in range(fields):
                    A[f, z, A_rows, :] = new[f][:, :lanes]
                hydro(
                    step + 1,
                    z,
                    lambda f: A[f, z],
                    lambda f, own: edges(own, *[new[f][EDGE : EDGE + width, lanes:]] * 2),
                )

    for z in range(depth):
        for copy in ring_copies(z):
            copy.wait_send()
        for phase in range(STEPS + 1):
            end_side(phase, *sides[phase], z)
        for step in range(STEPS):
            for f in range(fields):
                onward, inside = gather_copies(step, f, z)
                onward.wait_send()
                for copies in inside:
                    copies[0].wait_send()


def body(mesh, state, shifts):
    n_az, n_rad = mesh.shape["az"], mesh.shape["rad"]
    fields, depth, width, lanes = state.shape
    behind = SMAX + EDGE
    group = behind // width + 1
    window = (group + 1) * width
    count = width + 2 * EDGE
    vmem = lambda rows: pltpu.VMEM((fields, depth, rows, lanes), jnp.float32)
    dma = pltpu.SemaphoreType.DMA
    return pl.pallas_call(
        functools.partial(kernel, n_az, n_rad),
        out_shape=pltpu.VMEM(state.shape, state.dtype),
        in_specs=[pl.BlockSpec(memory_space=pl.ANY), pl.BlockSpec(memory_space=pltpu.VMEM)],
        out_specs=pl.BlockSpec(memory_space=pltpu.VMEM),
        scratch_shapes=[
            vmem(width),
            dma(()),
            vmem(width + 2 * TILE),
            vmem(window),
            vmem(window),
            vmem(count),
            vmem(count),
            vmem(width),
            vmem(width),
            vmem(count),
            vmem(count),
            vmem(count),
            vmem(count),
            dma((2, depth)),
            dma((2, depth)),
            dma((STEPS, group, fields, depth)),
            dma((STEPS, group, fields, depth)),
            dma((STEPS + 1, 2, depth)),
            dma((STEPS + 1, 2, depth)),
        ],
        compiler_params=pltpu.CompilerParams(collective_id=0, has_side_effects=True),
    )(state, shifts.reshape(1, -1))


GROUPS = 4


def lane_rows(x, shift):
    return pltpu.roll(x, shift % x.shape[1], 1)


def regroup(parts, lane):
    size = parts[0].shape[1] // GROUPS
    low = (lane & (2 * size)) == 0
    even = (lane & size) == 0
    a = [None] * GROUPS
    for g in range(2):
        p, q = parts[g], parts[g + 2]
        a[g] = jnp.where(low, p, lane_rows(q, 2 * size))
        a[g + 2] = jnp.where(low, lane_rows(p, 2 * size), q)
    out = []
    for g in (0, 2):
        p, q = a[g], a[g + 1]
        out.append(jnp.where(even, p, lane_rows(q, size)))
        out.append(jnp.where(even, lane_rows(p, -size), q))
    return out


def fold(x, lane, row):
    half = x.shape[1] // 2
    stay = (lane < half) == (row < TILE // 2)
    return jnp.where(stay, x, lane_rows(pltpu.roll(x, TILE // 2, 0), half))


def advect_all(state):
    rho, mr, mp = state[0], state[1], state[2]
    inverse = 1.0 / rho
    az_speeds = face_speeds(mp * inverse, 1, COURANT_AZIMUTH)
    rad_speeds = face_speeds(mr * inverse, 0, COURANT_RADIAL)

    def step(field):
        return field - advect(field, az_speeds, 1) - advect(field, rad_speeds, 0)

    return step


def push_all(state):
    rho, mr, mp, mz, energy = state
    inverse = 1.0 / rho
    pressure = (GAMMA_GAS - 1.0) * (energy - 0.5 * (mr * mr + mp * mp + mz * mz) * inverse)
    az_m, az_e = push(pressure, rho, mp * inverse, 1, COURANT_AZIMUTH)
    rad_m, rad_e = push(pressure, rho, mr * inverse, 0, COURANT_RADIAL)
    return mr + rad_m, mp + az_m, energy + az_e + rad_e


def turned_kernel(n_az, n_rad, x_in, shifts, out, *scratch):
    (x, T4, EP, EV, W4, WE, other, SC, PA, PB, PE, RA, RB, RE, load_sem, shift_sem, swap_sem, own_send, own_recv,
     side_send, side_recv, last_send, last_recv, pass_send, pass_recv, back_send, back_recv) = scratch
    fields, depth, width, lanes = x.shape
    blocks = n_az // (depth * n_rad)
    tiles = lanes // TILE
    rows = 4 * TILE
    MESH = pl.DeviceIdType.MESH
    me = lax.axis_index("az")
    core = lax.axis_index("rad")
    half = lax.rem(me, n_rad)
    layer = lax.rem(me // n_rad, depth)
    block = me // (n_rad * depth)
    place = (half * blocks + block) * 2 + core
    partner = {"rad": 1 - core}
    here = half == core

    def remote(src, dst, send, recv, where):
        return pltpu.make_async_remote_copy(
            src_ref=src, dst_ref=dst, send_sem=send, recv_sem=recv, device_id=where, device_id_type=MESH
        )

    loads = [pltpu.make_async_copy(x_in.at[:, l], x.at[:, l], load_sem.at[l]) for l in range(depth)]
    for load in loads:
        load.start()
    barrier = pltpu.get_barrier_semaphore()
    for k in range(1, n_az):
        pl.semaphore_signal(
            barrier, inc=1, device_id={"az": lax.rem(me + k, n_az), "rad": half}, device_id_type=MESH
        )
    pl.semaphore_signal(barrier, inc=1, device_id=partner, device_id_type=MESH)

    lane = lax.broadcasted_iota(jnp.int32, (TILE, lanes), 1)
    row = lax.broadcasted_iota(jnp.int32, (TILE, lanes), 0)
    group = lane // width

    for l in range(depth):
        loads[l].wait()
        T4[l, 1 : tiles + 1] = x[0:4, l].reshape(4 * width, lanes).T.reshape(tiles, TILE, lanes)
    energy = x[4].reshape(depth * width, lanes)
    turned = jnp.concatenate([energy] * (lanes // (depth * width)), axis=0).T.reshape(tiles, TILE, lanes)
    for l in range(depth):
        for m in range(tiles // GROUPS):
            packed = turned[GROUPS * m] if l == 0 else lane_rows(turned[GROUPS * m], -width * l)
            for g in range(1, GROUPS):
                packed = jnp.where(group == g, lane_rows(turned[GROUPS * m + g], width * (g - l)), packed)
            EP[l, 1 + m] = packed

    def pad(l, to, tile_from, energy_from):
        T4[l, to[0]] = T4[l, tile_from]
        EP[l, to[1]] = EP[l, energy_from]

    @pl.when(core == 0)
    def _():
        for l in range(depth):
            pad(l, (0, 0), 1, 1)

    @pl.when(core == 1)
    def _():
        for l in range(depth):
            pad(l, (tiles + 1, blocks + 1), tiles, blocks)

    def energy_window(l, s, c):
        own = EP[l, 1 + s]
        if c == 0:
            EV[l, s, c] = lane_rows(jnp.where(group == GROUPS - 1, EP[l, s], own), width)
        else:
            EV[l, s, c] = lane_rows(jnp.where(group == 0, EP[l, s + 2], own), -width)

    late = ((0, 0), (blocks - 1, 1))
    for l in range(depth):
        for s in range(blocks):
            for c in range(2):
                if (s, c) not in late:
                    energy_window(l, s, c)

    senders = jnp.where(here, 2 * (n_az // n_rad - 1) + 1, 2 * (n_az // n_rad) + 1)
    pl.semaphore_wait(barrier, senders)

    swap_shift = remote(shifts, other, shift_sem.at[0], shift_sem.at[1], partner)
    swap_shift.start()

    def swaps(l, up):
        src = (tiles, blocks) if up else (1, 1)
        dst = (0, 0) if up else (tiles + 1, blocks + 1)
        return [
            remote(T4.at[l, src[0]], T4.at[l, dst[0]], swap_sem.at[0, l], swap_sem.at[1, l], partner),
            remote(EP.at[l, src[1]], EP.at[l, dst[1]], swap_sem.at[2, l], swap_sem.at[3, l], partner),
        ]

    @pl.when(core == 0)
    def _():
        for l in range(depth):
            for copy in swaps(l, True):
                copy.start()

    @pl.when(core == 1)
    def _():
        for l in range(depth):
            for copy in swaps(l, False):
                copy.start()

    targets = [(ks, kl, kc) for ks in (2, 1, 3, 0) for kl in (1, 0) for kc in (1, 0)]

    def target(ks, kl, kc):
        s = lax.rem(block + ks, blocks)
        l = lax.rem(layer + kl, depth)
        c = lax.rem(core + kc, 2)
        return s, l, c, {"az": (s * depth + l) * n_rad + core, "rad": c}

    def send(kind, index):
        ks, kl, kc = targets[index]
        s, l, c, where = target(ks, kl, kc)
        if kind == "own":
            src, dst = T4.at[l, pl.ds(GROUPS * s + 1 + 2 * c, 2)], W4.at[me, pl.ds(1, 2)]
            sems = own_send.at[index], own_recv.at[me]
        elif kind == "side":
            src, dst = T4.at[l, GROUPS * s + 5 * c], W4.at[me, 3 * c]
            sems = side_send.at[index], side_recv.at[me]
        else:
            src, dst = EV.at[l, s, c], WE.at[me]
            sems = last_send.at[index], last_recv.at[me]
        across = remote(src, dst, *sems, where)
        if (ks, kl, kc) != (0, 0, 0):
            return across, None
        return across, pltpu.make_async_copy(src, dst, sems[1])

    def start(kind):
        for index in range(len(targets)):
            across, within = send(kind, index)
            if within is None:
                across.start()
            else:

                @pl.when(here)
                def _():
                    within.start()

                @pl.when(jnp.logical_not(here))
                def _():
                    across.start()

    def end(kind):
        for index in range(len(targets)):
            across, within = send(kind, index)
            if within is None:
                across.wait_send()
            else:

                @pl.when(jnp.logical_not(here))
                def _():
                    across.wait_send()

    start("own")
    for l in range(depth):
        for copy in swaps(l, True):
            copy.wait_recv()
    start("side")
    for l in range(depth):
        for s, c in late:
            energy_window(l, s, c)
    start("last")

    swap_shift.wait_recv()
    first = jnp.full((1, lanes), core, jnp.int32) == 0
    mine, theirs = shifts[...], other[...]
    for c in range(2):
        part = jnp.where(first, mine if c == 0 else theirs, theirs if c == 0 else mine)
        table = jnp.broadcast_to(part.astype(jnp.float32), (lanes, lanes)).T.astype(jnp.int32)
        SC[TILE + c * lanes : TILE + (c + 1) * lanes] = table
    SC[0:TILE] = jnp.zeros((TILE, lanes), jnp.int32)
    SC[TILE + 2 * lanes :] = jnp.zeros((TILE, lanes), jnp.int32)
    amount = SC[pl.ds(pl.multiple_of(place * 2 * TILE, TILE), rows)]

    def passes(i):
        return remote(W4.at[i, 2 - core], W4.at[i, 3 * core], pass_send.at[i], pass_recv.at[i], partner)

    def arrived(dst, recv):
        return pltpu.make_async_copy(dst, dst, recv)

    for k in range(n_az):
        i = lax.rem(me + k, n_az)
        arrived(W4.at[i, pl.ds(1, 2)], own_recv.at[i]).wait()
        passes(i).start()

    wide_lane = lax.broadcasted_iota(jnp.int32, (rows, lanes), 1)
    source = (wide_lane - amount) & (lanes - 1)
    inside = wide_lane >= amount

    def rotate(field):
        chunks = [field[:, v * lanes : (v + 1) * lanes] for v in range(GROUPS)]
        turned = [jnp.take_along_axis(chunk, source, axis=1) for chunk in chunks]
        return jnp.concatenate(
            [jnp.where(inside, turned[v], turned[v - 1]) for v in range(GROUPS)], axis=1
        )

    total = GROUPS * lanes
    at = jnp.full((TILE, total), place, jnp.int32)
    lowest = at == 0
    highest = at == 2 * blocks * n_rad - 1

    def edged(field):
        low = jnp.broadcast_to(field[TILE : TILE + 1], (TILE, total))
        high = jnp.broadcast_to(field[3 * TILE - 1 : 3 * TILE], (TILE, total))
        return jnp.concatenate(
            [
                jnp.where(lowest, low, field[:TILE]),
                field[TILE : 3 * TILE],
                jnp.where(highest, high, field[3 * TILE :]),
            ],
            axis=0,
        )

    for k in range(n_az):
        i = lax.rem(me + k, n_az)
        arrived(W4.at[i, 3 * core], side_recv.at[i]).wait()
    for i in range(n_az):
        passes(i).wait_recv()

    columns = []
    for v in range(GROUPS):
        parts = [W4[GROUPS * v + b].reshape(rows, lanes) for b in range(GROUPS)]
        columns.append(regroup(parts, wide_lane))
    state = [edged(jnp.concatenate([columns[v][f] for v in range(GROUPS)], axis=1)) for f in range(4)]
    step = advect_all(state)
    state = [edged(rotate(step(field))) for field in state]

    for k in range(n_az):
        i = lax.rem(me + k, n_az)
        arrived(WE.at[i], last_recv.at[i]).wait()
    columns = [regroup([WE[GROUPS * v + b] for b in range(GROUPS)], lane) for v in range(GROUPS)]
    field = jnp.concatenate(
        [jnp.concatenate([columns[v][w] for v in range(GROUPS)], axis=1) for w in range(4)], axis=0
    )
    state.append(edged(rotate(step(edged(field)))))

    mr, mp, en = push_all(state)
    state = [edged(field) for field in (state[0], mr, mp, state[3], en)]
    step = advect_all(state)

    plane = n_az // GROUPS
    order = [(q, j) for q in range(GROUPS) for j in [*range(1, plane), 0]]

    def back(kind, q, j):
        i = q * plane + lax.rem(me + j, plane)
        P, R = ((PA, RA), (PB, RB), (PE, RE))[kind]
        src, dst = P.at[i], R.at[layer, block, core]
        sems = back_send.at[kind, q * plane + j], back_recv.at[kind, (layer * blocks + block) * 2 + core]
        across = remote(src, dst, *sems, {"az": i, "rad": half})
        return across, None if j else pltpu.make_async_copy(src, dst, sems[1])

    def stays(q):
        return jnp.logical_and(here, me // plane == q)

    def start_back(kind, q):
        for at_q, j in order:
            if at_q != q:
                continue
            across, within = back(kind, q, j)
            if within is None:
                across.start()
            else:

                @pl.when(stays(q))
                def _():
                    within.start()

                @pl.when(jnp.logical_not(stays(q)))
                def _():
                    across.start()

    def pack(P, fields2):
        for v in range(GROUPS):
            cut = slice(v * lanes, (v + 1) * lanes)
            parts = [f[(1 + t) * TILE : (2 + t) * TILE, cut] for f in fields2 for t in range(2)]
            for b, part in enumerate(regroup(parts, lane)):
                P[GROUPS * v + b] = part

    rho, mz = (edged(rotate(step(state[f]))) for f in (0, 3))
    pack(PA, (rho, mz))
    for q in range(GROUPS):
        start_back(0, q)
    mr, mp, en = (edged(rotate(step(state[f]))) for f in (1, 2, 4))
    mr, mp, en = push_all((rho, mr, mp, mz, en))
    pack(PB, (mr, mp))
    for v in range(GROUPS // 2):
        cuts = [slice(u * lanes, (u + 1) * lanes) for u in (v, v + GROUPS // 2)]
        parts = [en[(1 + t) * TILE : (2 + t) * TILE, cut] for cut in cuts for t in range(2)]
        for b, part in enumerate(regroup(parts, lane)):
            folded = fold(part, lane, row)
            PE[GROUPS * v + b] = folded[: TILE // 2]
            PE[GROUPS * (v + GROUPS // 2) + b] = folded[TILE // 2 :]
    for q in range(GROUPS):
        start_back(1, q)
        start_back(2, q)

    def returned(kind, l, s, c):
        R = (RA, RB, RE)[kind]
        return arrived(R.at[l, s, c], back_recv.at[kind, (l * blocks + s) * 2 + c])

    everyone = [(l, s, c) for l in range(depth) for s in range(blocks) for c in range(2)]
    for kind in range(2):
        for l, s, c in everyone:
            returned(kind, l, s, c).wait()
    for l in range(depth):
        pieces = []
        for s in range(blocks):
            for c in range(2):
                A, B = RA[l, s, c], RB[l, s, c]
                for t in range(2):
                    a = lane_rows(A, width if t == 0 else -width)
                    b = lane_rows(B, width if t == 0 else -width)
                    if t == 0:
                        p, q, r, u = A, b, B, a
                    else:
                        p, q, r, u = a, B, b, A
                    pieces.append(
                        jnp.where(group < 2, jnp.where(group == 0, p, q), jnp.where(group == 2, r, u))
                    )
        block_out = jnp.concatenate(pieces, axis=0).T
        for f in range(4):
            out[f, l] = block_out[f * width : (f + 1) * width]
    for l, s, c in everyone:
        returned(2, l, s, c).wait()
    pieces = []
    for s in range(blocks):
        both = [fold(jnp.concatenate([RE[l, s, 0], RE[l, s, 1]], axis=0), lane, row) for l in range(depth)]
        for g in range(GROUPS):
            piece = lane_rows(both[0], -width * g)
            for l in range(1, depth):
                piece = jnp.where(group == l, lane_rows(both[l], width * (l - g)), piece)
            pieces.append(piece)
    block_out = jnp.concatenate(pieces, axis=0).T
    for l in range(depth):
        out[4, l] = block_out[l * width : (l + 1) * width]

    swap_shift.wait_send()
    for l in range(depth):
        for copy in swaps(l, True):
            copy.wait_send()
    for kind in ("own", "side", "last"):
        end(kind)
    for i in range(n_az):
        passes(i).wait_send()
    for kind in range(3):
        for q, j in order:
            across, within = back(kind, q, j)
            if within is None:
                across.wait_send()
            else:

                @pl.when(jnp.logical_not(stays(q)))
                def _():
                    across.wait_send()


def turned_body(mesh, state, shifts):
    n_az, n_rad = mesh.shape["az"], mesh.shape["rad"]
    fields, depth, width, lanes = state.shape
    blocks = n_az // (depth * n_rad)
    tiles = lanes // TILE
    vmem = lambda *shape: pltpu.VMEM(shape, jnp.float32)
    dma = pltpu.SemaphoreType.DMA
    tile = (TILE, lanes)
    return pl.pallas_call(
        functools.partial(turned_kernel, n_az, n_rad),
        out_shape=pltpu.VMEM(state.shape, state.dtype),
        in_specs=[pl.BlockSpec(memory_space=pl.ANY), pl.BlockSpec(memory_space=pltpu.VMEM)],
        out_specs=pl.BlockSpec(memory_space=pltpu.VMEM),
        scratch_shapes=[
            vmem(fields, depth, width, lanes),
            vmem(depth, tiles + 2, *tile),
            vmem(depth, blocks + 2, *tile),
            vmem(depth, blocks, 2, *tile),
            vmem(n_az, 4, *tile),
            vmem(n_az, *tile),
            pltpu.VMEM((1, lanes), jnp.int32),
            pltpu.VMEM((2 * lanes + 2 * TILE, lanes), jnp.int32),
            vmem(n_az, *tile),
            vmem(n_az, *tile),
            vmem(n_az, TILE // 2, lanes),
            vmem(depth, blocks, 2, *tile),
            vmem(depth, blocks, 2, *tile),
            vmem(depth, blocks, 2, TILE // 2, lanes),
            dma((depth,)),
            dma((2,)),
            dma((4, depth)),
            dma((n_az,)),
            dma((n_az,)),
            dma((n_az,)),
            dma((n_az,)),
            dma((n_az,)),
            dma((n_az,)),
            dma((n_az,)),
            dma((n_az,)),
            dma((3, n_az)),
            dma((3, n_az)),
        ],
        compiler_params=pltpu.CompilerParams(collective_id=0, has_side_effects=True),
    )(state, shifts.reshape(1, -1))


def turns(mesh, state):
    n_az, n_rad = mesh.shape["az"], mesh.shape["rad"]
    fields, depth, width, lanes = state.shape
    tiles = lanes // TILE
    return (
        n_rad == 2
        and fields == GROUPS + 1
        and width * GROUPS == lanes
        and n_az == GROUPS * GROUPS
        and n_az % (depth * n_rad) == 0
        and tiles == GROUPS * (n_az // (depth * n_rad))
        and depth * width <= lanes
        and SMAX <= lanes
    )


def choose(mesh, state, shifts):
    return (turned_body if turns(mesh, state) else body)(mesh, state, shifts)


def solution(mesh):
    in_specs = (P(None, None, "az", "rad"), P("rad"))
    out_specs = P(None, None, "az", "rad")
    return jax.shard_map(
        functools.partial(choose, mesh), mesh=mesh, in_specs=in_specs, out_specs=out_specs, check_vma=False
    )
```

```python
import functools

import jax
import jax.numpy as jnp
from jax import lax
from jax.experimental import pallas as pl
from jax.experimental.pallas import tpu as pltpu
from jax.sharding import PartitionSpec as P

STEPS = 2
SMIN = 4
SMAX = 96
EDGE = 4
TILE = 8

GAMMA_GAS = 1.4
COURANT_RADIAL = 0.15
COURANT_AZIMUTH = 0.15
VISCOSITY_COEF = 1.0


def up(x, axis):
    return pltpu.roll(x, x.shape[axis] - 1, axis)


def down(x, axis):
    return pltpu.roll(x, 1, axis)


def face_speeds(velocity, axis, courant):
    face = (0.5 * courant) * (velocity + up(velocity, axis))
    return jnp.maximum(face, 0.0), jnp.minimum(face, 0.0)


def advect(field, speeds, axis):
    low = field - down(field, axis)
    high = up(low, axis)
    product = low * high
    positive = product > 0
    half = jnp.where(positive, product / jnp.where(positive, low + high, 1.0), 0.0)
    flux = speeds[0] * (field + half) + speeds[1] * up(field - half, axis)
    return flux - down(flux, axis)


def push(pressure, density, speed, axis, courant):
    compress = jnp.minimum(up(speed, axis) - down(speed, axis), 0.0)
    total = pressure + VISCOSITY_COEF * density * compress * compress
    work = total * speed
    scale = -0.5 * courant
    return scale * (up(total, axis) - down(total, axis)), scale * (up(work, axis) - down(work, axis))


def shifted(window, shift_left, rows, longest):
    bits = longest.bit_length()
    x = window
    for bit in reversed(range(bits)):
        stride = 1 << bit
        left = stride - 1
        if stride >= TILE:
            keep = -(-(rows + left) // TILE) * TILE
            chosen = min(keep, x.shape[0] - stride)
            mask = (jnp.broadcast_to(shift_left, (chosen, shift_left.shape[1])) & stride) != 0
            y = jnp.where(mask, x[stride : stride + chosen], x[:chosen])
            x = y if chosen == keep else jnp.concatenate([y, x[chosen:keep]], axis=0)
        else:
            mask = (jnp.broadcast_to(shift_left, x.shape) & stride) != 0
            x = jnp.where(mask, pltpu.roll(x, x.shape[0] - stride, 0), x)
    return x[:rows]


def kernel(n_az, n_rad, x_in, shifts, out, *scratch):
    (x, load_sem, A, W0, W1, O0, O1, L0, R0, L1, R1, L2, R2, state_send, state_recv, gather_send, gather_recv,
     side_send, side_recv) = scratch
    fields, depth, width, lanes = x.shape
    behind = SMAX + EDGE
    whole = behind // width
    tail = behind % width
    tail_rows = -(-tail // TILE) * TILE
    group = whole + 1
    base = group * width
    first_row = width - tail_rows
    me = lax.axis_index("az")
    place = lax.rem(me, group)
    position = lax.axis_index("rad")

    def az(by):
        return {"az": lax.rem(me + by + n_az, n_az)}

    def member(by):
        return {"az": me - place + lax.rem(place + by + group, group)}

    def rad(by):
        return {"rad": position + by}

    barrier = pltpu.get_barrier_semaphore()
    MESH = pl.DeviceIdType.MESH
    load = pltpu.make_async_copy(x_in, x, load_sem)
    load.start()
    for by in (1, -1, -group):
        pl.semaphore_signal(barrier, inc=1, device_id=az(by), device_id_type=MESH)
    for h in range(1, group):
        pl.semaphore_signal(barrier, inc=1, device_id=member(h), device_id_type=MESH)

    has_left = position > 0
    has_right = position < n_rad - 1

    @pl.when(has_left)
    def _():
        pl.semaphore_signal(barrier, inc=1, device_id=rad(-1), device_id_type=MESH)

    @pl.when(has_right)
    def _():
        pl.semaphore_signal(barrier, inc=1, device_id=rad(1), device_id_type=MESH)

    load.wait()
    A[:, :, TILE : TILE + width, :] = x[...]
    beside_me = (position + n_rad - 1) // n_rad + (2 * n_rad - 2 - position) // n_rad
    pl.semaphore_wait(barrier, group + 2 + beside_me)

    def remote(src, dst, send, recv, where):
        return pltpu.make_async_remote_copy(
            src_ref=src, dst_ref=dst, send_sem=send, recv_sem=recv, device_id=where, device_id_type=MESH
        )

    def ring_copies(z):
        return [
            remote(x.at[:, z, width - TILE : width], A.at[:, z, 0:TILE],
                   state_send.at[0, z], state_recv.at[0, z], az(1)),
            remote(x.at[:, z, 0:TILE], A.at[:, z, TILE + width : 2 * TILE + width],
                   state_send.at[1, z], state_recv.at[1, z], az(-1)),
        ]

    def side_copies(phase, src, left_dst, right_dst, z):
        to_right = remote(src.at[:, z], left_dst.at[:, z], side_send.at[phase, 0, z],
                          side_recv.at[phase, 0, z], rad(1))
        to_left = remote(src.at[:, z], right_dst.at[:, z], side_send.at[phase, 1, z],
                         side_recv.at[phase, 1, z], rad(-1))
        return to_right, to_left

    def start_side(*args):
        to_right, to_left = side_copies(*args)

        @pl.when(has_right)
        def _():
            to_right.start()

        @pl.when(has_left)
        def _():
            to_left.start()

    def await_side(*args):
        to_right, to_left = side_copies(*args)

        @pl.when(has_left)
        def _():
            to_right.wait_recv()

        @pl.when(has_right)
        def _():
            to_left.wait_recv()

    def end_side(*args):
        to_right, to_left = side_copies(*args)

        @pl.when(has_right)
        def _():
            to_right.wait_send()

        @pl.when(has_left)
        def _():
            to_left.wait_send()

    windows = (W0, W1)
    rotated = (O0, O1)
    sides = ((x, L0, R0), (O0, L1, R1), (O1, L2, R2))

    def gather_copies(step, f, z):
        W = windows[step]
        own, back = W.at[f, z, base : base + width], W.at[f, z, 0:width]
        sems = lambda h: (gather_send.at[step, h, f, z], gather_recv.at[step, h, f, z])
        onward = remote(own, back, *sems(0), az(group))
        inside = []
        for h in range(1, group):
            dst = W.at[f, z, base - h * width : base - (h - 1) * width]
            inside.append([remote(src, dst, *sems(h), member(h)) for src in (own, back)])
        return onward, inside

    def send_own(step, f, z):
        onward, inside = gather_copies(step, f, z)
        onward.start()
        for h in range(1, group):

            @pl.when(place + h < group)
            def _():
                inside[h - 1][0].start()

    def pass_on(step, f, z):
        onward, inside = gather_copies(step, f, z)
        onward.wait_recv()
        for h in range(1, group):

            @pl.when(place + h >= group)
            def _():
                inside[h - 1][1].start()

    def edges(own, left, right):
        rows = own.shape[0]
        lane = lax.broadcasted_iota(jnp.int32, (rows, lanes), 1)
        at = jnp.full((rows, lanes), position, jnp.int32)
        left = jnp.where(at == 0, jnp.broadcast_to(own[:, 0:1], own.shape), left)
        right = jnp.where(at == n_rad - 1, jnp.broadcast_to(own[:, lanes - 1 : lanes], own.shape), right)
        return jnp.where(lane < lanes // 2, right, left)

    def wide(own, beside):
        return jnp.concatenate([own, beside], axis=1)

    def hydro(step, z, strip, beside):
        rows = slice(TILE, TILE + width)
        tall = [strip(f) for f in range(fields)]
        az_speeds = face_speeds(tall[2] / tall[0], 0, COURANT_AZIMUTH)
        broad = [wide(tall[f][rows], beside(f, tall[f][rows])) for f in range(fields)]
        rad_speeds = face_speeds(broad[1] / broad[0], 1, COURANT_RADIAL)
        for f in range(fields):
            along = advect(tall[f], az_speeds, 0)[rows]
            across = advect(broad[f], rad_speeds, 1)[:, :lanes]
            windows[step][f, z, base : base + width, :] = tall[f][rows] - along - across
            send_own(step, f, z)

    def viscous(z, state, extended):
        rho, mr, mp, mz, energy = state
        own = slice(None) if extended else slice(0, lanes)
        inverse = 1.0 / rho
        pressure = (GAMMA_GAS - 1.0) * (energy - 0.5 * (mr * mr + mp * mp + mz * mz) * inverse)
        az_m, az_e = push(pressure[:, own], rho[:, own], (mp * inverse)[:, own], 0, COURANT_AZIMUTH)
        rad_m, rad_e = push(pressure, rho, mr * inverse, 1, COURANT_RADIAL)
        return [
            rho[:, own],
            mr[:, own] + rad_m[:, own],
            mp[:, own] + az_m,
            mz[:, own],
            energy[:, own] + az_e + rad_e[:, own],
        ]

    count = width + 2 * EDGE

    for z in range(depth):
        for copy in ring_copies(z):
            copy.start()
    for z in range(depth):
        start_side(0, *sides[0], z)
    for z in range(depth):
        for copy in ring_copies(z):
            copy.wait_recv()
        await_side(0, *sides[0], z)
        hydro(0, z, lambda f: A[f, z], lambda f, own: edges(own, L0[f, z], R0[f, z]))

    for step in range(STEPS):
        for z in range(depth):
            for f in range(fields):
                pass_on(step, f, z)
        O, L, R = sides[step + 1]
        for z in range(depth):
            for f in range(fields):
                for copies in gather_copies(step, f, z)[1]:
                    copies[0].wait_recv()
                start = base - first_row - EDGE
                O[f, z] = shifted(windows[step][f, z, first_row:], start - shifts[...], count, start - SMIN)
            start_side(step + 1, O, L, R, z)
        for z in range(depth):
            await_side(step + 1, O, L, R, z)
            state = [wide(O[f, z], edges(O[f, z], L[f, z], R[f, z])) for f in range(fields)]
            if step == STEPS - 1:
                new = viscous(z, state, False)
                for f in range(fields):
                    out[f, z] = new[f][EDGE : EDGE + width]
            else:
                new = viscous(z, state, True)
                A_rows = slice(TILE - EDGE, TILE - EDGE + count)
                for f in range(fields):
                    A[f, z, A_rows, :] = new[f][:, :lanes]
                hydro(
                    step + 1,
                    z,
                    lambda f: A[f, z],
                    lambda f, own: edges(own, *[new[f][EDGE : EDGE + width, lanes:]] * 2),
                )

    for z in range(depth):
        for copy in ring_copies(z):
            copy.wait_send()
        for phase in range(STEPS + 1):
            end_side(phase, *sides[phase], z)
        for step in range(STEPS):
            for f in range(fields):
                onward, inside = gather_copies(step, f, z)
                onward.wait_send()
                for copies in inside:
                    copies[0].wait_send()


def body(mesh, state, shifts):
    n_az, n_rad = mesh.shape["az"], mesh.shape["rad"]
    fields, depth, width, lanes = state.shape
    behind = SMAX + EDGE
    group = behind // width + 1
    window = (group + 1) * width
    count = width + 2 * EDGE
    vmem = lambda rows: pltpu.VMEM((fields, depth, rows, lanes), jnp.float32)
    dma = pltpu.SemaphoreType.DMA
    return pl.pallas_call(
        functools.partial(kernel, n_az, n_rad),
        out_shape=pltpu.VMEM(state.shape, state.dtype),
        in_specs=[pl.BlockSpec(memory_space=pl.ANY), pl.BlockSpec(memory_space=pltpu.VMEM)],
        out_specs=pl.BlockSpec(memory_space=pltpu.VMEM),
        scratch_shapes=[
            vmem(width),
            dma(()),
            vmem(width + 2 * TILE),
            vmem(window),
            vmem(window),
            vmem(count),
            vmem(count),
            vmem(width),
            vmem(width),
            vmem(count),
            vmem(count),
            vmem(count),
            vmem(count),
            dma((2, depth)),
            dma((2, depth)),
            dma((STEPS, group, fields, depth)),
            dma((STEPS, group, fields, depth)),
            dma((STEPS + 1, 2, depth)),
            dma((STEPS + 1, 2, depth)),
        ],
        compiler_params=pltpu.CompilerParams(collective_id=0, has_side_effects=True),
    )(state, shifts.reshape(1, -1))


GROUPS = 4


def lane_rows(x, shift):
    return pltpu.roll(x, shift % x.shape[1], 1)


def regroup(parts, lane):
    size = parts[0].shape[1] // GROUPS
    low = (lane & (2 * size)) == 0
    even = (lane & size) == 0
    a = [None] * GROUPS
    for g in range(2):
        p, q = parts[g], parts[g + 2]
        a[g] = jnp.where(low, p, lane_rows(q, 2 * size))
        a[g + 2] = jnp.where(low, lane_rows(p, 2 * size), q)
    out = []
    for g in (0, 2):
        p, q = a[g], a[g + 1]
        out.append(jnp.where(even, p, lane_rows(q, size)))
        out.append(jnp.where(even, lane_rows(p, -size), q))
    return out


def fold(x, lane, row):
    half = x.shape[1] // 2
    stay = (lane < half) == (row < TILE // 2)
    return jnp.where(stay, x, lane_rows(pltpu.roll(x, TILE // 2, 0), half))


def advect_all(state):
    rho, mr, mp = state[0], state[1], state[2]
    inverse = 1.0 / rho
    az_speeds = face_speeds(mp * inverse, 1, COURANT_AZIMUTH)
    rad_speeds = face_speeds(mr * inverse, 0, COURANT_RADIAL)

    def step(field):
        return field - advect(field, az_speeds, 1) - advect(field, rad_speeds, 0)

    return step


def push_all(state):
    rho, mr, mp, mz, energy = state
    inverse = 1.0 / rho
    pressure = (GAMMA_GAS - 1.0) * (energy - 0.5 * (mr * mr + mp * mp + mz * mz) * inverse)
    az_m, az_e = push(pressure, rho, mp * inverse, 1, COURANT_AZIMUTH)
    rad_m, rad_e = push(pressure, rho, mr * inverse, 0, COURANT_RADIAL)
    return mr + rad_m, mp + az_m, energy + az_e + rad_e


def turned_kernel(n_az, n_rad, x_in, shifts, out, *scratch):
    (x, T4, EP, M, W, other, SC, B, R, load_sem, shift_sem, swap_sem, out_send, out_recv, pass_send, pass_recv,
     back_send, back_recv) = scratch
    fields, depth, width, lanes = x.shape
    blocks = n_az // (depth * n_rad)
    tiles = lanes // TILE
    rows = 4 * TILE
    MESH = pl.DeviceIdType.MESH
    me = lax.axis_index("az")
    core = lax.axis_index("rad")
    half = lax.rem(me, n_rad)
    layer = lax.rem(me // n_rad, depth)
    block = me // (n_rad * depth)
    place = (half * blocks + block) * 2 + core
    partner = {"rad": 1 - core}
    here = half == core

    def remote(src, dst, send, recv, where):
        return pltpu.make_async_remote_copy(
            src_ref=src, dst_ref=dst, send_sem=send, recv_sem=recv, device_id=where, device_id_type=MESH
        )

    loads = [pltpu.make_async_copy(x_in.at[:, l], x.at[:, l], load_sem.at[l]) for l in range(depth)]
    for load in loads:
        load.start()
    barrier = pltpu.get_barrier_semaphore()
    for k in range(1, n_az):
        pl.semaphore_signal(
            barrier, inc=1, device_id={"az": lax.rem(me + k, n_az), "rad": half}, device_id_type=MESH
        )
    pl.semaphore_signal(barrier, inc=1, device_id=partner, device_id_type=MESH)

    lane = lax.broadcasted_iota(jnp.int32, (TILE, lanes), 1)
    row = lax.broadcasted_iota(jnp.int32, (TILE, lanes), 0)
    group = lane // width

    for l in range(depth):
        loads[l].wait()
        T4[l, 1 : tiles + 1] = x[0:4, l].reshape(4 * width, lanes).T.reshape(tiles, TILE, lanes)
    energy = x[4].reshape(depth * width, lanes)
    turned = jnp.concatenate([energy] * (lanes // (depth * width)), axis=0).T.reshape(tiles, TILE, lanes)
    for l in range(depth):
        for m in range(tiles // GROUPS):
            packed = turned[GROUPS * m] if l == 0 else lane_rows(turned[GROUPS * m], -width * l)
            for g in range(1, GROUPS):
                packed = jnp.where(group == g, lane_rows(turned[GROUPS * m + g], width * (g - l)), packed)
            EP[l, 1 + m] = packed

    def pad(l, to, tile_from, energy_from):
        T4[l, to[0]] = T4[l, tile_from]
        EP[l, to[1]] = EP[l, energy_from]

    @pl.when(core == 0)
    def _():
        for l in range(depth):
            pad(l, (0, 0), 1, 1)

    @pl.when(core == 1)
    def _():
        for l in range(depth):
            pad(l, (tiles + 1, blocks + 1), tiles, blocks)

    def stage(l, s, c):
        own = EP[l, 1 + s]
        if c == 0:
            M[l, s, c, 0] = lane_rows(jnp.where(group == GROUPS - 1, EP[l, s], own), width)
            M[l, s, c, 1:4] = T4[l, GROUPS * s : GROUPS * s + 3]
        else:
            M[l, s, c, 0:3] = T4[l, GROUPS * s + 3 : GROUPS * s + 6]
            M[l, s, c, 3] = lane_rows(jnp.where(group == 0, EP[l, s + 2], own), -width)

    late = ((0, 0), (blocks - 1, 1))
    for l in range(depth):
        for s in range(blocks):
            for c in range(2):
                if (s, c) not in late:
                    stage(l, s, c)

    senders = jnp.where(here, 2 * (n_az // n_rad - 1) + 1, 2 * (n_az // n_rad) + 1)
    pl.semaphore_wait(barrier, senders)

    swap_shift = remote(shifts, other, shift_sem.at[0], shift_sem.at[1], partner)
    swap_shift.start()

    def swaps(l, up):
        src = (tiles, blocks) if up else (1, 1)
        dst = (0, 0) if up else (tiles + 1, blocks + 1)
        return [
            remote(T4.at[l, src[0]], T4.at[l, dst[0]], swap_sem.at[0, l], swap_sem.at[1, l], partner),
            remote(EP.at[l, src[1]], EP.at[l, dst[1]], swap_sem.at[2, l], swap_sem.at[3, l], partner),
        ]

    @pl.when(core == 0)
    def _():
        for l in range(depth):
            for copy in swaps(l, True):
                copy.start()

    @pl.when(core == 1)
    def _():
        for l in range(depth):
            for copy in swaps(l, False):
                copy.start()

    targets = [(ks, kl, kc) for ks in (2, 1, 3, 0) for kl in range(depth) for kc in (1, 0)]

    def send(index):
        ks, kl, kc = targets[index]
        s = lax.rem(block + ks, blocks)
        l = lax.rem(layer + kl, depth)
        c = lax.rem(core + kc, 2)
        src, dst = M.at[l, s, c], W.at[me, pl.ds(c, 4)]
        sems = out_send.at[index], out_recv.at[me]
        across = remote(src, dst, *sems, {"az": (s * depth + l) * n_rad + core, "rad": c})
        is_late = s == c * (blocks - 1)
        return across, None if ks or kl or kc else pltpu.make_async_copy(src, dst, sems[1]), is_late

    def start(want_late):
        for index in range(len(targets)):
            across, within, is_late = send(index)
            now = is_late if want_late else jnp.logical_not(is_late)
            if within is None:

                @pl.when(now)
                def _():
                    across.start()

            else:

                @pl.when(jnp.logical_and(now, here))
                def _():
                    within.start()

                @pl.when(jnp.logical_and(now, jnp.logical_not(here)))
                def _():
                    across.start()

    start(False)
    for l in range(depth):
        for copy in swaps(l, True):
            copy.wait_recv()
    for l in range(depth):
        for s, c in late:
            stage(l, s, c)
    start(True)

    swap_shift.wait_recv()
    lower = jnp.full((1, lanes), core, jnp.int32) == 0
    mine, theirs = shifts[...], other[...]
    for c in range(2):
        part = jnp.where(lower, mine if c == 0 else theirs, theirs if c == 0 else mine)
        table = jnp.broadcast_to(part.astype(jnp.float32), (lanes, lanes)).T.astype(jnp.int32)
        SC[TILE + c * lanes : TILE + (c + 1) * lanes] = table
    SC[0:TILE] = jnp.zeros((TILE, lanes), jnp.int32)
    SC[TILE + 2 * lanes :] = jnp.zeros((TILE, lanes), jnp.int32)
    amount = SC[pl.ds(pl.multiple_of(place * 2 * TILE, TILE), rows)]

    plane = n_az // GROUPS
    near = [lax.rem(me // plane + k, GROUPS) for k in (0, 1, 3, 2)]

    def passes(k):
        ahead = pl.ds(near[k] * plane, plane)
        return remote(W.at[ahead, 3 - 2 * core], W.at[ahead, 4 * core], pass_send.at[k], pass_recv.at[near[k]], partner)

    def passed(q):
        return remote(
            W.at[pl.ds(q * plane, plane), 3 - 2 * core], W.at[pl.ds(q * plane, plane), 4 - 4 * core],
            pass_send.at[q], pass_recv.at[q], partner
        )

    def arrived(dst, recv):
        return pltpu.make_async_copy(dst, dst, recv)

    for k in range(GROUPS):
        for j in range(plane):
            i = near[k] * plane + lax.rem(me + j, plane)
            arrived(W.at[i, pl.ds(core, 4)], out_recv.at[i]).wait()
        passes(k).start()

    wide_lane = lax.broadcasted_iota(jnp.int32, (rows, lanes), 1)
    source = (wide_lane - amount) & (lanes - 1)
    inside = wide_lane >= amount

    def rotate(field):
        chunks = [field[:, v * lanes : (v + 1) * lanes] for v in range(GROUPS)]
        turned = [jnp.take_along_axis(chunk, source, axis=1) for chunk in chunks]
        return jnp.concatenate(
            [jnp.where(inside, turned[v], turned[v - 1]) for v in range(GROUPS)], axis=1
        )

    total = GROUPS * lanes
    at = jnp.full((TILE, total), place, jnp.int32)
    lowest = at == 0
    highest = at == 2 * blocks * n_rad - 1

    def edged(field):
        low = jnp.broadcast_to(field[TILE : TILE + 1], (TILE, total))
        high = jnp.broadcast_to(field[3 * TILE - 1 : 3 * TILE], (TILE, total))
        return jnp.concatenate(
            [
                jnp.where(lowest, low, field[:TILE]),
                field[TILE : 3 * TILE],
                jnp.where(highest, high, field[3 * TILE :]),
            ],
            axis=0,
        )

    for q in range(GROUPS):
        passed(q).wait_recv()

    columns = []
    for v in range(GROUPS):
        parts = [W[GROUPS * v + b, pl.ds(1 - core, 4)].reshape(rows, lanes) for b in range(GROUPS)]
        columns.append(regroup(parts, wide_lane))
    state = [edged(jnp.concatenate([columns[v][f] for v in range(GROUPS)], axis=1)) for f in range(4)]
    step = advect_all(state)
    state = [edged(rotate(step(field))) for field in state]

    columns = [regroup([W[GROUPS * v + b, 4 * core] for b in range(GROUPS)], lane) for v in range(GROUPS)]
    field = jnp.concatenate(
        [jnp.concatenate([columns[v][w] for v in range(GROUPS)], axis=1) for w in range(4)], axis=0
    )
    state.append(edged(rotate(step(edged(field)))))

    mr, mp, en = push_all(state)
    state = [edged(field) for field in (state[0], mr, mp, state[3], en)]
    step = advect_all(state)

    order = [(k, j) for k in (2, 1, 3, 0) for j in [*range(1, plane), 0]]

    def back(index):
        k, j = order[index]
        i = lax.rem(me // plane + k, GROUPS) * plane + lax.rem(me + j, plane)
        src, dst = B.at[i], R.at[layer, block, core]
        sems = back_send.at[index], back_recv.at[(layer * blocks + block) * 2 + core]
        across = remote(src, dst, *sems, {"az": i, "rad": half})
        return across, None if k or j else pltpu.make_async_copy(src, dst, sems[1])

    def pack(to, fields2):
        for v in range(GROUPS):
            cut = slice(v * lanes, (v + 1) * lanes)
            parts = [f[(1 + t) * TILE : (2 + t) * TILE, cut] for f in fields2 for t in range(2)]
            for b, part in enumerate(regroup(parts, lane)):
                B[GROUPS * v + b, to * TILE : (to + 1) * TILE] = part

    rho, mz = (edged(rotate(step(state[f]))) for f in (0, 3))
    pack(0, (rho, mz))
    mr, mp, en = (edged(rotate(step(state[f]))) for f in (1, 2, 4))
    mr, mp, en = push_all((rho, mr, mp, mz, en))
    pack(1, (mr, mp))
    for v in range(GROUPS // 2):
        cuts = [slice(u * lanes, (u + 1) * lanes) for u in (v, v + GROUPS // 2)]
        parts = [en[(1 + t) * TILE : (2 + t) * TILE, cut] for cut in cuts for t in range(2)]
        for b, part in enumerate(regroup(parts, lane)):
            folded = fold(part, lane, row)
            B[GROUPS * v + b, 2 * TILE :] = folded[: TILE // 2]
            B[GROUPS * (v + GROUPS // 2) + b, 2 * TILE :] = folded[TILE // 2 :]
    for index in range(len(order)):
        across, within = back(index)
        if within is None:
            across.start()
        else:

            @pl.when(here)
            def _():
                within.start()

            @pl.when(jnp.logical_not(here))
            def _():
                across.start()

    for l in range(depth):
        for s in range(blocks):
            for c in range(2):
                arrived(R.at[l, s, c], back_recv.at[(l * blocks + s) * 2 + c]).wait()
    for l in range(depth):
        pieces = []
        for s in range(blocks):
            for c in range(2):
                first, second = R[l, s, c, :TILE], R[l, s, c, TILE : 2 * TILE]
                for t in range(2):
                    a = lane_rows(first, width if t == 0 else -width)
                    b = lane_rows(second, width if t == 0 else -width)
                    if t == 0:
                        p, q, r, u = first, b, second, a
                    else:
                        p, q, r, u = a, second, b, first
                    pieces.append(
                        jnp.where(group < 2, jnp.where(group == 0, p, q), jnp.where(group == 2, r, u))
                    )
        block_out = jnp.concatenate(pieces, axis=0).T
        for f in range(4):
            out[f, l] = block_out[f * width : (f + 1) * width]
    pieces = []
    for s in range(blocks):
        both = [fold(jnp.concatenate([R[l, s, c, 2 * TILE :] for c in range(2)], axis=0), lane, row) for l in range(depth)]
        for g in range(GROUPS):
            piece = lane_rows(both[0], -width * g)
            for l in range(1, depth):
                piece = jnp.where(group == l, lane_rows(both[l], width * (l - g)), piece)
            pieces.append(piece)
    block_out = jnp.concatenate(pieces, axis=0).T
    for l in range(depth):
        out[4, l] = block_out[l * width : (l + 1) * width]

    swap_shift.wait_send()
    for l in range(depth):
        for copy in swaps(l, True):
            copy.wait_send()
    for index in range(len(targets)):
        across, within, _ = send(index)
        if within is None:
            across.wait_send()
        else:

            @pl.when(jnp.logical_not(here))
            def _():
                across.wait_send()

    for k in range(GROUPS):
        passes(k).wait_send()
    for index in range(len(order)):
        across, within = back(index)
        if within is None:
            across.wait_send()
        else:

            @pl.when(jnp.logical_not(here))
            def _():
                across.wait_send()


def turned_body(mesh, state, shifts):
    n_az, n_rad = mesh.shape["az"], mesh.shape["rad"]
    fields, depth, width, lanes = state.shape
    blocks = n_az // (depth * n_rad)
    tiles = lanes // TILE
    vmem = lambda *shape: pltpu.VMEM(shape, jnp.float32)
    dma = pltpu.SemaphoreType.DMA
    tile = (TILE, lanes)
    return pl.pallas_call(
        functools.partial(turned_kernel, n_az, n_rad),
        out_shape=pltpu.VMEM(state.shape, state.dtype),
        in_specs=[pl.BlockSpec(memory_space=pl.ANY), pl.BlockSpec(memory_space=pltpu.VMEM)],
        out_specs=pl.BlockSpec(memory_space=pltpu.VMEM),
        scratch_shapes=[
            vmem(fields, depth, width, lanes),
            vmem(depth, tiles + 2, *tile),
            vmem(depth, blocks + 2, *tile),
            vmem(depth, blocks, 2, 4, *tile),
            vmem(n_az, 5, *tile),
            pltpu.VMEM((1, lanes), jnp.int32),
            pltpu.VMEM((2 * lanes + 2 * TILE, lanes), jnp.int32),
            vmem(n_az, 2 * TILE + TILE // 2, lanes),
            vmem(depth, blocks, 2, 2 * TILE + TILE // 2, lanes),
            dma((depth,)),
            dma((2,)),
            dma((4, depth)),
            dma((n_az,)),
            dma((n_az,)),
            dma((GROUPS,)),
            dma((GROUPS,)),
            dma((n_az,)),
            dma((n_az,)),
        ],
        compiler_params=pltpu.CompilerParams(collective_id=0, has_side_effects=True),
    )(state, shifts.reshape(1, -1))


def turns(mesh, state):
    n_az, n_rad = mesh.shape["az"], mesh.shape["rad"]
    fields, depth, width, lanes = state.shape
    tiles = lanes // TILE
    return (
        n_rad == 2
        and fields == GROUPS + 1
        and width * GROUPS == lanes
        and n_az == GROUPS * GROUPS
        and n_az % (depth * n_rad) == 0
        and tiles == GROUPS * (n_az // (depth * n_rad))
        and depth * width <= lanes
        and SMAX <= lanes
    )


def choose(mesh, state, shifts):
    return (turned_body if turns(mesh, state) else body)(mesh, state, shifts)


def solution(mesh):
    in_specs = (P(None, None, "az", "rad"), P("rad"))
    out_specs = P(None, None, "az", "rad")
    return jax.shard_map(
        functools.partial(choose, mesh), mesh=mesh, in_specs=in_specs, out_specs=out_specs, check_vma=False
    )
```

```python
import functools

import jax
import jax.numpy as jnp
from jax import lax
from jax.experimental import pallas as pl
from jax.experimental.pallas import tpu as pltpu
from jax.sharding import PartitionSpec as P

STEPS = 2
SMIN = 4
SMAX = 96
EDGE = 4
TILE = 8

GAMMA_GAS = 1.4
COURANT_RADIAL = 0.15
COURANT_AZIMUTH = 0.15
VISCOSITY_COEF = 1.0


def up(x, axis):
    return pltpu.roll(x, x.shape[axis] - 1, axis)


def down(x, axis):
    return pltpu.roll(x, 1, axis)


def face_speeds(velocity, axis, courant):
    face = (0.5 * courant) * (velocity + up(velocity, axis))
    return jnp.maximum(face, 0.0), jnp.minimum(face, 0.0)


def advect(field, speeds, axis):
    low = field - down(field, axis)
    high = up(low, axis)
    product = low * high
    positive = product > 0
    half = jnp.where(positive, product / jnp.where(positive, low + high, 1.0), 0.0)
    flux = speeds[0] * (field + half) + speeds[1] * up(field - half, axis)
    return flux - down(flux, axis)


def push(pressure, density, speed, axis, courant):
    compress = jnp.minimum(up(speed, axis) - down(speed, axis), 0.0)
    total = pressure + VISCOSITY_COEF * density * compress * compress
    work = total * speed
    scale = -0.5 * courant
    return scale * (up(total, axis) - down(total, axis)), scale * (up(work, axis) - down(work, axis))


def shifted(window, shift_left, rows, longest):
    bits = longest.bit_length()
    x = window
    for bit in reversed(range(bits)):
        stride = 1 << bit
        left = stride - 1
        if stride >= TILE:
            keep = -(-(rows + left) // TILE) * TILE
            chosen = min(keep, x.shape[0] - stride)
            mask = (jnp.broadcast_to(shift_left, (chosen, shift_left.shape[1])) & stride) != 0
            y = jnp.where(mask, x[stride : stride + chosen], x[:chosen])
            x = y if chosen == keep else jnp.concatenate([y, x[chosen:keep]], axis=0)
        else:
            mask = (jnp.broadcast_to(shift_left, x.shape) & stride) != 0
            x = jnp.where(mask, pltpu.roll(x, x.shape[0] - stride, 0), x)
    return x[:rows]


def kernel(n_az, n_rad, x_in, shifts, out, *scratch):
    (x, load_sem, A, W0, W1, O0, O1, L0, R0, L1, R1, L2, R2, state_send, state_recv, gather_send, gather_recv,
     side_send, side_recv) = scratch
    fields, depth, width, lanes = x.shape
    behind = SMAX + EDGE
    whole = behind // width
    tail = behind % width
    tail_rows = -(-tail // TILE) * TILE
    group = whole + 1
    base = group * width
    first_row = width - tail_rows
    me = lax.axis_index("az")
    place = lax.rem(me, group)
    position = lax.axis_index("rad")

    def az(by):
        return {"az": lax.rem(me + by + n_az, n_az)}

    def member(by):
        return {"az": me - place + lax.rem(place + by + group, group)}

    def rad(by):
        return {"rad": position + by}

    barrier = pltpu.get_barrier_semaphore()
    MESH = pl.DeviceIdType.MESH
    load = pltpu.make_async_copy(x_in, x, load_sem)
    load.start()
    for by in (1, -1, -group):
        pl.semaphore_signal(barrier, inc=1, device_id=az(by), device_id_type=MESH)
    for h in range(1, group):
        pl.semaphore_signal(barrier, inc=1, device_id=member(h), device_id_type=MESH)

    has_left = position > 0
    has_right = position < n_rad - 1

    @pl.when(has_left)
    def _():
        pl.semaphore_signal(barrier, inc=1, device_id=rad(-1), device_id_type=MESH)

    @pl.when(has_right)
    def _():
        pl.semaphore_signal(barrier, inc=1, device_id=rad(1), device_id_type=MESH)

    load.wait()
    A[:, :, TILE : TILE + width, :] = x[...]
    beside_me = (position + n_rad - 1) // n_rad + (2 * n_rad - 2 - position) // n_rad
    pl.semaphore_wait(barrier, group + 2 + beside_me)

    def remote(src, dst, send, recv, where):
        return pltpu.make_async_remote_copy(
            src_ref=src, dst_ref=dst, send_sem=send, recv_sem=recv, device_id=where, device_id_type=MESH
        )

    def ring_copies(z):
        return [
            remote(x.at[:, z, width - TILE : width], A.at[:, z, 0:TILE],
                   state_send.at[0, z], state_recv.at[0, z], az(1)),
            remote(x.at[:, z, 0:TILE], A.at[:, z, TILE + width : 2 * TILE + width],
                   state_send.at[1, z], state_recv.at[1, z], az(-1)),
        ]

    def side_copies(phase, src, left_dst, right_dst, z):
        to_right = remote(src.at[:, z], left_dst.at[:, z], side_send.at[phase, 0, z],
                          side_recv.at[phase, 0, z], rad(1))
        to_left = remote(src.at[:, z], right_dst.at[:, z], side_send.at[phase, 1, z],
                         side_recv.at[phase, 1, z], rad(-1))
        return to_right, to_left

    def start_side(*args):
        to_right, to_left = side_copies(*args)

        @pl.when(has_right)
        def _():
            to_right.start()

        @pl.when(has_left)
        def _():
            to_left.start()

    def await_side(*args):
        to_right, to_left = side_copies(*args)

        @pl.when(has_left)
        def _():
            to_right.wait_recv()

        @pl.when(has_right)
        def _():
            to_left.wait_recv()

    def end_side(*args):
        to_right, to_left = side_copies(*args)

        @pl.when(has_right)
        def _():
            to_right.wait_send()

        @pl.when(has_left)
        def _():
            to_left.wait_send()

    windows = (W0, W1)
    rotated = (O0, O1)
    sides = ((x, L0, R0), (O0, L1, R1), (O1, L2, R2))

    def gather_copies(step, f, z):
        W = windows[step]
        own, back = W.at[f, z, base : base + width], W.at[f, z, 0:width]
        sems = lambda h: (gather_send.at[step, h, f, z], gather_recv.at[step, h, f, z])
        onward = remote(own, back, *sems(0), az(group))
        inside = []
        for h in range(1, group):
            dst = W.at[f, z, base - h * width : base - (h - 1) * width]
            inside.append([remote(src, dst, *sems(h), member(h)) for src in (own, back)])
        return onward, inside

    def send_own(step, f, z):
        onward, inside = gather_copies(step, f, z)
        onward.start()
        for h in range(1, group):

            @pl.when(place + h < group)
            def _():
                inside[h - 1][0].start()

    def pass_on(step, f, z):
        onward, inside = gather_copies(step, f, z)
        onward.wait_recv()
        for h in range(1, group):

            @pl.when(place + h >= group)
            def _():
                inside[h - 1][1].start()

    def edges(own, left, right):
        rows = own.shape[0]
        lane = lax.broadcasted_iota(jnp.int32, (rows, lanes), 1)
        at = jnp.full((rows, lanes), position, jnp.int32)
        left = jnp.where(at == 0, jnp.broadcast_to(own[:, 0:1], own.shape), left)
        right = jnp.where(at == n_rad - 1, jnp.broadcast_to(own[:, lanes - 1 : lanes], own.shape), right)
        return jnp.where(lane < lanes // 2, right, left)

    def wide(own, beside):
        return jnp.concatenate([own, beside], axis=1)

    def hydro(step, z, strip, beside):
        rows = slice(TILE, TILE + width)
        tall = [strip(f) for f in range(fields)]
        az_speeds = face_speeds(tall[2] / tall[0], 0, COURANT_AZIMUTH)
        broad = [wide(tall[f][rows], beside(f, tall[f][rows])) for f in range(fields)]
        rad_speeds = face_speeds(broad[1] / broad[0], 1, COURANT_RADIAL)
        for f in range(fields):
            along = advect(tall[f], az_speeds, 0)[rows]
            across = advect(broad[f], rad_speeds, 1)[:, :lanes]
            windows[step][f, z, base : base + width, :] = tall[f][rows] - along - across
            send_own(step, f, z)

    def viscous(z, state, extended):
        rho, mr, mp, mz, energy = state
        own = slice(None) if extended else slice(0, lanes)
        inverse = 1.0 / rho
        pressure = (GAMMA_GAS - 1.0) * (energy - 0.5 * (mr * mr + mp * mp + mz * mz) * inverse)
        az_m, az_e = push(pressure[:, own], rho[:, own], (mp * inverse)[:, own], 0, COURANT_AZIMUTH)
        rad_m, rad_e = push(pressure, rho, mr * inverse, 1, COURANT_RADIAL)
        return [
            rho[:, own],
            mr[:, own] + rad_m[:, own],
            mp[:, own] + az_m,
            mz[:, own],
            energy[:, own] + az_e + rad_e[:, own],
        ]

    count = width + 2 * EDGE

    for z in range(depth):
        for copy in ring_copies(z):
            copy.start()
    for z in range(depth):
        start_side(0, *sides[0], z)
    for z in range(depth):
        for copy in ring_copies(z):
            copy.wait_recv()
        await_side(0, *sides[0], z)
        hydro(0, z, lambda f: A[f, z], lambda f, own: edges(own, L0[f, z], R0[f, z]))

    for step in range(STEPS):
        for z in range(depth):
            for f in range(fields):
                pass_on(step, f, z)
        O, L, R = sides[step + 1]
        for z in range(depth):
            for f in range(fields):
                for copies in gather_copies(step, f, z)[1]:
                    copies[0].wait_recv()
                start = base - first_row - EDGE
                O[f, z] = shifted(windows[step][f, z, first_row:], start - shifts[...], count, start - SMIN)
            start_side(step + 1, O, L, R, z)
        for z in range(depth):
            await_side(step + 1, O, L, R, z)
            state = [wide(O[f, z], edges(O[f, z], L[f, z], R[f, z])) for f in range(fields)]
            if step == STEPS - 1:
                new = viscous(z, state, False)
                for f in range(fields):
                    out[f, z] = new[f][EDGE : EDGE + width]
            else:
                new = viscous(z, state, True)
                A_rows = slice(TILE - EDGE, TILE - EDGE + count)
                for f in range(fields):
                    A[f, z, A_rows, :] = new[f][:, :lanes]
                hydro(
                    step + 1,
                    z,
                    lambda f: A[f, z],
                    lambda f, own: edges(own, *[new[f][EDGE : EDGE + width, lanes:]] * 2),
                )

    for z in range(depth):
        for copy in ring_copies(z):
            copy.wait_send()
        for phase in range(STEPS + 1):
            end_side(phase, *sides[phase], z)
        for step in range(STEPS):
            for f in range(fields):
                onward, inside = gather_copies(step, f, z)
                onward.wait_send()
                for copies in inside:
                    copies[0].wait_send()


def body(mesh, state, shifts):
    n_az, n_rad = mesh.shape["az"], mesh.shape["rad"]
    fields, depth, width, lanes = state.shape
    behind = SMAX + EDGE
    group = behind // width + 1
    window = (group + 1) * width
    count = width + 2 * EDGE
    vmem = lambda rows: pltpu.VMEM((fields, depth, rows, lanes), jnp.float32)
    dma = pltpu.SemaphoreType.DMA
    return pl.pallas_call(
        functools.partial(kernel, n_az, n_rad),
        out_shape=pltpu.VMEM(state.shape, state.dtype),
        in_specs=[pl.BlockSpec(memory_space=pl.ANY), pl.BlockSpec(memory_space=pltpu.VMEM)],
        out_specs=pl.BlockSpec(memory_space=pltpu.VMEM),
        scratch_shapes=[
            vmem(width),
            dma(()),
            vmem(width + 2 * TILE),
            vmem(window),
            vmem(window),
            vmem(count),
            vmem(count),
            vmem(width),
            vmem(width),
            vmem(count),
            vmem(count),
            vmem(count),
            vmem(count),
            dma((2, depth)),
            dma((2, depth)),
            dma((STEPS, group, fields, depth)),
            dma((STEPS, group, fields, depth)),
            dma((STEPS + 1, 2, depth)),
            dma((STEPS + 1, 2, depth)),
        ],
        compiler_params=pltpu.CompilerParams(collective_id=0, has_side_effects=True),
    )(state, shifts.reshape(1, -1))


GROUPS = 4


def lane_rows(x, shift):
    return pltpu.roll(x, shift % x.shape[1], 1)


def exchange(parts, lane):
    n = len(parts)
    out = [parts[-g % n] for g in range(n)]
    for bit in range(n.bit_length() - 1):
        far = (lane & (TILE << bit)) != 0
        out = [jnp.where(far, out[(g - (1 << bit)) % n], out[g]) for g in range(n)]
    return out


def fold(x, lane, row):
    half = x.shape[1] // 2
    stay = (lane < half) == (row < TILE // 2)
    return jnp.where(stay, x, lane_rows(pltpu.roll(x, TILE // 2, 0), half))


def line(tiles):
    return jnp.concatenate(tiles, axis=0)


def tiles_of(x):
    return [x[g * TILE : (g + 1) * TILE] for g in range(GROUPS)]


def next_of(x, axis):
    first = x[:TILE]
    return jnp.concatenate([x[TILE:], pltpu.roll(first, first.shape[axis] - 1, axis)], axis=0)


def last_of(x, axis):
    last = x[-TILE:]
    return jnp.concatenate([pltpu.roll(last, 1, axis), x[:-TILE]], axis=0)


def along(field, w):
    return line([field[u][w] for u in range(GROUPS)])


def across(field, u):
    return line(field[u])


def line_speeds(velocity, axis, courant):
    face = (0.5 * courant) * (velocity + next_of(velocity, axis))
    return jnp.maximum(face, 0.0), jnp.minimum(face, 0.0)


def line_advect(field, speeds, axis):
    low = field - last_of(field, axis)
    high = next_of(low, axis)
    product = low * high
    half = jnp.where(product > 0, product / (low + high), 0.0)
    flux = speeds[0] * (field + half) + speeds[1] * next_of(field - half, axis)
    return flux - last_of(flux, axis)


def line_push(pressure, density, speed, axis, courant):
    compress = jnp.minimum(next_of(speed, axis) - last_of(speed, axis), 0.0)
    total = pressure + VISCOSITY_COEF * density * compress * compress
    work = total * speed
    scale = -0.5 * courant
    return scale * (next_of(total, axis) - last_of(total, axis)), scale * (next_of(work, axis) - last_of(work, axis))


def advect_all(state):
    rho, mr, mp = state[:3]
    az_speeds, rad_speeds = [], []
    inverse = [tiles_of(1.0 / across(rho, u)) for u in range(GROUPS)]
    for g in range(GROUPS):
        az_speeds.append(line_speeds(along(mp, g) * along(inverse, g), 1, COURANT_AZIMUTH))
        rad_speeds.append(line_speeds(across(mr, g) * across(inverse, g), 0, COURANT_RADIAL))

    def step(field):
        turned = [along(field, w) for w in range(GROUPS)]
        turned = [tiles_of(turned[w] - line_advect(turned[w], az_speeds[w], 1)) for w in range(GROUPS)]
        out = []
        for u in range(GROUPS):
            rest = line([turned[w][u] for w in range(GROUPS)])
            out.append(tiles_of(rest - line_advect(across(field, u), rad_speeds[u], 0)))
        return out

    return step


def push_all(state):
    rho, mr, mp, mz, energy = state
    inverse, pressure, new_mr, rest = [], [], [], []
    for u in range(GROUPS):
        r, a, b, c, e = (across(f, u) for f in state)
        inv = 1.0 / r
        p = (GAMMA_GAS - 1.0) * (e - 0.5 * (a * a + b * b + c * c) * inv)
        rad_m, rad_e = line_push(p, r, a * inv, 0, COURANT_RADIAL)
        inverse.append(tiles_of(inv))
        pressure.append(tiles_of(p))
        new_mr.append(tiles_of(a + rad_m))
        rest.append(tiles_of(e + rad_e))
    new_mp = [[None] * GROUPS for _ in range(GROUPS)]
    new_energy = [[None] * GROUPS for _ in range(GROUPS)]
    for w in range(GROUPS):
        b = along(mp, w)
        az_m, az_e = line_push(along(pressure, w), along(rho, w), b * along(inverse, w), 1, COURANT_AZIMUTH)
        for u, (m, e) in enumerate(zip(tiles_of(b + az_m), tiles_of(along(rest, w) + az_e))):
            new_mp[u][w], new_energy[u][w] = m, e
    return new_mr, new_mp, new_energy


def turned_kernel(n_az, n_rad, x_in, shifts, out, *scratch):
    (x, T4, EP, M, W, other, SC, AM, F, G, B, R, load_sem, shift_sem, swap_sem, out_send, out_recv, pass_send, pass_recv,
     back_send, back_recv) = scratch
    fields, depth, width, lanes = x.shape
    blocks = n_az // (depth * n_rad)
    tiles = lanes // TILE
    rows = 4 * TILE
    MESH = pl.DeviceIdType.MESH
    me = lax.axis_index("az")
    core = lax.axis_index("rad")
    half = lax.rem(me, n_rad)
    layer = lax.rem(me // n_rad, depth)
    block = me // (n_rad * depth)
    place = (half * blocks + block) * 2 + core
    partner = {"rad": 1 - core}
    here = half == core

    def remote(src, dst, send, recv, where):
        return pltpu.make_async_remote_copy(
            src_ref=src, dst_ref=dst, send_sem=send, recv_sem=recv, device_id=where, device_id_type=MESH
        )

    loads = [pltpu.make_async_copy(x_in.at[:, l], x.at[:, l], load_sem.at[l]) for l in range(depth)]
    for load in loads:
        load.start()
    barrier = pltpu.get_barrier_semaphore()
    for k in range(1, n_az):
        pl.semaphore_signal(
            barrier, inc=1, device_id={"az": lax.rem(me + k, n_az), "rad": half}, device_id_type=MESH
        )
    pl.semaphore_signal(barrier, inc=1, device_id=partner, device_id_type=MESH)

    lane = lax.broadcasted_iota(jnp.int32, (TILE, lanes), 1)
    row = lax.broadcasted_iota(jnp.int32, (TILE, lanes), 0)
    group = lane // width

    spin = me * TILE

    def rows_of(f, l):
        return [x[f, l, pl.ds(u, width // GROUPS, stride=GROUPS), :] for u in range(GROUPS)]

    for l in range(depth):
        loads[l].wait()
        cells = jnp.concatenate([part for f in range(GROUPS) for part in rows_of(f, l)], axis=0)
        T4[l, 1 : tiles + 1] = pltpu.roll(cells.T, spin, 1).reshape(tiles, TILE, lanes)
    energy = [part for l in range(depth) for part in rows_of(4, l)]
    turned = jnp.concatenate(energy * (lanes // (depth * width)), axis=0).T.reshape(tiles, TILE, lanes)
    for l in range(depth):
        for m in range(tiles // GROUPS):
            packed = turned[GROUPS * m] if l == 0 else lane_rows(turned[GROUPS * m], -width * l)
            for g in range(1, GROUPS):
                packed = jnp.where(group == g, lane_rows(turned[GROUPS * m + g], width * (g - l)), packed)
            EP[l, 1 + m] = packed

    @pl.when(core == 0)
    def _():
        for l in range(depth):
            T4[l, 0] = jnp.broadcast_to(T4[l, 1, 0:1], (TILE, lanes))
            EP[l, 0] = jnp.broadcast_to(lane_rows(EP[l, 1], -width)[0:1], (TILE, lanes))

    @pl.when(core == 1)
    def _():
        for l in range(depth):
            T4[l, tiles + 1] = jnp.broadcast_to(T4[l, tiles, TILE - 1 : TILE], (TILE, lanes))
            EP[l, blocks + 1] = jnp.broadcast_to(lane_rows(EP[l, blocks], width)[TILE - 1 : TILE], (TILE, lanes))

    def stage(l, s, c):
        own = EP[l, 1 + s]
        if c == 0:
            M[l, s, c, 0] = pltpu.roll(jnp.where(group == GROUPS - 1, EP[l, s], own), lax.rem(spin + width, lanes), 1)
            M[l, s, c, 1:4] = T4[l, GROUPS * s : GROUPS * s + 3]
        else:
            M[l, s, c, 0:3] = T4[l, GROUPS * s + 3 : GROUPS * s + 6]
            M[l, s, c, 3] = pltpu.roll(jnp.where(group == 0, EP[l, s + 2], own), lax.rem(spin + lanes - width, lanes), 1)

    late = ((0, 0), (blocks - 1, 1))
    for l in range(depth):
        for s in range(blocks):
            for c in range(2):
                if (s, c) not in late:
                    stage(l, s, c)

    senders = jnp.where(here, 2 * (n_az // n_rad - 1) + 1, 2 * (n_az // n_rad) + 1)
    pl.semaphore_wait(barrier, senders)

    swap_shift = remote(shifts, other, shift_sem.at[0], shift_sem.at[1], partner)
    swap_shift.start()

    def swaps(l, up):
        src = (tiles, blocks) if up else (1, 1)
        dst = (0, 0) if up else (tiles + 1, blocks + 1)
        return [
            remote(T4.at[l, src[0]], T4.at[l, dst[0]], swap_sem.at[0, l], swap_sem.at[1, l], partner),
            remote(EP.at[l, src[1]], EP.at[l, dst[1]], swap_sem.at[2, l], swap_sem.at[3, l], partner),
        ]

    @pl.when(core == 0)
    def _():
        for l in range(depth):
            for copy in swaps(l, True):
                copy.start()

    @pl.when(core == 1)
    def _():
        for l in range(depth):
            for copy in swaps(l, False):
                copy.start()

    targets = [(ks, kl, kc) for ks in (2, 1, 3, 0) for kl in range(depth) for kc in (1, 0)]

    def send(index):
        ks, kl, kc = targets[index]
        s = lax.rem(block + ks, blocks)
        l = lax.rem(layer + kl, depth)
        c = lax.rem(core + kc, 2)
        src, dst = M.at[l, s, c], W.at[me, pl.ds(c, 4)]
        sems = out_send.at[index], out_recv.at[me]
        sent = remote(src, dst, *sems, {"az": (s * depth + l) * n_rad + core, "rad": c})
        is_late = s == c * (blocks - 1)
        return sent, None if ks or kl or kc else pltpu.make_async_copy(src, dst, sems[1]), is_late

    def start(want_late):
        for index in range(len(targets)):
            sent, within, is_late = send(index)
            now = is_late if want_late else jnp.logical_not(is_late)
            if within is None:

                @pl.when(now)
                def _():
                    sent.start()

            else:

                @pl.when(jnp.logical_and(now, here))
                def _():
                    within.start()

                @pl.when(jnp.logical_and(now, jnp.logical_not(here)))
                def _():
                    sent.start()

    start(False)
    for l in range(depth):
        for copy in swaps(l, True):
            copy.wait_recv()
    for l in range(depth):
        for s, c in late:
            stage(l, s, c)
    start(True)

    swap_shift.wait_recv()
    lower = jnp.full((1, lanes), core, jnp.int32) == 0
    mine, theirs = shifts[...], other[...]
    for c in range(2):
        part = jnp.where(lower, mine if c == 0 else theirs, theirs if c == 0 else mine)
        table = jnp.broadcast_to(part.astype(jnp.float32), (lanes, lanes)).T.astype(jnp.int32)
        SC[TILE + c * lanes : TILE + (c + 1) * lanes] = table
    SC[0:TILE] = jnp.zeros((TILE, lanes), jnp.int32)
    SC[TILE + 2 * lanes :] = jnp.zeros((TILE, lanes), jnp.int32)
    AM[...] = SC[pl.ds(pl.multiple_of(place * 2 * TILE, TILE), rows)]
    amounts = [AM[pl.ds(w, TILE, stride=GROUPS), :] for w in range(GROUPS)]
    coarse = [amount // GROUPS for amount in amounts]
    odd = [(amount & 1) != 0 for amount in amounts]
    two = [(amount & 2) != 0 for amount in amounts]
    source = [
        [(lane - coarse[w] - jnp.where(u < (amounts[w] & (GROUPS - 1)), 1, 0)) & (lanes - 1) for w in range(GROUPS)]
        for u in range(GROUPS)
    ]

    plane = n_az // GROUPS
    near = [lax.rem(me // plane + k, GROUPS) for k in (0, 1, 3, 2)]

    def passes(k):
        ahead = pl.ds(near[k] * plane, plane)
        return remote(W.at[ahead, 3 - 2 * core], W.at[ahead, 4 * core], pass_send.at[k], pass_recv.at[near[k]], partner)

    def passed(q):
        return remote(
            W.at[pl.ds(q * plane, plane), 3 - 2 * core], W.at[pl.ds(q * plane, plane), 4 - 4 * core],
            pass_send.at[q], pass_recv.at[q], partner
        )

    def arrived(dst, recv):
        return pltpu.make_async_copy(dst, dst, recv)

    for k in range(GROUPS):
        for j in range(plane):
            i = near[k] * plane + lax.rem(me + j, plane)
            arrived(W.at[i, pl.ds(core, 4)], out_recv.at[i]).wait()
        passes(k).start()

    def rotate(field):
        out = [[None] * GROUPS for _ in range(GROUPS)]
        for w in range(GROUPS):
            near_by = [jnp.where(odd[w], field[u - 1][w], field[u][w]) for u in range(GROUPS)]
            for u in range(GROUPS):
                chosen = jnp.where(two[w], near_by[u - 2], near_by[u])
                out[u][w] = jnp.take_along_axis(chosen, source[u][w], axis=1)
        return out

    at = jnp.full((TILE, lanes), place, jnp.int32)
    lowest = jnp.logical_and(at == 0, row < 2)
    highest = jnp.logical_and(at == 2 * blocks * n_rad - 1, row >= TILE - 2)

    def edged(field):
        out = []
        for u in range(GROUPS):
            low = jnp.broadcast_to(field[u][0][2:3], (TILE, lanes))
            high = jnp.broadcast_to(field[u][3][TILE - 3 : TILE - 2], (TILE, lanes))
            out.append(
                [jnp.where(highest, high, field[u][w]) for w in range(2)]
                + [jnp.where(lowest, low, field[u][w]) for w in range(2, GROUPS)]
            )
        return out

    def unpack(parts):
        return [lane_rows(part, -TILE * g) for g, part in enumerate(exchange(parts, lane_of[parts[0].shape[0]]))]

    lane_of = {n * TILE: lax.broadcasted_iota(jnp.int32, (n * TILE, lanes), 1) for n in (1, 2, 3)}

    direct = unpack([W[i, 1:4].reshape(3 * TILE, lanes) for i in range(n_az)])
    for g in range(GROUPS * GROUPS):
        F[g, pl.ds(pl.multiple_of(core * TILE, TILE), 3 * TILE)] = direct[g]
    for g, part in enumerate(unpack([W[i, 4 * core] for i in range(n_az)])):
        w, u = g // GROUPS, g % GROUPS
        F[GROUPS * GROUPS + u, w * TILE : (w + 1) * TILE] = part
    for q in range(GROUPS):
        passed(q).wait_recv()
    for g, part in enumerate(unpack([W[i, 4 - 4 * core] for i in range(n_az)])):
        F[g, pl.ds(pl.multiple_of((1 - core) * 3 * TILE, TILE), TILE)] = part

    state = [
        [[F[GROUPS * f + u, pl.ds(w, TILE, stride=GROUPS), :] for w in range(GROUPS)] for u in range(GROUPS)]
        for f in range(fields)
    ]
    step = advect_all(state)
    state = [edged(rotate(step(field))) for field in state]
    mr, mp, en = push_all(state)
    state = [edged(field) for field in (state[0], mr, mp, state[3], en)]
    step = advect_all(state)
    state = [edged(rotate(step(field))) for field in state]
    mr, mp, en = push_all(state)
    for f, field in enumerate((state[0], mr, mp, state[3], en)):
        for u in range(GROUPS):
            for w in range(GROUPS):
                G[GROUPS * f + u, pl.ds(w, TILE, stride=GROUPS), :] = field[u][w]

    order = [(k, j) for k in (2, 1, 3, 0) for j in [*range(1, plane), 0]]

    def back(index):
        k, j = order[index]
        i = lax.rem(me // plane + k, GROUPS) * plane + lax.rem(me + j, plane)
        src, dst = B.at[i], R.at[layer, block, core]
        sems = back_send.at[index], back_recv.at[(layer * blocks + block) * 2 + core]
        sent = remote(src, dst, *sems, {"az": i, "rad": half})
        return sent, None if k or j else pltpu.make_async_copy(src, dst, sems[1])

    own = [lane_rows(G[g, TILE : 3 * TILE], TILE * g) for g in range(GROUPS * GROUPS)]
    for i, part in enumerate(exchange(own, lane_of[2 * TILE])):
        B[i, : 2 * TILE] = part
    own = [
        lane_rows(G[GROUPS * GROUPS + u, (1 + t) * TILE : (2 + t) * TILE], TILE * (GROUPS * t + u))
        for t in range(2)
        for u in range(GROUPS)
    ]
    for i, part in enumerate(exchange(own, lane)):
        folded = fold(lane_rows(part, -TILE * i), lane, row)
        B[i, 2 * TILE :] = folded[: TILE // 2]
        B[i + n_az // 2, 2 * TILE :] = folded[TILE // 2 :]
    for index in range(len(order)):
        sent, within = back(index)
        if within is None:
            sent.start()
        else:

            @pl.when(here)
            def _():
                within.start()

            @pl.when(jnp.logical_not(here))
            def _():
                sent.start()

    for l in range(depth):
        for s in range(blocks):
            for c in range(2):
                arrived(R.at[l, s, c], back_recv.at[(l * blocks + s) * 2 + c]).wait()
    for l in range(depth):
        pieces = [R[l, s, c, : 2 * TILE] for s in range(blocks) for c in range(2)]
        cells = pltpu.roll(jnp.concatenate(pieces, axis=0), lax.rem(lanes - spin, lanes), 1).T
        for f in range(GROUPS):
            for u in range(GROUPS):
                g = GROUPS * f + u
                out[f, l, pl.ds(u, TILE, stride=GROUPS), :] = cells[g * TILE : (g + 1) * TILE]
    pieces = []
    for s in range(blocks):
        both = [fold(jnp.concatenate([R[l, s, c, 2 * TILE :] for c in range(2)], axis=0), lane, row) for l in range(depth)]
        for g in range(GROUPS):
            piece = lane_rows(both[0], -width * g)
            for l in range(1, depth):
                piece = jnp.where(group == l, lane_rows(both[l], width * (l - g)), piece)
            pieces.append(piece)
    cells = jnp.concatenate(pieces, axis=0).T
    for l in range(depth):
        for u in range(GROUPS):
            g = GROUPS * l + u
            out[4, l, pl.ds(u, TILE, stride=GROUPS), :] = cells[g * TILE : (g + 1) * TILE]

    swap_shift.wait_send()
    for l in range(depth):
        for copy in swaps(l, True):
            copy.wait_send()
    for index in range(len(targets)):
        sent, within, _ = send(index)
        if within is None:
            sent.wait_send()
        else:

            @pl.when(jnp.logical_not(here))
            def _():
                sent.wait_send()

    for k in range(GROUPS):
        passes(k).wait_send()
    for index in range(len(order)):
        sent, within = back(index)
        if within is None:
            sent.wait_send()
        else:

            @pl.when(jnp.logical_not(here))
            def _():
                sent.wait_send()


def turned_body(mesh, state, shifts):
    n_az, n_rad = mesh.shape["az"], mesh.shape["rad"]
    fields, depth, width, lanes = state.shape
    blocks = n_az // (depth * n_rad)
    tiles = lanes // TILE
    vmem = lambda *shape: pltpu.VMEM(shape, jnp.float32)
    dma = pltpu.SemaphoreType.DMA
    tile = (TILE, lanes)
    return pl.pallas_call(
        functools.partial(turned_kernel, n_az, n_rad),
        out_shape=pltpu.VMEM(state.shape, state.dtype),
        in_specs=[pl.BlockSpec(memory_space=pl.ANY), pl.BlockSpec(memory_space=pltpu.VMEM)],
        out_specs=pl.BlockSpec(memory_space=pltpu.VMEM),
        scratch_shapes=[
            vmem(fields, depth, width, lanes),
            vmem(depth, tiles + 2, *tile),
            vmem(depth, blocks + 2, *tile),
            vmem(depth, blocks, 2, 4, *tile),
            vmem(n_az, 5, *tile),
            pltpu.VMEM((1, lanes), jnp.int32),
            pltpu.VMEM((2 * lanes + 2 * TILE, lanes), jnp.int32),
            pltpu.VMEM((4 * TILE, lanes), jnp.int32),
            vmem(GROUPS * fields, 4 * TILE, lanes),
            vmem(GROUPS * fields, 4 * TILE, lanes),
            vmem(n_az, 2 * TILE + TILE // 2, lanes),
            vmem(depth, blocks, 2, 2 * TILE + TILE // 2, lanes),
            dma((depth,)),
            dma((2,)),
            dma((4, depth)),
            dma((n_az,)),
            dma((n_az,)),
            dma((GROUPS,)),
            dma((GROUPS,)),
            dma((n_az,)),
            dma((n_az,)),
        ],
        compiler_params=pltpu.CompilerParams(collective_id=0, has_side_effects=True),
    )(state, shifts.reshape(1, -1))


def turns(mesh, state):
    n_az, n_rad = mesh.shape["az"], mesh.shape["rad"]
    fields, depth, width, lanes = state.shape
    tiles = lanes // TILE
    return (
        n_rad == 2
        and fields == GROUPS + 1
        and width * GROUPS == lanes
        and n_az == GROUPS * GROUPS
        and width == GROUPS * TILE
        and lanes == n_az * TILE
        and n_az % (depth * n_rad) == 0
        and tiles == GROUPS * (n_az // (depth * n_rad))
        and depth * width <= lanes
        and SMAX <= lanes
    )


def choose(mesh, state, shifts):
    return (turned_body if turns(mesh, state) else body)(mesh, state, shifts)


def solution(mesh):
    in_specs = (P(None, None, "az", "rad"), P("rad"))
    out_specs = P(None, None, "az", "rad")
    return jax.shard_map(
        functools.partial(choose, mesh), mesh=mesh, in_specs=in_specs, out_specs=out_specs, check_vma=False
    )
```

```python
import functools

import jax
import jax.numpy as jnp
from jax import lax
from jax.experimental import pallas as pl
from jax.experimental.pallas import tpu as pltpu
from jax.sharding import PartitionSpec as P

STEPS = 2
SMIN = 4
SMAX = 96
EDGE = 4
TILE = 8

GAMMA_GAS = 1.4
COURANT_RADIAL = 0.15
COURANT_AZIMUTH = 0.15
VISCOSITY_COEF = 1.0


def up(x, axis):
    return pltpu.roll(x, x.shape[axis] - 1, axis)


def down(x, axis):
    return pltpu.roll(x, 1, axis)


def face_speeds(velocity, axis, courant):
    face = (0.5 * courant) * (velocity + up(velocity, axis))
    return jnp.maximum(face, 0.0), jnp.minimum(face, 0.0)


def advect(field, speeds, axis):
    low = field - down(field, axis)
    high = up(low, axis)
    product = low * high
    positive = product > 0
    half = jnp.where(positive, product / jnp.where(positive, low + high, 1.0), 0.0)
    flux = speeds[0] * (field + half) + speeds[1] * up(field - half, axis)
    return flux - down(flux, axis)


def push(pressure, density, speed, axis, courant):
    compress = jnp.minimum(up(speed, axis) - down(speed, axis), 0.0)
    total = pressure + VISCOSITY_COEF * density * compress * compress
    work = total * speed
    scale = -0.5 * courant
    return scale * (up(total, axis) - down(total, axis)), scale * (up(work, axis) - down(work, axis))


def shifted(window, shift_left, rows, longest):
    bits = longest.bit_length()
    x = window
    for bit in reversed(range(bits)):
        stride = 1 << bit
        left = stride - 1
        if stride >= TILE:
            keep = -(-(rows + left) // TILE) * TILE
            chosen = min(keep, x.shape[0] - stride)
            mask = (jnp.broadcast_to(shift_left, (chosen, shift_left.shape[1])) & stride) != 0
            y = jnp.where(mask, x[stride : stride + chosen], x[:chosen])
            x = y if chosen == keep else jnp.concatenate([y, x[chosen:keep]], axis=0)
        else:
            mask = (jnp.broadcast_to(shift_left, x.shape) & stride) != 0
            x = jnp.where(mask, pltpu.roll(x, x.shape[0] - stride, 0), x)
    return x[:rows]


def kernel(n_az, n_rad, x_in, shifts, out, *scratch):
    (x, load_sem, A, W0, W1, O0, O1, L0, R0, L1, R1, L2, R2, state_send, state_recv, gather_send, gather_recv,
     side_send, side_recv) = scratch
    fields, depth, width, lanes = x.shape
    behind = SMAX + EDGE
    whole = behind // width
    tail = behind % width
    tail_rows = -(-tail // TILE) * TILE
    group = whole + 1
    base = group * width
    first_row = width - tail_rows
    me = lax.axis_index("az")
    place = lax.rem(me, group)
    position = lax.axis_index("rad")

    def az(by):
        return {"az": lax.rem(me + by + n_az, n_az)}

    def member(by):
        return {"az": me - place + lax.rem(place + by + group, group)}

    def rad(by):
        return {"rad": position + by}

    barrier = pltpu.get_barrier_semaphore()
    MESH = pl.DeviceIdType.MESH
    load = pltpu.make_async_copy(x_in, x, load_sem)
    load.start()
    for by in (1, -1, -group):
        pl.semaphore_signal(barrier, inc=1, device_id=az(by), device_id_type=MESH)
    for h in range(1, group):
        pl.semaphore_signal(barrier, inc=1, device_id=member(h), device_id_type=MESH)

    has_left = position > 0
    has_right = position < n_rad - 1

    @pl.when(has_left)
    def _():
        pl.semaphore_signal(barrier, inc=1, device_id=rad(-1), device_id_type=MESH)

    @pl.when(has_right)
    def _():
        pl.semaphore_signal(barrier, inc=1, device_id=rad(1), device_id_type=MESH)

    load.wait()
    A[:, :, TILE : TILE + width, :] = x[...]
    beside_me = (position + n_rad - 1) // n_rad + (2 * n_rad - 2 - position) // n_rad
    pl.semaphore_wait(barrier, group + 2 + beside_me)

    def remote(src, dst, send, recv, where):
        return pltpu.make_async_remote_copy(
            src_ref=src, dst_ref=dst, send_sem=send, recv_sem=recv, device_id=where, device_id_type=MESH
        )

    def ring_copies(z):
        return [
            remote(x.at[:, z, width - TILE : width], A.at[:, z, 0:TILE],
                   state_send.at[0, z], state_recv.at[0, z], az(1)),
            remote(x.at[:, z, 0:TILE], A.at[:, z, TILE + width : 2 * TILE + width],
                   state_send.at[1, z], state_recv.at[1, z], az(-1)),
        ]

    def side_copies(phase, src, left_dst, right_dst, z):
        to_right = remote(src.at[:, z], left_dst.at[:, z], side_send.at[phase, 0, z],
                          side_recv.at[phase, 0, z], rad(1))
        to_left = remote(src.at[:, z], right_dst.at[:, z], side_send.at[phase, 1, z],
                         side_recv.at[phase, 1, z], rad(-1))
        return to_right, to_left

    def start_side(*args):
        to_right, to_left = side_copies(*args)

        @pl.when(has_right)
        def _():
            to_right.start()

        @pl.when(has_left)
        def _():
            to_left.start()

    def await_side(*args):
        to_right, to_left = side_copies(*args)

        @pl.when(has_left)
        def _():
            to_right.wait_recv()

        @pl.when(has_right)
        def _():
            to_left.wait_recv()

    def end_side(*args):
        to_right, to_left = side_copies(*args)

        @pl.when(has_right)
        def _():
            to_right.wait_send()

        @pl.when(has_left)
        def _():
            to_left.wait_send()

    windows = (W0, W1)
    rotated = (O0, O1)
    sides = ((x, L0, R0), (O0, L1, R1), (O1, L2, R2))

    def gather_copies(step, f, z):
        W = windows[step]
        own, back = W.at[f, z, base : base + width], W.at[f, z, 0:width]
        sems = lambda h: (gather_send.at[step, h, f, z], gather_recv.at[step, h, f, z])
        onward = remote(own, back, *sems(0), az(group))
        inside = []
        for h in range(1, group):
            dst = W.at[f, z, base - h * width : base - (h - 1) * width]
            inside.append([remote(src, dst, *sems(h), member(h)) for src in (own, back)])
        return onward, inside

    def send_own(step, f, z):
        onward, inside = gather_copies(step, f, z)
        onward.start()
        for h in range(1, group):

            @pl.when(place + h < group)
            def _():
                inside[h - 1][0].start()

    def pass_on(step, f, z):
        onward, inside = gather_copies(step, f, z)
        onward.wait_recv()
        for h in range(1, group):

            @pl.when(place + h >= group)
            def _():
                inside[h - 1][1].start()

    def edges(own, left, right):
        rows = own.shape[0]
        lane = lax.broadcasted_iota(jnp.int32, (rows, lanes), 1)
        at = jnp.full((rows, lanes), position, jnp.int32)
        left = jnp.where(at == 0, jnp.broadcast_to(own[:, 0:1], own.shape), left)
        right = jnp.where(at == n_rad - 1, jnp.broadcast_to(own[:, lanes - 1 : lanes], own.shape), right)
        return jnp.where(lane < lanes // 2, right, left)

    def wide(own, beside):
        return jnp.concatenate([own, beside], axis=1)

    def hydro(step, z, strip, beside):
        rows = slice(TILE, TILE + width)
        tall = [strip(f) for f in range(fields)]
        az_speeds = face_speeds(tall[2] / tall[0], 0, COURANT_AZIMUTH)
        broad = [wide(tall[f][rows], beside(f, tall[f][rows])) for f in range(fields)]
        rad_speeds = face_speeds(broad[1] / broad[0], 1, COURANT_RADIAL)
        for f in range(fields):
            along = advect(tall[f], az_speeds, 0)[rows]
            across = advect(broad[f], rad_speeds, 1)[:, :lanes]
            windows[step][f, z, base : base + width, :] = tall[f][rows] - along - across
            send_own(step, f, z)

    def viscous(z, state, extended):
        rho, mr, mp, mz, energy = state
        own = slice(None) if extended else slice(0, lanes)
        inverse = 1.0 / rho
        pressure = (GAMMA_GAS - 1.0) * (energy - 0.5 * (mr * mr + mp * mp + mz * mz) * inverse)
        az_m, az_e = push(pressure[:, own], rho[:, own], (mp * inverse)[:, own], 0, COURANT_AZIMUTH)
        rad_m, rad_e = push(pressure, rho, mr * inverse, 1, COURANT_RADIAL)
        return [
            rho[:, own],
            mr[:, own] + rad_m[:, own],
            mp[:, own] + az_m,
            mz[:, own],
            energy[:, own] + az_e + rad_e[:, own],
        ]

    count = width + 2 * EDGE

    for z in range(depth):
        for copy in ring_copies(z):
            copy.start()
    for z in range(depth):
        start_side(0, *sides[0], z)
    for z in range(depth):
        for copy in ring_copies(z):
            copy.wait_recv()
        await_side(0, *sides[0], z)
        hydro(0, z, lambda f: A[f, z], lambda f, own: edges(own, L0[f, z], R0[f, z]))

    for step in range(STEPS):
        for z in range(depth):
            for f in range(fields):
                pass_on(step, f, z)
        O, L, R = sides[step + 1]
        for z in range(depth):
            for f in range(fields):
                for copies in gather_copies(step, f, z)[1]:
                    copies[0].wait_recv()
                start = base - first_row - EDGE
                O[f, z] = shifted(windows[step][f, z, first_row:], start - shifts[...], count, start - SMIN)
            start_side(step + 1, O, L, R, z)
        for z in range(depth):
            await_side(step + 1, O, L, R, z)
            state = [wide(O[f, z], edges(O[f, z], L[f, z], R[f, z])) for f in range(fields)]
            if step == STEPS - 1:
                new = viscous(z, state, False)
                for f in range(fields):
                    out[f, z] = new[f][EDGE : EDGE + width]
            else:
                new = viscous(z, state, True)
                A_rows = slice(TILE - EDGE, TILE - EDGE + count)
                for f in range(fields):
                    A[f, z, A_rows, :] = new[f][:, :lanes]
                hydro(
                    step + 1,
                    z,
                    lambda f: A[f, z],
                    lambda f, own: edges(own, *[new[f][EDGE : EDGE + width, lanes:]] * 2),
                )

    for z in range(depth):
        for copy in ring_copies(z):
            copy.wait_send()
        for phase in range(STEPS + 1):
            end_side(phase, *sides[phase], z)
        for step in range(STEPS):
            for f in range(fields):
                onward, inside = gather_copies(step, f, z)
                onward.wait_send()
                for copies in inside:
                    copies[0].wait_send()


def body(mesh, state, shifts):
    n_az, n_rad = mesh.shape["az"], mesh.shape["rad"]
    fields, depth, width, lanes = state.shape
    behind = SMAX + EDGE
    group = behind // width + 1
    window = (group + 1) * width
    count = width + 2 * EDGE
    vmem = lambda rows: pltpu.VMEM((fields, depth, rows, lanes), jnp.float32)
    dma = pltpu.SemaphoreType.DMA
    return pl.pallas_call(
        functools.partial(kernel, n_az, n_rad),
        out_shape=pltpu.VMEM(state.shape, state.dtype),
        in_specs=[pl.BlockSpec(memory_space=pl.ANY), pl.BlockSpec(memory_space=pltpu.VMEM)],
        out_specs=pl.BlockSpec(memory_space=pltpu.VMEM),
        scratch_shapes=[
            vmem(width),
            dma(()),
            vmem(width + 2 * TILE),
            vmem(window),
            vmem(window),
            vmem(count),
            vmem(count),
            vmem(width),
            vmem(width),
            vmem(count),
            vmem(count),
            vmem(count),
            vmem(count),
            dma((2, depth)),
            dma((2, depth)),
            dma((STEPS, group, fields, depth)),
            dma((STEPS, group, fields, depth)),
            dma((STEPS + 1, 2, depth)),
            dma((STEPS + 1, 2, depth)),
        ],
        compiler_params=pltpu.CompilerParams(collective_id=0, has_side_effects=True),
    )(state, shifts.reshape(1, -1))


GROUPS = 4


def lane_rows(x, shift):
    return pltpu.roll(x, shift % x.shape[1], 1)


def exchange(parts, lane):
    n = len(parts)
    out = [parts[-g % n] for g in range(n)]
    for bit in range(n.bit_length() - 1):
        far = (lane & (TILE << bit)) != 0
        out = [jnp.where(far, out[(g - (1 << bit)) % n], out[g]) for g in range(n)]
    return out


def fold(x, lane, row):
    half = x.shape[1] // 2
    stay = (lane < half) == (row < TILE // 2)
    return jnp.where(stay, x, lane_rows(pltpu.roll(x, TILE // 2, 0), half))


def line(tiles):
    return jnp.concatenate(tiles, axis=0)


def tiles_of(x):
    return [x[g * TILE : (g + 1) * TILE] for g in range(GROUPS)]


def next_of(x, axis):
    first = x[:TILE]
    return jnp.concatenate([x[TILE:], pltpu.roll(first, first.shape[axis] - 1, axis)], axis=0)


def last_of(x, axis):
    last = x[-TILE:]
    return jnp.concatenate([pltpu.roll(last, 1, axis), x[:-TILE]], axis=0)


def along(field, w):
    return line([field[u][w] for u in range(GROUPS)])


def across(field, u):
    return line(field[u])


def line_speeds(velocity, axis, courant):
    face = (0.5 * courant) * (velocity + next_of(velocity, axis))
    return jnp.maximum(face, 0.0), jnp.minimum(face, 0.0)


def line_advect(field, speeds, axis):
    low = field - last_of(field, axis)
    high = next_of(low, axis)
    product = low * high
    half = jnp.where(product > 0, product / (low + high), 0.0)
    flux = speeds[0] * (field + half) + speeds[1] * next_of(field - half, axis)
    return flux - last_of(flux, axis)


def line_push(pressure, density, speed, axis, courant):
    compress = jnp.minimum(next_of(speed, axis) - last_of(speed, axis), 0.0)
    total = pressure + VISCOSITY_COEF * density * compress * compress
    work = total * speed
    scale = -0.5 * courant
    return scale * (next_of(total, axis) - last_of(total, axis)), scale * (next_of(work, axis) - last_of(work, axis))


def advect_all(state):
    rho, mr, mp = state[:3]
    az_speeds, rad_speeds = [], []
    inverse = [tiles_of(1.0 / across(rho, u)) for u in range(GROUPS)]
    for g in range(GROUPS):
        az_speeds.append(line_speeds(along(mp, g) * along(inverse, g), 1, COURANT_AZIMUTH))
        rad_speeds.append(line_speeds(across(mr, g) * across(inverse, g), 0, COURANT_RADIAL))

    def step(field):
        turned = [along(field, w) for w in range(GROUPS)]
        turned = [tiles_of(turned[w] - line_advect(turned[w], az_speeds[w], 1)) for w in range(GROUPS)]
        out = []
        for u in range(GROUPS):
            rest = line([turned[w][u] for w in range(GROUPS)])
            out.append(tiles_of(rest - line_advect(across(field, u), rad_speeds[u], 0)))
        return out

    return step


def push_all(state):
    rho, mr, mp, mz, energy = state
    inverse, pressure, new_mr, rest = [], [], [], []
    for u in range(GROUPS):
        r, a, b, c, e = (across(f, u) for f in state)
        inv = 1.0 / r
        p = (GAMMA_GAS - 1.0) * (e - 0.5 * (a * a + b * b + c * c) * inv)
        rad_m, rad_e = line_push(p, r, a * inv, 0, COURANT_RADIAL)
        inverse.append(tiles_of(inv))
        pressure.append(tiles_of(p))
        new_mr.append(tiles_of(a + rad_m))
        rest.append(tiles_of(e + rad_e))
    new_mp = [[None] * GROUPS for _ in range(GROUPS)]
    new_energy = [[None] * GROUPS for _ in range(GROUPS)]
    for w in range(GROUPS):
        b = along(mp, w)
        az_m, az_e = line_push(along(pressure, w), along(rho, w), b * along(inverse, w), 1, COURANT_AZIMUTH)
        for u, (m, e) in enumerate(zip(tiles_of(b + az_m), tiles_of(along(rest, w) + az_e))):
            new_mp[u][w], new_energy[u][w] = m, e
    return new_mr, new_mp, new_energy


def turned_kernel(n_az, n_rad, x_in, shifts, out, *scratch):
    (x, T4, EP, M, W, other, SC, AM, F, G, B, R, load_sem, shift_sem, swap_sem, out_send, out_recv, pass_send, pass_recv,
     back_send, back_recv) = scratch
    fields, depth, width, lanes = x.shape
    blocks = n_az // (depth * n_rad)
    tiles = lanes // TILE
    rows = 4 * TILE
    MESH = pl.DeviceIdType.MESH
    me = lax.axis_index("az")
    core = lax.axis_index("rad")
    half = lax.rem(me, n_rad)
    layer = lax.rem(me // n_rad, depth)
    block = me // (n_rad * depth)
    place = (half * blocks + block) * 2 + core
    partner = {"rad": 1 - core}
    here = half == core

    def remote(src, dst, send, recv, where):
        return pltpu.make_async_remote_copy(
            src_ref=src, dst_ref=dst, send_sem=send, recv_sem=recv, device_id=where, device_id_type=MESH
        )

    loads = [pltpu.make_async_copy(x_in.at[:, l], x.at[:, l], load_sem.at[l]) for l in range(depth)]
    for load in loads:
        load.start()
    barrier = pltpu.get_barrier_semaphore()
    for k in range(1, n_az):
        pl.semaphore_signal(
            barrier, inc=1, device_id={"az": lax.rem(me + k, n_az), "rad": half}, device_id_type=MESH
        )
    pl.semaphore_signal(barrier, inc=1, device_id=partner, device_id_type=MESH)

    lane = lax.broadcasted_iota(jnp.int32, (TILE, lanes), 1)
    row = lax.broadcasted_iota(jnp.int32, (TILE, lanes), 0)
    group = lane // width

    spin = me * TILE

    def rows_of(f, l):
        return [x[f, l, pl.ds(u, width // GROUPS, stride=GROUPS), :] for u in range(GROUPS)]

    for l in range(depth):
        loads[l].wait()
        cells = jnp.concatenate([part for f in range(GROUPS) for part in rows_of(f, l)], axis=0)
        T4[l, 1 : tiles + 1] = pltpu.roll(cells.T, spin, 1).reshape(tiles, TILE, lanes)
    energy = [part for l in range(depth) for part in rows_of(4, l)]
    turned = jnp.concatenate(energy * (lanes // (depth * width)), axis=0).T.reshape(tiles, TILE, lanes)
    for l in range(depth):
        for m in range(tiles // GROUPS):
            packed = turned[GROUPS * m] if l == 0 else lane_rows(turned[GROUPS * m], -width * l)
            for g in range(1, GROUPS):
                packed = jnp.where(group == g, lane_rows(turned[GROUPS * m + g], width * (g - l)), packed)
            EP[l, 1 + m] = packed

    @pl.when(core == 0)
    def _():
        for l in range(depth):
            T4[l, 0] = jnp.broadcast_to(T4[l, 1, 0:1], (TILE, lanes))
            EP[l, 0] = jnp.broadcast_to(lane_rows(EP[l, 1], -width)[0:1], (TILE, lanes))

    @pl.when(core == 1)
    def _():
        for l in range(depth):
            T4[l, tiles + 1] = jnp.broadcast_to(T4[l, tiles, TILE - 1 : TILE], (TILE, lanes))
            EP[l, blocks + 1] = jnp.broadcast_to(lane_rows(EP[l, blocks], width)[TILE - 1 : TILE], (TILE, lanes))

    def stage(l, s, c):
        own = EP[l, 1 + s]
        if c == 0:
            M[l, s, c, 0] = pltpu.roll(jnp.where(group == GROUPS - 1, EP[l, s], own), lax.rem(spin + width, lanes), 1)
            M[l, s, c, 1:3] = T4[l, GROUPS * s : GROUPS * s + 2]
        else:
            M[l, s, c, 1:3] = T4[l, GROUPS * s + 4 : GROUPS * s + 6]
            M[l, s, c, 3] = pltpu.roll(jnp.where(group == 0, EP[l, s + 2], own), lax.rem(spin + lanes - width, lanes), 1)

    late = ((0, 0), (blocks - 1, 1))
    for l in range(depth):
        for s in range(blocks):
            for c in range(2):
                M[l, s, c, 3 - 3 * c] = T4[l, GROUPS * s + 2 + c]
                if (s, c) not in late:
                    stage(l, s, c)

    senders = jnp.where(here, 2 * (n_az // n_rad - 1) + 1, 2 * (n_az // n_rad) + 1)
    pl.semaphore_wait(barrier, senders)

    swap_shift = remote(shifts, other, shift_sem.at[0], shift_sem.at[1], partner)
    swap_shift.start()

    def swaps(l, up):
        src = (tiles, blocks) if up else (1, 1)
        dst = (0, 0) if up else (tiles + 1, blocks + 1)
        return [
            remote(T4.at[l, src[0]], T4.at[l, dst[0]], swap_sem.at[0, l], swap_sem.at[1, l], partner),
            remote(EP.at[l, src[1]], EP.at[l, dst[1]], swap_sem.at[2, l], swap_sem.at[3, l], partner),
        ]

    @pl.when(core == 0)
    def _():
        for l in range(depth):
            for copy in swaps(l, True):
                copy.start()

    @pl.when(core == 1)
    def _():
        for l in range(depth):
            for copy in swaps(l, False):
                copy.start()

    targets = [(ks, kl, kc) for ks in (2, 1, 3, 0) for kl in range(depth) for kc in (1, 0)]

    def send(index, first):
        ks, kl, kc = targets[index]
        s = lax.rem(block + ks, blocks)
        l = lax.rem(layer + kl, depth)
        c = lax.rem(core + kc, 2)
        if first:
            src, dst = M.at[l, s, c, 3 - 3 * c], W.at[me, 3 - 2 * c]
            sems = out_send.at[0, index], out_recv.at[0, me]
        else:
            src, dst = M.at[l, s, c, pl.ds(c, 3)], W.at[me, pl.ds(2 * c, 3)]
            sems = out_send.at[1, index], out_recv.at[1, me]
        sent = remote(src, dst, *sems, {"az": (s * depth + l) * n_rad + core, "rad": c})
        is_late = s == c * (blocks - 1)
        return sent, None if ks or kl or kc else pltpu.make_async_copy(src, dst, sems[1]), is_late

    def start(first, when=None):
        for index in range(len(targets)):
            sent, within, is_late = send(index, first)
            if within is None and when is None:
                sent.start()
                continue
            now = True if when is None else when(is_late)
            for copy, also in ((sent, None),) if within is None else ((within, here), (sent, jnp.logical_not(here))):

                @pl.when(now if also is None else jnp.logical_and(now, also))
                def _():
                    copy.start()

    start(True)
    start(False, jnp.logical_not)
    for l in range(depth):
        for copy in swaps(l, True):
            copy.wait_recv()
    for l in range(depth):
        for s, c in late:
            stage(l, s, c)
    start(False, lambda is_late: is_late)

    swap_shift.wait_recv()
    lower = jnp.full((1, lanes), core, jnp.int32) == 0
    mine, theirs = shifts[...], other[...]
    for c in range(2):
        part = jnp.where(lower, mine if c == 0 else theirs, theirs if c == 0 else mine)
        table = jnp.broadcast_to(part.astype(jnp.float32), (lanes, lanes)).T.astype(jnp.int32)
        SC[TILE + c * lanes : TILE + (c + 1) * lanes] = table
    SC[0:TILE] = jnp.zeros((TILE, lanes), jnp.int32)
    SC[TILE + 2 * lanes :] = jnp.zeros((TILE, lanes), jnp.int32)
    AM[...] = SC[pl.ds(pl.multiple_of(place * 2 * TILE, TILE), rows)]
    amounts = [AM[pl.ds(w, TILE, stride=GROUPS), :] for w in range(GROUPS)]
    coarse = [amount // GROUPS for amount in amounts]
    odd = [(amount & 1) != 0 for amount in amounts]
    two = [(amount & 2) != 0 for amount in amounts]
    source = [
        [(lane - coarse[w] - jnp.where(u < (amounts[w] & (GROUPS - 1)), 1, 0)) & (lanes - 1) for w in range(GROUPS)]
        for u in range(GROUPS)
    ]

    plane = n_az // GROUPS
    near = [lax.rem(me // plane + k, GROUPS) for k in (0, 1, 3, 2)]

    def passes(k):
        ahead = pl.ds(near[k] * plane, plane)
        return remote(W.at[ahead, 3 - 2 * core], W.at[ahead, 4 * core], pass_send.at[k], pass_recv.at[near[k]], partner)

    def passed(q):
        return remote(
            W.at[pl.ds(q * plane, plane), 3 - 2 * core], W.at[pl.ds(q * plane, plane), 4 - 4 * core],
            pass_send.at[q], pass_recv.at[q], partner
        )

    def arrived(dst, recv):
        return pltpu.make_async_copy(dst, dst, recv)

    for k in range(GROUPS):
        for j in range(plane):
            i = near[k] * plane + lax.rem(me + j, plane)
            arrived(W.at[i, 3 - 2 * core], out_recv.at[0, i]).wait()
        passes(k).start()

    def rotate(field):
        out = [[None] * GROUPS for _ in range(GROUPS)]
        for w in range(GROUPS):
            near_by = [jnp.where(odd[w], field[u - 1][w], field[u][w]) for u in range(GROUPS)]
            for u in range(GROUPS):
                chosen = jnp.where(two[w], near_by[u - 2], near_by[u])
                out[u][w] = jnp.take_along_axis(chosen, source[u][w], axis=1)
        return out

    at = jnp.full((TILE, lanes), place, jnp.int32)
    lowest = jnp.logical_and(at == 0, row < 2)
    highest = jnp.logical_and(at == 2 * blocks * n_rad - 1, row >= TILE - 2)

    def edged(field):
        out = []
        for u in range(GROUPS):
            low = jnp.broadcast_to(field[u][0][2:3], (TILE, lanes))
            high = jnp.broadcast_to(field[u][3][TILE - 3 : TILE - 2], (TILE, lanes))
            out.append(
                [jnp.where(highest, high, field[u][w]) for w in range(2)]
                + [jnp.where(lowest, low, field[u][w]) for w in range(2, GROUPS)]
            )
        return out

    def unpack(parts):
        return [lane_rows(part, -TILE * g) for g, part in enumerate(exchange(parts, lane_of[parts[0].shape[0]]))]

    lane_of = {n * TILE: lax.broadcasted_iota(jnp.int32, (n * TILE, lanes), 1) for n in (1, 2, 3)}

    for k in range(GROUPS):
        for j in range(plane):
            i = near[k] * plane + lax.rem(me + j, plane)
            arrived(W.at[i, pl.ds(2 * core, 3)], out_recv.at[1, i]).wait()
    direct = unpack([W[i, 1:4].reshape(3 * TILE, lanes) for i in range(n_az)])
    for g in range(GROUPS * GROUPS):
        F[g, pl.ds(pl.multiple_of(core * TILE, TILE), 3 * TILE)] = direct[g]
    for g, part in enumerate(unpack([W[i, 4 * core] for i in range(n_az)])):
        w, u = g // GROUPS, g % GROUPS
        F[GROUPS * GROUPS + u, w * TILE : (w + 1) * TILE] = part
    for q in range(GROUPS):
        passed(q).wait_recv()
    for g, part in enumerate(unpack([W[i, 4 - 4 * core] for i in range(n_az)])):
        F[g, pl.ds(pl.multiple_of((1 - core) * 3 * TILE, TILE), TILE)] = part

    state = [
        [[F[GROUPS * f + u, pl.ds(w, TILE, stride=GROUPS), :] for w in range(GROUPS)] for u in range(GROUPS)]
        for f in range(fields)
    ]
    step = advect_all(state)
    state = [edged(rotate(step(field))) for field in state]
    mr, mp, en = push_all(state)
    state = [edged(field) for field in (state[0], mr, mp, state[3], en)]
    step = advect_all(state)
    state = [edged(rotate(step(field))) for field in state]
    mr, mp, en = push_all(state)
    for f, field in enumerate((state[0], mr, mp, state[3], en)):
        for u in range(GROUPS):
            for w in range(GROUPS):
                G[GROUPS * f + u, pl.ds(w, TILE, stride=GROUPS), :] = field[u][w]

    order = [(k, j) for k in (2, 1, 3, 0) for j in [*range(1, plane), 0]]

    def back(index):
        k, j = order[index]
        i = lax.rem(me // plane + k, GROUPS) * plane + lax.rem(me + j, plane)
        src, dst = B.at[i], R.at[layer, block, core]
        sems = back_send.at[index], back_recv.at[(layer * blocks + block) * 2 + core]
        sent = remote(src, dst, *sems, {"az": i, "rad": half})
        return sent, None if k or j else pltpu.make_async_copy(src, dst, sems[1])

    own = [lane_rows(G[g, TILE : 3 * TILE], TILE * g) for g in range(GROUPS * GROUPS)]
    for i, part in enumerate(exchange(own, lane_of[2 * TILE])):
        B[i, : 2 * TILE] = part
    own = [
        lane_rows(G[GROUPS * GROUPS + u, (1 + t) * TILE : (2 + t) * TILE], TILE * (GROUPS * t + u))
        for t in range(2)
        for u in range(GROUPS)
    ]
    for i, part in enumerate(exchange(own, lane)):
        folded = fold(lane_rows(part, -TILE * i), lane, row)
        B[i, 2 * TILE :] = folded[: TILE // 2]
        B[i + n_az // 2, 2 * TILE :] = folded[TILE // 2 :]
    for index in range(len(order)):
        sent, within = back(index)
        if within is None:
            sent.start()
        else:

            @pl.when(here)
            def _():
                within.start()

            @pl.when(jnp.logical_not(here))
            def _():
                sent.start()

    for l in range(depth):
        for s in range(blocks):
            for c in range(2):
                arrived(R.at[l, s, c], back_recv.at[(l * blocks + s) * 2 + c]).wait()
    for l in range(depth):
        pieces = [R[l, s, c, : 2 * TILE] for s in range(blocks) for c in range(2)]
        cells = pltpu.roll(jnp.concatenate(pieces, axis=0), lax.rem(lanes - spin, lanes), 1).T
        for f in range(GROUPS):
            for u in range(GROUPS):
                g = GROUPS * f + u
                out[f, l, pl.ds(u, TILE, stride=GROUPS), :] = cells[g * TILE : (g + 1) * TILE]
    pieces = []
    for s in range(blocks):
        both = [fold(jnp.concatenate([R[l, s, c, 2 * TILE :] for c in range(2)], axis=0), lane, row) for l in range(depth)]
        for g in range(GROUPS):
            piece = lane_rows(both[0], -width * g)
            for l in range(1, depth):
                piece = jnp.where(group == l, lane_rows(both[l], width * (l - g)), piece)
            pieces.append(piece)
    cells = jnp.concatenate(pieces, axis=0).T
    for l in range(depth):
        for u in range(GROUPS):
            g = GROUPS * l + u
            out[4, l, pl.ds(u, TILE, stride=GROUPS), :] = cells[g * TILE : (g + 1) * TILE]

    swap_shift.wait_send()
    for l in range(depth):
        for copy in swaps(l, True):
            copy.wait_send()
    for first in (True, False):
        for index in range(len(targets)):
            sent, within, _ = send(index, first)
            if within is None:
                sent.wait_send()
            else:

                @pl.when(jnp.logical_not(here))
                def _():
                    sent.wait_send()

    for k in range(GROUPS):
        passes(k).wait_send()
    for index in range(len(order)):
        sent, within = back(index)
        if within is None:
            sent.wait_send()
        else:

            @pl.when(jnp.logical_not(here))
            def _():
                sent.wait_send()


def turned_body(mesh, state, shifts):
    n_az, n_rad = mesh.shape["az"], mesh.shape["rad"]
    fields, depth, width, lanes = state.shape
    blocks = n_az // (depth * n_rad)
    tiles = lanes // TILE
    vmem = lambda *shape: pltpu.VMEM(shape, jnp.float32)
    dma = pltpu.SemaphoreType.DMA
    tile = (TILE, lanes)
    return pl.pallas_call(
        functools.partial(turned_kernel, n_az, n_rad),
        out_shape=pltpu.VMEM(state.shape, state.dtype),
        in_specs=[pl.BlockSpec(memory_space=pl.ANY), pl.BlockSpec(memory_space=pltpu.VMEM)],
        out_specs=pl.BlockSpec(memory_space=pltpu.VMEM),
        scratch_shapes=[
            vmem(fields, depth, width, lanes),
            vmem(depth, tiles + 2, *tile),
            vmem(depth, blocks + 2, *tile),
            vmem(depth, blocks, 2, 4, *tile),
            vmem(n_az, 5, *tile),
            pltpu.VMEM((1, lanes), jnp.int32),
            pltpu.VMEM((2 * lanes + 2 * TILE, lanes), jnp.int32),
            pltpu.VMEM((4 * TILE, lanes), jnp.int32),
            vmem(GROUPS * fields, 4 * TILE, lanes),
            vmem(GROUPS * fields, 4 * TILE, lanes),
            vmem(n_az, 2 * TILE + TILE // 2, lanes),
            vmem(depth, blocks, 2, 2 * TILE + TILE // 2, lanes),
            dma((depth,)),
            dma((2,)),
            dma((4, depth)),
            dma((2, n_az)),
            dma((2, n_az)),
            dma((GROUPS,)),
            dma((GROUPS,)),
            dma((n_az,)),
            dma((n_az,)),
        ],
        compiler_params=pltpu.CompilerParams(collective_id=0, has_side_effects=True),
    )(state, shifts.reshape(1, -1))


def turns(mesh, state):
    n_az, n_rad = mesh.shape["az"], mesh.shape["rad"]
    fields, depth, width, lanes = state.shape
    tiles = lanes // TILE
    return (
        n_rad == 2
        and fields == GROUPS + 1
        and width * GROUPS == lanes
        and n_az == GROUPS * GROUPS
        and width == GROUPS * TILE
        and lanes == n_az * TILE
        and n_az % (depth * n_rad) == 0
        and tiles == GROUPS * (n_az // (depth * n_rad))
        and depth * width <= lanes
        and SMAX <= lanes
    )


def choose(mesh, state, shifts):
    return (turned_body if turns(mesh, state) else body)(mesh, state, shifts)


def solution(mesh):
    in_specs = (P(None, None, "az", "rad"), P("rad"))
    out_specs = P(None, None, "az", "rad")
    return jax.shard_map(
        functools.partial(choose, mesh), mesh=mesh, in_specs=in_specs, out_specs=out_specs, check_vma=False
    )
```

```python
import functools

import jax
import jax.numpy as jnp
from jax import lax
from jax.experimental import pallas as pl
from jax.experimental.pallas import tpu as pltpu
from jax.sharding import PartitionSpec as P

STEPS = 2
SMIN = 4
SMAX = 96
EDGE = 4
TILE = 8

GAMMA_GAS = 1.4
COURANT_RADIAL = 0.15
COURANT_AZIMUTH = 0.15
VISCOSITY_COEF = 1.0


def up(x, axis):
    return pltpu.roll(x, x.shape[axis] - 1, axis)


def down(x, axis):
    return pltpu.roll(x, 1, axis)


def face_speeds(velocity, axis, courant):
    face = (0.5 * courant) * (velocity + up(velocity, axis))
    return jnp.maximum(face, 0.0), jnp.minimum(face, 0.0)


def advect(field, speeds, axis):
    low = field - down(field, axis)
    high = up(low, axis)
    product = low * high
    positive = product > 0
    half = jnp.where(positive, product / jnp.where(positive, low + high, 1.0), 0.0)
    flux = speeds[0] * (field + half) + speeds[1] * up(field - half, axis)
    return flux - down(flux, axis)


def push(pressure, density, speed, axis, courant):
    compress = jnp.minimum(up(speed, axis) - down(speed, axis), 0.0)
    total = pressure + VISCOSITY_COEF * density * compress * compress
    work = total * speed
    scale = -0.5 * courant
    return scale * (up(total, axis) - down(total, axis)), scale * (up(work, axis) - down(work, axis))


def shifted(window, shift_left, rows, longest):
    bits = longest.bit_length()
    x = window
    for bit in reversed(range(bits)):
        stride = 1 << bit
        left = stride - 1
        if stride >= TILE:
            keep = -(-(rows + left) // TILE) * TILE
            chosen = min(keep, x.shape[0] - stride)
            mask = (jnp.broadcast_to(shift_left, (chosen, shift_left.shape[1])) & stride) != 0
            y = jnp.where(mask, x[stride : stride + chosen], x[:chosen])
            x = y if chosen == keep else jnp.concatenate([y, x[chosen:keep]], axis=0)
        else:
            mask = (jnp.broadcast_to(shift_left, x.shape) & stride) != 0
            x = jnp.where(mask, pltpu.roll(x, x.shape[0] - stride, 0), x)
    return x[:rows]


def kernel(n_az, n_rad, x_in, shifts, out, *scratch):
    (x, load_sem, A, W0, W1, O0, O1, L0, R0, L1, R1, L2, R2, state_send, state_recv, gather_send, gather_recv,
     side_send, side_recv) = scratch
    fields, depth, width, lanes = x.shape
    behind = SMAX + EDGE
    whole = behind // width
    tail = behind % width
    tail_rows = -(-tail // TILE) * TILE
    group = whole + 1
    base = group * width
    first_row = width - tail_rows
    me = lax.axis_index("az")
    place = lax.rem(me, group)
    position = lax.axis_index("rad")

    def az(by):
        return {"az": lax.rem(me + by + n_az, n_az)}

    def member(by):
        return {"az": me - place + lax.rem(place + by + group, group)}

    def rad(by):
        return {"rad": position + by}

    barrier = pltpu.get_barrier_semaphore()
    MESH = pl.DeviceIdType.MESH
    load = pltpu.make_async_copy(x_in, x, load_sem)
    load.start()
    for by in (1, -1, -group):
        pl.semaphore_signal(barrier, inc=1, device_id=az(by), device_id_type=MESH)
    for h in range(1, group):
        pl.semaphore_signal(barrier, inc=1, device_id=member(h), device_id_type=MESH)

    has_left = position > 0
    has_right = position < n_rad - 1

    @pl.when(has_left)
    def _():
        pl.semaphore_signal(barrier, inc=1, device_id=rad(-1), device_id_type=MESH)

    @pl.when(has_right)
    def _():
        pl.semaphore_signal(barrier, inc=1, device_id=rad(1), device_id_type=MESH)

    load.wait()
    A[:, :, TILE : TILE + width, :] = x[...]
    beside_me = (position + n_rad - 1) // n_rad + (2 * n_rad - 2 - position) // n_rad
    pl.semaphore_wait(barrier, group + 2 + beside_me)

    def remote(src, dst, send, recv, where):
        return pltpu.make_async_remote_copy(
            src_ref=src, dst_ref=dst, send_sem=send, recv_sem=recv, device_id=where, device_id_type=MESH
        )

    def ring_copies(z):
        return [
            remote(x.at[:, z, width - TILE : width], A.at[:, z, 0:TILE],
                   state_send.at[0, z], state_recv.at[0, z], az(1)),
            remote(x.at[:, z, 0:TILE], A.at[:, z, TILE + width : 2 * TILE + width],
                   state_send.at[1, z], state_recv.at[1, z], az(-1)),
        ]

    def side_copies(phase, src, left_dst, right_dst, z):
        to_right = remote(src.at[:, z], left_dst.at[:, z], side_send.at[phase, 0, z],
                          side_recv.at[phase, 0, z], rad(1))
        to_left = remote(src.at[:, z], right_dst.at[:, z], side_send.at[phase, 1, z],
                         side_recv.at[phase, 1, z], rad(-1))
        return to_right, to_left

    def start_side(*args):
        to_right, to_left = side_copies(*args)

        @pl.when(has_right)
        def _():
            to_right.start()

        @pl.when(has_left)
        def _():
            to_left.start()

    def await_side(*args):
        to_right, to_left = side_copies(*args)

        @pl.when(has_left)
        def _():
            to_right.wait_recv()

        @pl.when(has_right)
        def _():
            to_left.wait_recv()

    def end_side(*args):
        to_right, to_left = side_copies(*args)

        @pl.when(has_right)
        def _():
            to_right.wait_send()

        @pl.when(has_left)
        def _():
            to_left.wait_send()

    windows = (W0, W1)
    rotated = (O0, O1)
    sides = ((x, L0, R0), (O0, L1, R1), (O1, L2, R2))

    def gather_copies(step, f, z):
        W = windows[step]
        own, back = W.at[f, z, base : base + width], W.at[f, z, 0:width]
        sems = lambda h: (gather_send.at[step, h, f, z], gather_recv.at[step, h, f, z])
        onward = remote(own, back, *sems(0), az(group))
        inside = []
        for h in range(1, group):
            dst = W.at[f, z, base - h * width : base - (h - 1) * width]
            inside.append([remote(src, dst, *sems(h), member(h)) for src in (own, back)])
        return onward, inside

    def send_own(step, f, z):
        onward, inside = gather_copies(step, f, z)
        onward.start()
        for h in range(1, group):

            @pl.when(place + h < group)
            def _():
                inside[h - 1][0].start()

    def pass_on(step, f, z):
        onward, inside = gather_copies(step, f, z)
        onward.wait_recv()
        for h in range(1, group):

            @pl.when(place + h >= group)
            def _():
                inside[h - 1][1].start()

    def edges(own, left, right):
        rows = own.shape[0]
        lane = lax.broadcasted_iota(jnp.int32, (rows, lanes), 1)
        at = jnp.full((rows, lanes), position, jnp.int32)
        left = jnp.where(at == 0, jnp.broadcast_to(own[:, 0:1], own.shape), left)
        right = jnp.where(at == n_rad - 1, jnp.broadcast_to(own[:, lanes - 1 : lanes], own.shape), right)
        return jnp.where(lane < lanes // 2, right, left)

    def wide(own, beside):
        return jnp.concatenate([own, beside], axis=1)

    def hydro(step, z, strip, beside):
        rows = slice(TILE, TILE + width)
        tall = [strip(f) for f in range(fields)]
        az_speeds = face_speeds(tall[2] / tall[0], 0, COURANT_AZIMUTH)
        broad = [wide(tall[f][rows], beside(f, tall[f][rows])) for f in range(fields)]
        rad_speeds = face_speeds(broad[1] / broad[0], 1, COURANT_RADIAL)
        for f in range(fields):
            along = advect(tall[f], az_speeds, 0)[rows]
            across = advect(broad[f], rad_speeds, 1)[:, :lanes]
            windows[step][f, z, base : base + width, :] = tall[f][rows] - along - across
            send_own(step, f, z)

    def viscous(z, state, extended):
        rho, mr, mp, mz, energy = state
        own = slice(None) if extended else slice(0, lanes)
        inverse = 1.0 / rho
        pressure = (GAMMA_GAS - 1.0) * (energy - 0.5 * (mr * mr + mp * mp + mz * mz) * inverse)
        az_m, az_e = push(pressure[:, own], rho[:, own], (mp * inverse)[:, own], 0, COURANT_AZIMUTH)
        rad_m, rad_e = push(pressure, rho, mr * inverse, 1, COURANT_RADIAL)
        return [
            rho[:, own],
            mr[:, own] + rad_m[:, own],
            mp[:, own] + az_m,
            mz[:, own],
            energy[:, own] + az_e + rad_e[:, own],
        ]

    count = width + 2 * EDGE

    for z in range(depth):
        for copy in ring_copies(z):
            copy.start()
    for z in range(depth):
        start_side(0, *sides[0], z)
    for z in range(depth):
        for copy in ring_copies(z):
            copy.wait_recv()
        await_side(0, *sides[0], z)
        hydro(0, z, lambda f: A[f, z], lambda f, own: edges(own, L0[f, z], R0[f, z]))

    for step in range(STEPS):
        for z in range(depth):
            for f in range(fields):
                pass_on(step, f, z)
        O, L, R = sides[step + 1]
        for z in range(depth):
            for f in range(fields):
                for copies in gather_copies(step, f, z)[1]:
                    copies[0].wait_recv()
                start = base - first_row - EDGE
                O[f, z] = shifted(windows[step][f, z, first_row:], start - shifts[...], count, start - SMIN)
            start_side(step + 1, O, L, R, z)
        for z in range(depth):
            await_side(step + 1, O, L, R, z)
            state = [wide(O[f, z], edges(O[f, z], L[f, z], R[f, z])) for f in range(fields)]
            if step == STEPS - 1:
                new = viscous(z, state, False)
                for f in range(fields):
                    out[f, z] = new[f][EDGE : EDGE + width]
            else:
                new = viscous(z, state, True)
                A_rows = slice(TILE - EDGE, TILE - EDGE + count)
                for f in range(fields):
                    A[f, z, A_rows, :] = new[f][:, :lanes]
                hydro(
                    step + 1,
                    z,
                    lambda f: A[f, z],
                    lambda f, own: edges(own, *[new[f][EDGE : EDGE + width, lanes:]] * 2),
                )

    for z in range(depth):
        for copy in ring_copies(z):
            copy.wait_send()
        for phase in range(STEPS + 1):
            end_side(phase, *sides[phase], z)
        for step in range(STEPS):
            for f in range(fields):
                onward, inside = gather_copies(step, f, z)
                onward.wait_send()
                for copies in inside:
                    copies[0].wait_send()


def body(mesh, state, shifts):
    n_az, n_rad = mesh.shape["az"], mesh.shape["rad"]
    fields, depth, width, lanes = state.shape
    behind = SMAX + EDGE
    group = behind // width + 1
    window = (group + 1) * width
    count = width + 2 * EDGE
    vmem = lambda rows: pltpu.VMEM((fields, depth, rows, lanes), jnp.float32)
    dma = pltpu.SemaphoreType.DMA
    return pl.pallas_call(
        functools.partial(kernel, n_az, n_rad),
        out_shape=pltpu.VMEM(state.shape, state.dtype),
        in_specs=[pl.BlockSpec(memory_space=pl.ANY), pl.BlockSpec(memory_space=pltpu.VMEM)],
        out_specs=pl.BlockSpec(memory_space=pltpu.VMEM),
        scratch_shapes=[
            vmem(width),
            dma(()),
            vmem(width + 2 * TILE),
            vmem(window),
            vmem(window),
            vmem(count),
            vmem(count),
            vmem(width),
            vmem(width),
            vmem(count),
            vmem(count),
            vmem(count),
            vmem(count),
            dma((2, depth)),
            dma((2, depth)),
            dma((STEPS, group, fields, depth)),
            dma((STEPS, group, fields, depth)),
            dma((STEPS + 1, 2, depth)),
            dma((STEPS + 1, 2, depth)),
        ],
        compiler_params=pltpu.CompilerParams(collective_id=0, has_side_effects=True),
    )(state, shifts.reshape(1, -1))


GROUPS = 4


def lane_rows(x, shift):
    return pltpu.roll(x, shift % x.shape[1], 1)


def exchange(parts, lane):
    n = len(parts)
    out = [parts[-g % n] for g in range(n)]
    for bit in range(n.bit_length() - 1):
        far = (lane & (TILE << bit)) != 0
        out = [jnp.where(far, out[(g - (1 << bit)) % n], out[g]) for g in range(n)]
    return out


def fold(x, lane, row):
    half = x.shape[1] // 2
    stay = (lane < half) == (row < TILE // 2)
    return jnp.where(stay, x, lane_rows(pltpu.roll(x, TILE // 2, 0), half))


def line(tiles):
    return jnp.concatenate(tiles, axis=0)


def tiles_of(x):
    return [x[g * TILE : (g + 1) * TILE] for g in range(GROUPS)]


def next_of(x, axis):
    first = x[:TILE]
    return jnp.concatenate([x[TILE:], pltpu.roll(first, first.shape[axis] - 1, axis)], axis=0)


def last_of(x, axis):
    last = x[-TILE:]
    return jnp.concatenate([pltpu.roll(last, 1, axis), x[:-TILE]], axis=0)


def along(field, w):
    return line([field[u][w] for u in range(GROUPS)])


def across(field, u):
    return line(field[u])


def line_speeds(velocity, axis, courant):
    face = (0.5 * courant) * (velocity + next_of(velocity, axis))
    return jnp.maximum(face, 0.0), jnp.minimum(face, 0.0)


def line_advect(field, speeds, axis):
    low = field - last_of(field, axis)
    high = next_of(low, axis)
    product = low * high
    half = jnp.where(product > 0, product / (low + high), 0.0)
    flux = speeds[0] * (field + half) + speeds[1] * next_of(field - half, axis)
    return flux - last_of(flux, axis)


def line_push(pressure, density, speed, axis, courant):
    compress = jnp.minimum(next_of(speed, axis) - last_of(speed, axis), 0.0)
    total = pressure + VISCOSITY_COEF * density * compress * compress
    work = total * speed
    scale = -0.5 * courant
    return scale * (next_of(total, axis) - last_of(total, axis)), scale * (next_of(work, axis) - last_of(work, axis))


def advect_all(state):
    rho, mr, mp = state[:3]
    az_speeds, rad_speeds = [], []
    inverse = [tiles_of(1.0 / across(rho, u)) for u in range(GROUPS)]
    for g in range(GROUPS):
        az_speeds.append(line_speeds(along(mp, g) * along(inverse, g), 1, COURANT_AZIMUTH))
        rad_speeds.append(line_speeds(across(mr, g) * across(inverse, g), 0, COURANT_RADIAL))

    def step(field):
        turned = [along(field, w) for w in range(GROUPS)]
        turned = [tiles_of(turned[w] - line_advect(turned[w], az_speeds[w], 1)) for w in range(GROUPS)]
        out = []
        for u in range(GROUPS):
            rest = line([turned[w][u] for w in range(GROUPS)])
            out.append(tiles_of(rest - line_advect(across(field, u), rad_speeds[u], 0)))
        return out

    return step


def push_all(state):
    rho, mr, mp, mz, energy = state
    inverse, pressure, new_mr, rest = [], [], [], []
    for u in range(GROUPS):
        r, a, b, c, e = (across(f, u) for f in state)
        inv = 1.0 / r
        p = (GAMMA_GAS - 1.0) * (e - 0.5 * (a * a + b * b + c * c) * inv)
        rad_m, rad_e = line_push(p, r, a * inv, 0, COURANT_RADIAL)
        inverse.append(tiles_of(inv))
        pressure.append(tiles_of(p))
        new_mr.append(tiles_of(a + rad_m))
        rest.append(tiles_of(e + rad_e))
    new_mp = [[None] * GROUPS for _ in range(GROUPS)]
    new_energy = [[None] * GROUPS for _ in range(GROUPS)]
    for w in range(GROUPS):
        b = along(mp, w)
        az_m, az_e = line_push(along(pressure, w), along(rho, w), b * along(inverse, w), 1, COURANT_AZIMUTH)
        for u, (m, e) in enumerate(zip(tiles_of(b + az_m), tiles_of(along(rest, w) + az_e))):
            new_mp[u][w], new_energy[u][w] = m, e
    return new_mr, new_mp, new_energy


def turned_kernel(n_az, n_rad, x_in, shifts, out, *scratch):
    (x, T4, EP, M, W, other, SC, AM, F, G, B, R, load_sem, shift_sem, swap_sem, out_send, out_recv, pass_send, pass_recv,
     back_send, back_recv) = scratch
    fields, depth, width, lanes = x.shape
    blocks = n_az // (depth * n_rad)
    tiles = lanes // TILE
    rows = 4 * TILE
    MESH = pl.DeviceIdType.MESH
    me = lax.axis_index("az")
    core = lax.axis_index("rad")
    half = lax.rem(me, n_rad)
    layer = lax.rem(me // n_rad, depth)
    block = me // (n_rad * depth)
    place = (half * blocks + block) * 2 + core
    partner = {"rad": 1 - core}
    here = half == core

    def remote(src, dst, send, recv, where):
        return pltpu.make_async_remote_copy(
            src_ref=src, dst_ref=dst, send_sem=send, recv_sem=recv, device_id=where, device_id_type=MESH
        )

    loads = [pltpu.make_async_copy(x_in.at[:, l], x.at[:, l], load_sem.at[l]) for l in range(depth)]
    for load in loads:
        load.start()
    barrier = pltpu.get_barrier_semaphore()
    for k in range(1, n_az):
        pl.semaphore_signal(
            barrier, inc=1, device_id={"az": lax.rem(me + k, n_az), "rad": half}, device_id_type=MESH
        )
    pl.semaphore_signal(barrier, inc=1, device_id=partner, device_id_type=MESH)

    lane = lax.broadcasted_iota(jnp.int32, (TILE, lanes), 1)
    row = lax.broadcasted_iota(jnp.int32, (TILE, lanes), 0)
    group = lane // width

    spin = me * TILE

    def rows_of(f, l):
        return [x[f, l, pl.ds(u, width // GROUPS, stride=GROUPS), :] for u in range(GROUPS)]

    for l in range(depth):
        loads[l].wait()
        cells = jnp.concatenate([part for f in range(GROUPS) for part in rows_of(f, l)], axis=0)
        T4[l, 1 : tiles + 1] = pltpu.roll(cells.T, spin, 1).reshape(tiles, TILE, lanes)
    energy = [part for l in range(depth) for part in rows_of(4, l)]
    turned = jnp.concatenate(energy * (lanes // (depth * width)), axis=0).T.reshape(tiles, TILE, lanes)
    for l in range(depth):
        for m in range(tiles // GROUPS):
            packed = turned[GROUPS * m] if l == 0 else lane_rows(turned[GROUPS * m], -width * l)
            for g in range(1, GROUPS):
                packed = jnp.where(group == g, lane_rows(turned[GROUPS * m + g], width * (g - l)), packed)
            EP[l, 1 + m] = packed

    @pl.when(core == 0)
    def _():
        for l in range(depth):
            T4[l, 0] = jnp.broadcast_to(T4[l, 1, 0:1], (TILE, lanes))
            EP[l, 0] = jnp.broadcast_to(lane_rows(EP[l, 1], -width)[0:1], (TILE, lanes))

    @pl.when(core == 1)
    def _():
        for l in range(depth):
            T4[l, tiles + 1] = jnp.broadcast_to(T4[l, tiles, TILE - 1 : TILE], (TILE, lanes))
            EP[l, blocks + 1] = jnp.broadcast_to(lane_rows(EP[l, blocks], width)[TILE - 1 : TILE], (TILE, lanes))

    def stage(l, s, c):
        own = EP[l, 1 + s]
        if c == 0:
            M[l, s, c, 0] = pltpu.roll(jnp.where(group == GROUPS - 1, EP[l, s], own), lax.rem(spin + width, lanes), 1)
            M[l, s, c, 1:3] = T4[l, GROUPS * s : GROUPS * s + 2]
        else:
            M[l, s, c, 1:3] = T4[l, GROUPS * s + 4 : GROUPS * s + 6]
            M[l, s, c, 3] = pltpu.roll(jnp.where(group == 0, EP[l, s + 2], own), lax.rem(spin + lanes - width, lanes), 1)

    late = ((0, 0), (blocks - 1, 1))
    for l in range(depth):
        for s in range(blocks):
            for c in range(2):
                M[l, s, c, 3 - 3 * c] = T4[l, GROUPS * s + 2 + c]
                if (s, c) not in late:
                    stage(l, s, c)

    senders = jnp.where(here, 2 * (n_az // n_rad - 1) + 1, 2 * (n_az // n_rad) + 1)
    pl.semaphore_wait(barrier, senders)

    swap_shift = remote(shifts, other, shift_sem.at[0], shift_sem.at[1], partner)
    swap_shift.start()

    def swaps(l, up):
        src = (tiles, blocks) if up else (1, 1)
        dst = (0, 0) if up else (tiles + 1, blocks + 1)
        return [
            remote(T4.at[l, src[0]], T4.at[l, dst[0]], swap_sem.at[0, l], swap_sem.at[1, l], partner),
            remote(EP.at[l, src[1]], EP.at[l, dst[1]], swap_sem.at[2, l], swap_sem.at[3, l], partner),
        ]

    @pl.when(core == 0)
    def _():
        for l in range(depth):
            for copy in swaps(l, True):
                copy.start()

    @pl.when(core == 1)
    def _():
        for l in range(depth):
            for copy in swaps(l, False):
                copy.start()

    targets = [(ks, kl, kc) for ks in (2, 1, 3, 0) for kl in range(depth) for kc in (1, 0)]

    def send(index, first):
        ks, kl, kc = targets[index]
        s = lax.rem(block + ks, blocks)
        l = lax.rem(layer + kl, depth)
        c = lax.rem(core + kc, 2)
        if first:
            src, dst = M.at[l, s, c, 3 - 3 * c], W.at[me, 3 - 2 * c]
            sems = out_send.at[0, index], out_recv.at[0, me]
        else:
            src, dst = M.at[l, s, c, pl.ds(c, 3)], W.at[me, pl.ds(2 * c, 3)]
            sems = out_send.at[1, index], out_recv.at[1, me]
        sent = remote(src, dst, *sems, {"az": (s * depth + l) * n_rad + core, "rad": c})
        is_late = s == c * (blocks - 1)
        return sent, None if ks or kl or kc else pltpu.make_async_copy(src, dst, sems[1]), is_late

    def start(first, when=None):
        for index in range(len(targets)):
            sent, within, is_late = send(index, first)
            if within is None and when is None:
                sent.start()
                continue
            now = True if when is None else when(is_late)
            for copy, also in ((sent, None),) if within is None else ((within, here), (sent, jnp.logical_not(here))):

                @pl.when(now if also is None else jnp.logical_and(now, also))
                def _():
                    copy.start()

    start(True)
    start(False, jnp.logical_not)
    for l in range(depth):
        for copy in swaps(l, True):
            copy.wait_recv()
    for l in range(depth):
        for s, c in late:
            stage(l, s, c)
    start(False, lambda is_late: is_late)

    swap_shift.wait_recv()
    lower = jnp.full((1, lanes), core, jnp.int32) == 0
    mine, theirs = shifts[...], other[...]
    for c in range(2):
        part = jnp.where(lower, mine if c == 0 else theirs, theirs if c == 0 else mine)
        table = jnp.broadcast_to(part.astype(jnp.float32), (lanes, lanes)).T.astype(jnp.int32)
        SC[TILE + c * lanes : TILE + (c + 1) * lanes] = table
    SC[0:TILE] = jnp.zeros((TILE, lanes), jnp.int32)
    SC[TILE + 2 * lanes :] = jnp.zeros((TILE, lanes), jnp.int32)
    AM[...] = SC[pl.ds(pl.multiple_of(place * 2 * TILE, TILE), rows)]
    amounts = [AM[pl.ds(w, TILE, stride=GROUPS), :] for w in range(GROUPS)]
    coarse = [amount // GROUPS for amount in amounts]
    odd = [(amount & 1) != 0 for amount in amounts]
    two = [(amount & 2) != 0 for amount in amounts]
    source = [
        [(lane - coarse[w] - jnp.where(u < (amounts[w] & (GROUPS - 1)), 1, 0)) & (lanes - 1) for w in range(GROUPS)]
        for u in range(GROUPS)
    ]

    plane = n_az // GROUPS
    near = [lax.rem(me // plane + k, GROUPS) for k in (0, 1, 3, 2)]

    def passes(k):
        ahead = pl.ds(near[k] * plane, plane)
        return remote(W.at[ahead, 3 - 2 * core], W.at[ahead, 4 * core], pass_send.at[k], pass_recv.at[near[k]], partner)

    def passed(q):
        return remote(
            W.at[pl.ds(q * plane, plane), 3 - 2 * core], W.at[pl.ds(q * plane, plane), 4 - 4 * core],
            pass_send.at[q], pass_recv.at[q], partner
        )

    def arrived(dst, recv):
        return pltpu.make_async_copy(dst, dst, recv)

    for k in range(GROUPS):
        for j in range(plane):
            i = near[k] * plane + lax.rem(me + j, plane)
            arrived(W.at[i, 3 - 2 * core], out_recv.at[0, i]).wait()
        passes(k).start()

    def rotate(field):
        out = [[None] * GROUPS for _ in range(GROUPS)]
        for w in range(GROUPS):
            near_by = [jnp.where(odd[w], field[u - 1][w], field[u][w]) for u in range(GROUPS)]
            for u in range(GROUPS):
                chosen = jnp.where(two[w], near_by[u - 2], near_by[u])
                out[u][w] = jnp.take_along_axis(chosen, source[u][w], axis=1)
        return out

    at = jnp.full((TILE, lanes), place, jnp.int32)
    lowest = jnp.logical_and(at == 0, row < 2)
    highest = jnp.logical_and(at == 2 * blocks * n_rad - 1, row >= TILE - 2)

    def edged(field):
        out = []
        for u in range(GROUPS):
            low = jnp.broadcast_to(field[u][0][2:3], (TILE, lanes))
            high = jnp.broadcast_to(field[u][3][TILE - 3 : TILE - 2], (TILE, lanes))
            out.append(
                [jnp.where(highest, high, field[u][w]) for w in range(2)]
                + [jnp.where(lowest, low, field[u][w]) for w in range(2, GROUPS)]
            )
        return out

    def unpack(parts):
        return [lane_rows(part, -TILE * g) for g, part in enumerate(exchange(parts, lane_of[parts[0].shape[0]]))]

    lane_of = {n * TILE: lax.broadcasted_iota(jnp.int32, (n * TILE, lanes), 1) for n in (1, 2, 3)}

    for k in range(GROUPS):
        for j in range(plane):
            i = near[k] * plane + lax.rem(me + j, plane)
            arrived(W.at[i, pl.ds(2 * core, 3)], out_recv.at[1, i]).wait()
    direct = unpack([W[i, 1:4].reshape(3 * TILE, lanes) for i in range(n_az)])
    for g in range(GROUPS * GROUPS):
        F[g, pl.ds(pl.multiple_of(core * TILE, TILE), 3 * TILE)] = direct[g]
    for g, part in enumerate(unpack([W[i, 4 * core] for i in range(n_az)])):
        w, u = g // GROUPS, g % GROUPS
        F[GROUPS * GROUPS + u, w * TILE : (w + 1) * TILE] = part
    for q in range(GROUPS):
        passed(q).wait_recv()
    for g, part in enumerate(unpack([W[i, 4 - 4 * core] for i in range(n_az)])):
        F[g, pl.ds(pl.multiple_of((1 - core) * 3 * TILE, TILE), TILE)] = part

    state = [
        [[F[GROUPS * f + u, pl.ds(w, TILE, stride=GROUPS), :] for w in range(GROUPS)] for u in range(GROUPS)]
        for f in range(fields)
    ]
    step = advect_all(state)
    state = [edged(rotate(step(field))) for field in state]
    mr, mp, en = push_all(state)
    state = [edged(field) for field in (state[0], mr, mp, state[3], en)]
    step = advect_all(state)
    state = [edged(rotate(step(field))) for field in state]
    mr, mp, en = push_all(state)
    for f, field in enumerate((state[0], mr, mp, state[3], en)):
        for u in range(GROUPS):
            for w in range(GROUPS):
                G[GROUPS * f + u, pl.ds(w, TILE, stride=GROUPS), :] = field[u][w]

    order = [(k, j) for k in (2, 1, 3, 0) for j in [*range(1, plane), 0]]

    def back(index):
        k, j = order[index]
        n = order.index((k, j))
        if n == 0:
            i = 0
        elif n < 4:
            i = 1 + lax.rem(me + n - 1, 3)
        elif n < 8:
            i = 4 + lax.rem(me + n + 1, 4)
        else:
            i = 8 + lax.rem(me + n + 1, 8)
        src, dst = B.at[i], R.at[layer, block, core]
        sems = back_send.at[index], back_recv.at[(layer * blocks + block) * 2 + core]
        sent = remote(src, dst, *sems, {"az": i, "rad": half})
        return sent, None if n not in (0, 3, 7, 15) else pltpu.make_async_copy(src, dst, sems[1]), i == me

    own = [lane_rows(G[g, TILE : 3 * TILE], TILE * g) for g in range(GROUPS * GROUPS)]
    for i, part in enumerate(exchange(own, lane_of[2 * TILE])):
        B[i, : 2 * TILE] = part
    own = [
        lane_rows(G[GROUPS * GROUPS + u, (1 + t) * TILE : (2 + t) * TILE], TILE * (GROUPS * t + u))
        for t in range(2)
        for u in range(GROUPS)
    ]
    for i, part in enumerate(exchange(own, lane)):
        folded = fold(lane_rows(part, -TILE * i), lane, row)
        B[i, 2 * TILE :] = folded[: TILE // 2]
        B[i + n_az // 2, 2 * TILE :] = folded[TILE // 2 :]
    for index in range(len(order)):
        sent, within, same = back(index)
        if within is None:
            sent.start()
        else:

            @pl.when(jnp.logical_and(here, same))
            def _():
                within.start()

            @pl.when(jnp.logical_not(jnp.logical_and(here, same)))
            def _():
                sent.start()

    for l in range(depth):
        for s in range(blocks):
            for c in range(2):
                arrived(R.at[l, s, c], back_recv.at[(l * blocks + s) * 2 + c]).wait()
    for l in range(depth):
        pieces = [R[l, s, c, : 2 * TILE] for s in range(blocks) for c in range(2)]
        cells = pltpu.roll(jnp.concatenate(pieces, axis=0), lax.rem(lanes - spin, lanes), 1).T
        for f in range(GROUPS):
            for u in range(GROUPS):
                g = GROUPS * f + u
                out[f, l, pl.ds(u, TILE, stride=GROUPS), :] = cells[g * TILE : (g + 1) * TILE]
    pieces = []
    for s in range(blocks):
        both = [fold(jnp.concatenate([R[l, s, c, 2 * TILE :] for c in range(2)], axis=0), lane, row) for l in range(depth)]
        for g in range(GROUPS):
            piece = lane_rows(both[0], -width * g)
            for l in range(1, depth):
                piece = jnp.where(group == l, lane_rows(both[l], width * (l - g)), piece)
            pieces.append(piece)
    cells = jnp.concatenate(pieces, axis=0).T
    for l in range(depth):
        for u in range(GROUPS):
            g = GROUPS * l + u
            out[4, l, pl.ds(u, TILE, stride=GROUPS), :] = cells[g * TILE : (g + 1) * TILE]

    swap_shift.wait_send()
    for l in range(depth):
        for copy in swaps(l, True):
            copy.wait_send()
    for first in (True, False):
        for index in range(len(targets)):
            sent, within, _ = send(index, first)
            if within is None:
                sent.wait_send()
            else:

                @pl.when(jnp.logical_not(here))
                def _():
                    sent.wait_send()

    for k in range(GROUPS):
        passes(k).wait_send()
    for index in range(len(order)):
        sent, within, same = back(index)
        if within is None:
            sent.wait_send()
        else:

            @pl.when(jnp.logical_not(jnp.logical_and(here, same)))
            def _():
                sent.wait_send()


def turned_body(mesh, state, shifts):
    n_az, n_rad = mesh.shape["az"], mesh.shape["rad"]
    fields, depth, width, lanes = state.shape
    blocks = n_az // (depth * n_rad)
    tiles = lanes // TILE
    vmem = lambda *shape: pltpu.VMEM(shape, jnp.float32)
    dma = pltpu.SemaphoreType.DMA
    tile = (TILE, lanes)
    return pl.pallas_call(
        functools.partial(turned_kernel, n_az, n_rad),
        out_shape=pltpu.VMEM(state.shape, state.dtype),
        in_specs=[pl.BlockSpec(memory_space=pl.ANY), pl.BlockSpec(memory_space=pltpu.VMEM)],
        out_specs=pl.BlockSpec(memory_space=pltpu.VMEM),
        scratch_shapes=[
            vmem(fields, depth, width, lanes),
            vmem(depth, tiles + 2, *tile),
            vmem(depth, blocks + 2, *tile),
            vmem(depth, blocks, 2, 4, *tile),
            vmem(n_az, 5, *tile),
            pltpu.VMEM((1, lanes), jnp.int32),
            pltpu.VMEM((2 * lanes + 2 * TILE, lanes), jnp.int32),
            pltpu.VMEM((4 * TILE, lanes), jnp.int32),
            vmem(GROUPS * fields, 4 * TILE, lanes),
            vmem(GROUPS * fields, 4 * TILE, lanes),
            vmem(n_az, 2 * TILE + TILE // 2, lanes),
            vmem(depth, blocks, 2, 2 * TILE + TILE // 2, lanes),
            dma((depth,)),
            dma((2,)),
            dma((4, depth)),
            dma((2, n_az)),
            dma((2, n_az)),
            dma((GROUPS,)),
            dma((GROUPS,)),
            dma((n_az,)),
            dma((n_az,)),
        ],
        compiler_params=pltpu.CompilerParams(collective_id=0, has_side_effects=True),
    )(state, shifts.reshape(1, -1))


def turns(mesh, state):
    n_az, n_rad = mesh.shape["az"], mesh.shape["rad"]
    fields, depth, width, lanes = state.shape
    tiles = lanes // TILE
    return (
        n_rad == 2
        and fields == GROUPS + 1
        and width * GROUPS == lanes
        and n_az == GROUPS * GROUPS
        and width == GROUPS * TILE
        and lanes == n_az * TILE
        and n_az % (depth * n_rad) == 0
        and tiles == GROUPS * (n_az // (depth * n_rad))
        and depth * width <= lanes
        and SMAX <= lanes
    )


def choose(mesh, state, shifts):
    return (turned_body if turns(mesh, state) else body)(mesh, state, shifts)


def solution(mesh):
    in_specs = (P(None, None, "az", "rad"), P("rad"))
    out_specs = P(None, None, "az", "rad")
    return jax.shard_map(
        functools.partial(choose, mesh), mesh=mesh, in_specs=in_specs, out_specs=out_specs, check_vma=False
    )
```

```python
import functools

import jax
import jax.numpy as jnp
from jax import lax
from jax.experimental import pallas as pl
from jax.experimental.pallas import tpu as pltpu
from jax.sharding import PartitionSpec as P

STEPS = 2
SMIN = 4
SMAX = 96
EDGE = 4
TILE = 8

GAMMA_GAS = 1.4
COURANT_RADIAL = 0.15
COURANT_AZIMUTH = 0.15
VISCOSITY_COEF = 1.0


def up(x, axis):
    return pltpu.roll(x, x.shape[axis] - 1, axis)


def down(x, axis):
    return pltpu.roll(x, 1, axis)


def face_speeds(velocity, axis, courant):
    face = (0.5 * courant) * (velocity + up(velocity, axis))
    return jnp.maximum(face, 0.0), jnp.minimum(face, 0.0)


def advect(field, speeds, axis):
    low = field - down(field, axis)
    high = up(low, axis)
    product = low * high
    positive = product > 0
    half = jnp.where(positive, product / jnp.where(positive, low + high, 1.0), 0.0)
    flux = speeds[0] * (field + half) + speeds[1] * up(field - half, axis)
    return flux - down(flux, axis)


def push(pressure, density, speed, axis, courant):
    compress = jnp.minimum(up(speed, axis) - down(speed, axis), 0.0)
    total = pressure + VISCOSITY_COEF * density * compress * compress
    work = total * speed
    scale = -0.5 * courant
    return scale * (up(total, axis) - down(total, axis)), scale * (up(work, axis) - down(work, axis))


def shifted(window, shift_left, rows, longest):
    bits = longest.bit_length()
    x = window
    for bit in reversed(range(bits)):
        stride = 1 << bit
        left = stride - 1
        if stride >= TILE:
            keep = -(-(rows + left) // TILE) * TILE
            chosen = min(keep, x.shape[0] - stride)
            mask = (jnp.broadcast_to(shift_left, (chosen, shift_left.shape[1])) & stride) != 0
            y = jnp.where(mask, x[stride : stride + chosen], x[:chosen])
            x = y if chosen == keep else jnp.concatenate([y, x[chosen:keep]], axis=0)
        else:
            mask = (jnp.broadcast_to(shift_left, x.shape) & stride) != 0
            x = jnp.where(mask, pltpu.roll(x, x.shape[0] - stride, 0), x)
    return x[:rows]


def kernel(n_az, n_rad, x_in, shifts, out, *scratch):
    (x, load_sem, A, W0, W1, O0, O1, L0, R0, L1, R1, L2, R2, state_send, state_recv, gather_send, gather_recv,
     side_send, side_recv) = scratch
    fields, depth, width, lanes = x.shape
    behind = SMAX + EDGE
    whole = behind // width
    tail = behind % width
    tail_rows = -(-tail // TILE) * TILE
    group = whole + 1
    base = group * width
    first_row = width - tail_rows
    me = lax.axis_index("az")
    place = lax.rem(me, group)
    position = lax.axis_index("rad")

    def az(by):
        return {"az": lax.rem(me + by + n_az, n_az)}

    def member(by):
        return {"az": me - place + lax.rem(place + by + group, group)}

    def rad(by):
        return {"rad": position + by}

    barrier = pltpu.get_barrier_semaphore()
    MESH = pl.DeviceIdType.MESH
    load = pltpu.make_async_copy(x_in, x, load_sem)
    load.start()
    for by in (1, -1, -group):
        pl.semaphore_signal(barrier, inc=1, device_id=az(by), device_id_type=MESH)
    for h in range(1, group):
        pl.semaphore_signal(barrier, inc=1, device_id=member(h), device_id_type=MESH)

    has_left = position > 0
    has_right = position < n_rad - 1

    @pl.when(has_left)
    def _():
        pl.semaphore_signal(barrier, inc=1, device_id=rad(-1), device_id_type=MESH)

    @pl.when(has_right)
    def _():
        pl.semaphore_signal(barrier, inc=1, device_id=rad(1), device_id_type=MESH)

    load.wait()
    A[:, :, TILE : TILE + width, :] = x[...]
    beside_me = (position + n_rad - 1) // n_rad + (2 * n_rad - 2 - position) // n_rad
    pl.semaphore_wait(barrier, group + 2 + beside_me)

    def remote(src, dst, send, recv, where):
        return pltpu.make_async_remote_copy(
            src_ref=src, dst_ref=dst, send_sem=send, recv_sem=recv, device_id=where, device_id_type=MESH
        )

    def ring_copies(z):
        return [
            remote(x.at[:, z, width - TILE : width], A.at[:, z, 0:TILE],
                   state_send.at[0, z], state_recv.at[0, z], az(1)),
            remote(x.at[:, z, 0:TILE], A.at[:, z, TILE + width : 2 * TILE + width],
                   state_send.at[1, z], state_recv.at[1, z], az(-1)),
        ]

    def side_copies(phase, src, left_dst, right_dst, z):
        to_right = remote(src.at[:, z], left_dst.at[:, z], side_send.at[phase, 0, z],
                          side_recv.at[phase, 0, z], rad(1))
        to_left = remote(src.at[:, z], right_dst.at[:, z], side_send.at[phase, 1, z],
                         side_recv.at[phase, 1, z], rad(-1))
        return to_right, to_left

    def start_side(*args):
        to_right, to_left = side_copies(*args)

        @pl.when(has_right)
        def _():
            to_right.start()

        @pl.when(has_left)
        def _():
            to_left.start()

    def await_side(*args):
        to_right, to_left = side_copies(*args)

        @pl.when(has_left)
        def _():
            to_right.wait_recv()

        @pl.when(has_right)
        def _():
            to_left.wait_recv()

    def end_side(*args):
        to_right, to_left = side_copies(*args)

        @pl.when(has_right)
        def _():
            to_right.wait_send()

        @pl.when(has_left)
        def _():
            to_left.wait_send()

    windows = (W0, W1)
    rotated = (O0, O1)
    sides = ((x, L0, R0), (O0, L1, R1), (O1, L2, R2))

    def gather_copies(step, f, z):
        W = windows[step]
        own, back = W.at[f, z, base : base + width], W.at[f, z, 0:width]
        sems = lambda h: (gather_send.at[step, h, f, z], gather_recv.at[step, h, f, z])
        onward = remote(own, back, *sems(0), az(group))
        inside = []
        for h in range(1, group):
            dst = W.at[f, z, base - h * width : base - (h - 1) * width]
            inside.append([remote(src, dst, *sems(h), member(h)) for src in (own, back)])
        return onward, inside

    def send_own(step, f, z):
        onward, inside = gather_copies(step, f, z)
        onward.start()
        for h in range(1, group):

            @pl.when(place + h < group)
            def _():
                inside[h - 1][0].start()

    def pass_on(step, f, z):
        onward, inside = gather_copies(step, f, z)
        onward.wait_recv()
        for h in range(1, group):

            @pl.when(place + h >= group)
            def _():
                inside[h - 1][1].start()

    def edges(own, left, right):
        rows = own.shape[0]
        lane = lax.broadcasted_iota(jnp.int32, (rows, lanes), 1)
        at = jnp.full((rows, lanes), position, jnp.int32)
        left = jnp.where(at == 0, jnp.broadcast_to(own[:, 0:1], own.shape), left)
        right = jnp.where(at == n_rad - 1, jnp.broadcast_to(own[:, lanes - 1 : lanes], own.shape), right)
        return jnp.where(lane < lanes // 2, right, left)

    def wide(own, beside):
        return jnp.concatenate([own, beside], axis=1)

    def hydro(step, z, strip, beside):
        rows = slice(TILE, TILE + width)
        tall = [strip(f) for f in range(fields)]
        az_speeds = face_speeds(tall[2] / tall[0], 0, COURANT_AZIMUTH)
        broad = [wide(tall[f][rows], beside(f, tall[f][rows])) for f in range(fields)]
        rad_speeds = face_speeds(broad[1] / broad[0], 1, COURANT_RADIAL)
        for f in range(fields):
            along = advect(tall[f], az_speeds, 0)[rows]
            across = advect(broad[f], rad_speeds, 1)[:, :lanes]
            windows[step][f, z, base : base + width, :] = tall[f][rows] - along - across
            send_own(step, f, z)

    def viscous(z, state, extended):
        rho, mr, mp, mz, energy = state
        own = slice(None) if extended else slice(0, lanes)
        inverse = 1.0 / rho
        pressure = (GAMMA_GAS - 1.0) * (energy - 0.5 * (mr * mr + mp * mp + mz * mz) * inverse)
        az_m, az_e = push(pressure[:, own], rho[:, own], (mp * inverse)[:, own], 0, COURANT_AZIMUTH)
        rad_m, rad_e = push(pressure, rho, mr * inverse, 1, COURANT_RADIAL)
        return [
            rho[:, own],
            mr[:, own] + rad_m[:, own],
            mp[:, own] + az_m,
            mz[:, own],
            energy[:, own] + az_e + rad_e[:, own],
        ]

    count = width + 2 * EDGE

    for z in range(depth):
        for copy in ring_copies(z):
            copy.start()
    for z in range(depth):
        start_side(0, *sides[0], z)
    for z in range(depth):
        for copy in ring_copies(z):
            copy.wait_recv()
        await_side(0, *sides[0], z)
        hydro(0, z, lambda f: A[f, z], lambda f, own: edges(own, L0[f, z], R0[f, z]))

    for step in range(STEPS):
        for z in range(depth):
            for f in range(fields):
                pass_on(step, f, z)
        O, L, R = sides[step + 1]
        for z in range(depth):
            for f in range(fields):
                for copies in gather_copies(step, f, z)[1]:
                    copies[0].wait_recv()
                start = base - first_row - EDGE
                O[f, z] = shifted(windows[step][f, z, first_row:], start - shifts[...], count, start - SMIN)
            start_side(step + 1, O, L, R, z)
        for z in range(depth):
            await_side(step + 1, O, L, R, z)
            state = [wide(O[f, z], edges(O[f, z], L[f, z], R[f, z])) for f in range(fields)]
            if step == STEPS - 1:
                new = viscous(z, state, False)
                for f in range(fields):
                    out[f, z] = new[f][EDGE : EDGE + width]
            else:
                new = viscous(z, state, True)
                A_rows = slice(TILE - EDGE, TILE - EDGE + count)
                for f in range(fields):
                    A[f, z, A_rows, :] = new[f][:, :lanes]
                hydro(
                    step + 1,
                    z,
                    lambda f: A[f, z],
                    lambda f, own: edges(own, *[new[f][EDGE : EDGE + width, lanes:]] * 2),
                )

    for z in range(depth):
        for copy in ring_copies(z):
            copy.wait_send()
        for phase in range(STEPS + 1):
            end_side(phase, *sides[phase], z)
        for step in range(STEPS):
            for f in range(fields):
                onward, inside = gather_copies(step, f, z)
                onward.wait_send()
                for copies in inside:
                    copies[0].wait_send()


def body(mesh, state, shifts):
    n_az, n_rad = mesh.shape["az"], mesh.shape["rad"]
    fields, depth, width, lanes = state.shape
    behind = SMAX + EDGE
    group = behind // width + 1
    window = (group + 1) * width
    count = width + 2 * EDGE
    vmem = lambda rows: pltpu.VMEM((fields, depth, rows, lanes), jnp.float32)
    dma = pltpu.SemaphoreType.DMA
    return pl.pallas_call(
        functools.partial(kernel, n_az, n_rad),
        out_shape=pltpu.VMEM(state.shape, state.dtype),
        in_specs=[pl.BlockSpec(memory_space=pl.ANY), pl.BlockSpec(memory_space=pltpu.VMEM)],
        out_specs=pl.BlockSpec(memory_space=pltpu.VMEM),
        scratch_shapes=[
            vmem(width),
            dma(()),
            vmem(width + 2 * TILE),
            vmem(window),
            vmem(window),
            vmem(count),
            vmem(count),
            vmem(width),
            vmem(width),
            vmem(count),
            vmem(count),
            vmem(count),
            vmem(count),
            dma((2, depth)),
            dma((2, depth)),
            dma((STEPS, group, fields, depth)),
            dma((STEPS, group, fields, depth)),
            dma((STEPS + 1, 2, depth)),
            dma((STEPS + 1, 2, depth)),
        ],
        compiler_params=pltpu.CompilerParams(collective_id=0, has_side_effects=True),
    )(state, shifts.reshape(1, -1))


GROUPS = 4


def lane_rows(x, shift):
    return pltpu.roll(x, shift % x.shape[1], 1)


def exchange(parts, lane):
    n = len(parts)
    out = [parts[-g % n] for g in range(n)]
    for bit in range(n.bit_length() - 1):
        far = (lane & (TILE << bit)) != 0
        out = [jnp.where(far, out[(g - (1 << bit)) % n], out[g]) for g in range(n)]
    return out


def fold(x, lane, row):
    half = x.shape[1] // 2
    stay = (lane < half) == (row < TILE // 2)
    return jnp.where(stay, x, lane_rows(pltpu.roll(x, TILE // 2, 0), half))


def line(tiles):
    return jnp.concatenate(tiles, axis=0)


def tiles_of(x):
    return [x[g * TILE : (g + 1) * TILE] for g in range(GROUPS)]


def next_of(x, axis):
    first = x[:TILE]
    return jnp.concatenate([x[TILE:], pltpu.roll(first, first.shape[axis] - 1, axis)], axis=0)


def last_of(x, axis):
    last = x[-TILE:]
    return jnp.concatenate([pltpu.roll(last, 1, axis), x[:-TILE]], axis=0)


def along(field, w):
    return line([field[u][w] for u in range(GROUPS)])


def across(field, u):
    return line(field[u])


def line_speeds(velocity, axis, courant):
    face = (0.5 * courant) * (velocity + next_of(velocity, axis))
    return jnp.maximum(face, 0.0), jnp.minimum(face, 0.0)


def line_advect(field, speeds, axis):
    low = field - last_of(field, axis)
    high = next_of(low, axis)
    product = low * high
    half = jnp.where(product > 0, product / (low + high), 0.0)
    flux = speeds[0] * (field + half) + speeds[1] * next_of(field - half, axis)
    return flux - last_of(flux, axis)


def line_push(pressure, density, speed, axis):
    compress = jnp.minimum(next_of(speed, axis) - last_of(speed, axis), 0.0)
    total = pressure + density * compress * compress
    work = total * speed
    return next_of(total, axis) - last_of(total, axis), next_of(work, axis) - last_of(work, axis)


def advect_all(state):
    rho, mr, mp = state[:3]
    az_speeds, rad_speeds = [], []
    inverse = [tiles_of(1.0 / across(rho, u)) for u in range(GROUPS)]
    for g in range(GROUPS):
        az_speeds.append(line_speeds(along(mp, g) * along(inverse, g), 1, COURANT_AZIMUTH))
        rad_speeds.append(line_speeds(across(mr, g) * across(inverse, g), 0, COURANT_RADIAL))

    def step(field):
        turned = [along(field, w) for w in range(GROUPS)]
        turned = [tiles_of(turned[w] - line_advect(turned[w], az_speeds[w], 1)) for w in range(GROUPS)]
        out = []
        for u in range(GROUPS):
            rest = line([turned[w][u] for w in range(GROUPS)])
            out.append(tiles_of(rest - line_advect(across(field, u), rad_speeds[u], 0)))
        return out

    return step


def push_all(state):
    scale = -0.5 * COURANT_AZIMUTH
    assert COURANT_RADIAL == COURANT_AZIMUTH
    rho, mr, mp, mz, energy = state
    inverse, pressure, density, new_mr, rest = [], [], [], [], []
    for u in range(GROUPS):
        r, a, b, c, e = (across(f, u) for f in state)
        inv = 1.0 / r
        p = (scale * (GAMMA_GAS - 1.0)) * (e - 0.5 * (a * a + b * b + c * c) * inv)
        d = (scale * VISCOSITY_COEF) * r
        rad_m, rad_e = line_push(p, d, a * inv, 0)
        inverse.append(tiles_of(inv))
        pressure.append(tiles_of(p))
        density.append(tiles_of(d))
        new_mr.append(tiles_of(a + rad_m))
        rest.append(tiles_of(e + rad_e))
    new_mp = [[None] * GROUPS for _ in range(GROUPS)]
    new_energy = [[None] * GROUPS for _ in range(GROUPS)]
    for w in range(GROUPS):
        b = along(mp, w)
        az_m, az_e = line_push(along(pressure, w), along(density, w), b * along(inverse, w), 1)
        for u, (m, e) in enumerate(zip(tiles_of(b + az_m), tiles_of(along(rest, w) + az_e))):
            new_mp[u][w], new_energy[u][w] = m, e
    return new_mr, new_mp, new_energy


def turned_kernel(n_az, n_rad, x_in, shifts, out, *scratch):
    (x, T4, EP, M, W, other, SC, AM, F, G, B, R, load_sem, shift_sem, swap_sem, out_send, out_recv, pass_send, pass_recv,
     back_send, back_recv) = scratch
    fields, depth, width, lanes = x.shape
    blocks = n_az // (depth * n_rad)
    tiles = lanes // TILE
    rows = 4 * TILE
    MESH = pl.DeviceIdType.MESH
    me = lax.axis_index("az")
    core = lax.axis_index("rad")
    half = lax.rem(me // 2, 2)
    layer = lax.rem(me, 2)
    block = me // 4
    place = (half * blocks + block) * 2 + core
    partner = {"rad": 1 - core}
    here = half == core

    def remote(src, dst, send, recv, where):
        return pltpu.make_async_remote_copy(
            src_ref=src, dst_ref=dst, send_sem=send, recv_sem=recv, device_id=where, device_id_type=MESH
        )

    loads = [pltpu.make_async_copy(x_in.at[:, l], x.at[:, l], load_sem.at[l]) for l in range(depth)]
    for load in loads:
        load.start()
    barrier = pltpu.get_barrier_semaphore()
    for k in range(1, n_az):
        pl.semaphore_signal(
            barrier, inc=1, device_id={"az": lax.rem(me + k, n_az), "rad": half}, device_id_type=MESH
        )
    pl.semaphore_signal(barrier, inc=1, device_id=partner, device_id_type=MESH)

    lane = lax.broadcasted_iota(jnp.int32, (TILE, lanes), 1)
    row = lax.broadcasted_iota(jnp.int32, (TILE, lanes), 0)
    group = lane // width

    spin = me * TILE

    def rows_of(f, l):
        return [x[f, l, pl.ds(u, width // GROUPS, stride=GROUPS), :] for u in range(GROUPS)]

    for l in range(depth):
        loads[l].wait()
        cells = jnp.concatenate([part for f in range(GROUPS) for part in rows_of(f, l)], axis=0)
        T4[l, 1 : tiles + 1] = pltpu.roll(cells.T, spin, 1).reshape(tiles, TILE, lanes)
    energy = [part for l in range(depth) for part in rows_of(4, l)]
    turned = jnp.concatenate(energy * (lanes // (depth * width)), axis=0).T.reshape(tiles, TILE, lanes)
    for l in range(depth):
        for m in range(tiles // GROUPS):
            packed = turned[GROUPS * m] if l == 0 else lane_rows(turned[GROUPS * m], -width * l)
            for g in range(1, GROUPS):
                packed = jnp.where(group == g, lane_rows(turned[GROUPS * m + g], width * (g - l)), packed)
            EP[l, 1 + m] = packed

    @pl.when(core == 0)
    def _():
        for l in range(depth):
            T4[l, 0] = jnp.broadcast_to(T4[l, 1, 0:1], (TILE, lanes))
            EP[l, 0] = jnp.broadcast_to(lane_rows(EP[l, 1], -width)[0:1], (TILE, lanes))

    @pl.when(core == 1)
    def _():
        for l in range(depth):
            T4[l, tiles + 1] = jnp.broadcast_to(T4[l, tiles, TILE - 1 : TILE], (TILE, lanes))
            EP[l, blocks + 1] = jnp.broadcast_to(lane_rows(EP[l, blocks], width)[TILE - 1 : TILE], (TILE, lanes))

    def stage(l, s, c):
        own = EP[l, 1 + s]
        if c == 0:
            M[l, s, c, 0] = pltpu.roll(jnp.where(group == GROUPS - 1, EP[l, s], own), lax.rem(spin + width, lanes), 1)
            M[l, s, c, 1:3] = T4[l, GROUPS * s : GROUPS * s + 2]
        else:
            M[l, s, c, 1:3] = T4[l, GROUPS * s + 4 : GROUPS * s + 6]
            M[l, s, c, 3] = pltpu.roll(jnp.where(group == 0, EP[l, s + 2], own), lax.rem(spin + lanes - width, lanes), 1)

    late = ((0, 0), (blocks - 1, 1))
    for l in range(depth):
        for s in range(blocks):
            for c in range(2):
                M[l, s, c, 3 - 3 * c] = T4[l, GROUPS * s + 2 + c]
                if (s, c) not in late:
                    stage(l, s, c)

    senders = jnp.where(here, 2 * (n_az // n_rad - 1) + 1, 2 * (n_az // n_rad) + 1)
    pl.semaphore_wait(barrier, senders)

    swap_shift = remote(shifts, other, shift_sem.at[0], shift_sem.at[1], partner)
    swap_shift.start()

    def swaps(l, up):
        src = (tiles, blocks) if up else (1, 1)
        dst = (0, 0) if up else (tiles + 1, blocks + 1)
        return [
            remote(T4.at[l, src[0]], T4.at[l, dst[0]], swap_sem.at[0, l], swap_sem.at[1, l], partner),
            remote(EP.at[l, src[1]], EP.at[l, dst[1]], swap_sem.at[2, l], swap_sem.at[3, l], partner),
        ]

    @pl.when(core == 0)
    def _():
        for l in range(depth):
            for copy in swaps(l, True):
                copy.start()

    @pl.when(core == 1)
    def _():
        for l in range(depth):
            for copy in swaps(l, False):
                copy.start()

    whole = ()
    split = (2, 1, 3, 0)
    targets = [(ks, kl, kc) for ks in (*whole, *split) for kl in (1, 0) for kc in (0, 1)]

    def send(index, first):
        ks, kl, kc = targets[index]
        s = lax.rem(block + ks, blocks)
        l = lax.rem(layer + kl, depth)
        c = lax.rem(core + kc, 2)
        if first:
            src, dst = M.at[l, s, c, 3 - 3 * c], W.at[me, 3 - 2 * c]
            sems = out_send.at[0, index], out_recv.at[0, me]
        else:
            if ks in split:
                src, dst = M.at[l, s, c, pl.ds(c, 3)], W.at[me, pl.ds(2 * c, 3)]
            else:
                src, dst = M.at[l, s, c], W.at[me, pl.ds(c, 4)]
            sems = out_send.at[1, index], out_recv.at[1, me]
        sent = remote(src, dst, *sems, {"az": s * 4 + core * 2 + l, "rad": c})
        is_late = s == c * (blocks - 1)
        return sent, None if ks or kl or kc else pltpu.make_async_copy(src, dst, sems[1]), is_late

    messages = [(index, True) for index, t in enumerate(targets) if t[0] in split]
    messages += [(index, False) for index in range(len(targets))]

    def start(first, when=None):
        for index, part in messages:
            if part != first:
                continue
            sent, within, is_late = send(index, first)
            if within is None and when is None:
                sent.start()
                continue
            now = True if when is None else when(is_late)
            for copy, also in ((sent, None),) if within is None else ((within, here), (sent, jnp.logical_not(here))):

                @pl.when(now if also is None else jnp.logical_and(now, also))
                def _():
                    copy.start()

    start(True)
    start(False, jnp.logical_not)
    for l in range(depth):
        for copy in swaps(l, True):
            copy.wait_recv()
    for l in range(depth):
        for s, c in late:
            stage(l, s, c)
    start(False, lambda is_late: is_late)

    swap_shift.wait_recv()
    lower = jnp.full((1, lanes), core, jnp.int32) == 0
    mine, theirs = shifts[...], other[...]
    for c in range(2):
        part = jnp.where(lower, mine if c == 0 else theirs, theirs if c == 0 else mine)
        table = jnp.broadcast_to(part.astype(jnp.float32), (lanes, lanes)).T.astype(jnp.int32)
        SC[TILE + c * lanes : TILE + (c + 1) * lanes] = table
    SC[0:TILE] = jnp.zeros((TILE, lanes), jnp.int32)
    SC[TILE + 2 * lanes :] = jnp.zeros((TILE, lanes), jnp.int32)
    AM[...] = SC[pl.ds(pl.multiple_of(place * 2 * TILE, TILE), rows)]
    amounts = [AM[pl.ds(w, TILE, stride=GROUPS), :] for w in range(GROUPS)]
    coarse = [amount // GROUPS for amount in amounts]
    odd = [(amount & 1) != 0 for amount in amounts]
    two = [(amount & 2) != 0 for amount in amounts]
    source = [
        [(lane - coarse[w] - jnp.where(u < (amounts[w] & (GROUPS - 1)), 1, 0)) & (lanes - 1) for w in range(GROUPS)]
        for u in range(GROUPS)
    ]

    plane = n_az // GROUPS

    def sender(ks):
        return lax.rem(block + blocks - ks, blocks)

    def passes(ks):
        ahead = pl.ds(sender(ks) * plane, plane)
        return remote(
            W.at[ahead, 3 - 2 * core], W.at[ahead, 4 * core], pass_send.at[ks], pass_recv.at[sender(ks)], partner
        )

    def passed(q):
        return remote(
            W.at[pl.ds(q * plane, plane), 3 - 2 * core], W.at[pl.ds(q * plane, plane), 4 - 4 * core],
            pass_send.at[q], pass_recv.at[q], partner
        )

    def arrived(dst, recv):
        return pltpu.make_async_copy(dst, dst, recv)

    def await_senders(ks, first):
        for j in range(plane):
            i = sender(ks) * plane + lax.rem(me + j, plane)
            if first:
                arrived(W.at[i, 3 - 2 * core], out_recv.at[0, i]).wait()
            elif ks in split:
                arrived(W.at[i, pl.ds(2 * core, 3)], out_recv.at[1, i]).wait()
            else:
                arrived(W.at[i, pl.ds(core, 4)], out_recv.at[1, i]).wait()

    for ks in split:
        await_senders(ks, True)
        passes(ks).start()
    for ks in whole:
        await_senders(ks, False)
        passes(ks).start()

    def rotate(field):
        out = [[None] * GROUPS for _ in range(GROUPS)]
        for w in range(GROUPS):
            near_by = [jnp.where(odd[w], field[u - 1][w], field[u][w]) for u in range(GROUPS)]
            for u in range(GROUPS):
                chosen = jnp.where(two[w], near_by[u - 2], near_by[u])
                out[u][w] = jnp.take_along_axis(chosen, source[u][w], axis=1)
        return out

    at = jnp.full((TILE, lanes), place, jnp.int32)
    lowest = jnp.logical_and(at == 0, row < 2)
    highest = jnp.logical_and(at == 2 * blocks * n_rad - 1, row >= TILE - 2)

    def edged(field):
        out = []
        for u in range(GROUPS):
            low = jnp.broadcast_to(field[u][0][2:3], (TILE, lanes))
            high = jnp.broadcast_to(field[u][3][TILE - 3 : TILE - 2], (TILE, lanes))
            out.append(
                [jnp.where(highest, high, field[u][w]) for w in range(2)]
                + [jnp.where(lowest, low, field[u][w]) for w in range(2, GROUPS)]
            )
        return out

    def unpack(parts):
        return [lane_rows(part, -TILE * g) for g, part in enumerate(exchange(parts, lane_of[parts[0].shape[0]]))]

    lane_of = {n * TILE: lax.broadcasted_iota(jnp.int32, (n * TILE, lanes), 1) for n in (1, 2, 3)}

    def settle(slot, at_row):
        for g, part in enumerate(unpack([W[i, pl.ds(slot, 2)].reshape(2 * TILE, lanes) for i in range(n_az)])):
            F[g, pl.ds(pl.multiple_of(at_row, TILE), 2 * TILE)] = part

    for q in range(GROUPS):
        passed(q).wait_recv()
    settle(3 - 3 * core, 2 * TILE * (1 - core))
    for ks in split:
        await_senders(ks, False)
    settle(1 + core, 2 * TILE * core)
    for g, part in enumerate(unpack([W[i, 4 * core] for i in range(n_az)])):
        w, u = g // GROUPS, g % GROUPS
        F[GROUPS * GROUPS + u, w * TILE : (w + 1) * TILE] = part

    state = [
        [[F[GROUPS * f + u, pl.ds(w, TILE, stride=GROUPS), :] for w in range(GROUPS)] for u in range(GROUPS)]
        for f in range(fields)
    ]
    step = advect_all(state)
    state = [edged(rotate(step(field))) for field in state]
    mr, mp, en = push_all(state)
    state = [edged(field) for field in (state[0], mr, mp, state[3], en)]
    step = advect_all(state)
    state = [edged(rotate(step(field))) for field in state]
    mr, mp, en = push_all(state)
    for f, field in enumerate((state[0], mr, mp, state[3], en)):
        for u in range(GROUPS):
            for w in range(GROUPS):
                G[GROUPS * f + u, pl.ds(w, TILE, stride=GROUPS), :] = field[u][w]

    order = [(k, j) for k in (2, 1, 3, 0) for j in [*range(1, plane), 0]]

    def back(index):
        k, j = order[index]
        n = order.index((k, j))
        if n == 0:
            i = 0
        elif n < 4:
            i = 1 + lax.rem(me + n - 1, 3)
        elif n < 8:
            i = 4 + lax.rem(me + n + 1, 4)
        else:
            i = 8 + lax.rem(me + n + 1, 8)
        src, dst = B.at[i], R.at[layer, block, core]
        sems = back_send.at[index], back_recv.at[(layer * blocks + block) * 2 + core]
        sent = remote(src, dst, *sems, {"az": i, "rad": half})
        return sent, None if n not in (0, 3, 7, 15) else pltpu.make_async_copy(src, dst, sems[1]), i == me

    own = [lane_rows(G[g, TILE : 3 * TILE], TILE * g) for g in range(GROUPS * GROUPS)]
    for i, part in enumerate(exchange(own, lane_of[2 * TILE])):
        B[i, : 2 * TILE] = part
    own = [
        lane_rows(G[GROUPS * GROUPS + u, (1 + t) * TILE : (2 + t) * TILE], TILE * (GROUPS * t + u))
        for t in range(2)
        for u in range(GROUPS)
    ]
    for i, part in enumerate(exchange(own, lane)):
        folded = fold(lane_rows(part, -TILE * i), lane, row)
        B[i, 2 * TILE :] = folded[: TILE // 2]
        B[i + n_az // 2, 2 * TILE :] = folded[TILE // 2 :]
    for index in range(len(order)):
        sent, within, same = back(index)
        if within is None:
            sent.start()
        else:

            @pl.when(jnp.logical_and(here, same))
            def _():
                within.start()

            @pl.when(jnp.logical_not(jnp.logical_and(here, same)))
            def _():
                sent.start()

    for l in range(depth):
        for s in range(blocks):
            for c in range(2):
                arrived(R.at[l, s, c], back_recv.at[(l * blocks + s) * 2 + c]).wait()
        pieces = [R[l, s, c, : 2 * TILE] for s in range(blocks) for c in range(2)]
        cells = pltpu.roll(jnp.concatenate(pieces, axis=0), lax.rem(lanes - spin, lanes), 1).T
        for f in range(GROUPS):
            for u in range(GROUPS):
                g = GROUPS * f + u
                out[f, l, pl.ds(u, TILE, stride=GROUPS), :] = cells[g * TILE : (g + 1) * TILE]
    pieces = []
    for s in range(blocks):
        both = [fold(jnp.concatenate([R[l, s, c, 2 * TILE :] for c in range(2)], axis=0), lane, row) for l in range(depth)]
        for g in range(GROUPS):
            piece = lane_rows(both[0], -width * g)
            for l in range(1, depth):
                piece = jnp.where(group == l, lane_rows(both[l], width * (l - g)), piece)
            pieces.append(piece)
    cells = jnp.concatenate(pieces, axis=0).T
    for l in range(depth):
        for u in range(GROUPS):
            g = GROUPS * l + u
            out[4, l, pl.ds(u, TILE, stride=GROUPS), :] = cells[g * TILE : (g + 1) * TILE]

    swap_shift.wait_send()
    for l in range(depth):
        for copy in swaps(l, True):
            copy.wait_send()
    for index, first in messages:
        sent, within, _ = send(index, first)
        if within is None:
            sent.wait_send()
        else:

            @pl.when(jnp.logical_not(here))
            def _():
                sent.wait_send()

    for k in range(GROUPS):
        passes(k).wait_send()
    for index in range(len(order)):
        sent, within, same = back(index)
        if within is None:
            sent.wait_send()
        else:

            @pl.when(jnp.logical_not(jnp.logical_and(here, same)))
            def _():
                sent.wait_send()


def turned_body(mesh, state, shifts):
    n_az, n_rad = mesh.shape["az"], mesh.shape["rad"]
    fields, depth, width, lanes = state.shape
    blocks = n_az // (depth * n_rad)
    tiles = lanes // TILE
    vmem = lambda *shape: pltpu.VMEM(shape, jnp.float32)
    dma = pltpu.SemaphoreType.DMA
    tile = (TILE, lanes)
    return pl.pallas_call(
        functools.partial(turned_kernel, n_az, n_rad),
        out_shape=pltpu.VMEM(state.shape, state.dtype),
        in_specs=[pl.BlockSpec(memory_space=pl.ANY), pl.BlockSpec(memory_space=pltpu.VMEM)],
        out_specs=pl.BlockSpec(memory_space=pltpu.VMEM),
        scratch_shapes=[
            vmem(fields, depth, width, lanes),
            vmem(depth, tiles + 2, *tile),
            vmem(depth, blocks + 2, *tile),
            vmem(depth, blocks, 2, 4, *tile),
            vmem(n_az, 5, *tile),
            pltpu.VMEM((1, lanes), jnp.int32),
            pltpu.VMEM((2 * lanes + 2 * TILE, lanes), jnp.int32),
            pltpu.VMEM((4 * TILE, lanes), jnp.int32),
            vmem(GROUPS * fields, 4 * TILE, lanes),
            vmem(GROUPS * fields, 4 * TILE, lanes),
            vmem(n_az, 2 * TILE + TILE // 2, lanes),
            vmem(depth, blocks, 2, 2 * TILE + TILE // 2, lanes),
            dma((depth,)),
            dma((2,)),
            dma((4, depth)),
            dma((2, n_az)),
            dma((2, n_az)),
            dma((GROUPS,)),
            dma((GROUPS,)),
            dma((n_az,)),
            dma((n_az,)),
        ],
        compiler_params=pltpu.CompilerParams(collective_id=0, has_side_effects=True),
    )(state, shifts.reshape(1, -1))


def turns(mesh, state):
    n_az, n_rad = mesh.shape["az"], mesh.shape["rad"]
    fields, depth, width, lanes = state.shape
    tiles = lanes // TILE
    return (
        n_rad == 2
        and fields == GROUPS + 1
        and width * GROUPS == lanes
        and n_az == GROUPS * GROUPS
        and width == GROUPS * TILE
        and lanes == n_az * TILE
        and n_az % (depth * n_rad) == 0
        and tiles == GROUPS * (n_az // (depth * n_rad))
        and depth * width <= lanes
        and SMAX <= lanes
    )


def choose(mesh, state, shifts):
    return (turned_body if turns(mesh, state) else body)(mesh, state, shifts)


def solution(mesh):
    in_specs = (P(None, None, "az", "rad"), P("rad"))
    out_specs = P(None, None, "az", "rad")
    return jax.shard_map(
        functools.partial(choose, mesh), mesh=mesh, in_specs=in_specs, out_specs=out_specs, check_vma=False
    )
```

```python
import functools

import jax
import jax.numpy as jnp
from jax import lax
from jax.experimental import pallas as pl
from jax.experimental.pallas import tpu as pltpu
from jax.sharding import PartitionSpec as P

STEPS = 2
SMIN = 4
SMAX = 96
EDGE = 4
TILE = 8

GAMMA_GAS = 1.4
COURANT_RADIAL = 0.15
COURANT_AZIMUTH = 0.15
VISCOSITY_COEF = 1.0


def up(x, axis):
    return pltpu.roll(x, x.shape[axis] - 1, axis)


def down(x, axis):
    return pltpu.roll(x, 1, axis)


def face_speeds(velocity, axis, courant):
    face = (0.5 * courant) * (velocity + up(velocity, axis))
    return jnp.maximum(face, 0.0), jnp.minimum(face, 0.0)


def advect(field, speeds, axis):
    low = field - down(field, axis)
    high = up(low, axis)
    product = low * high
    positive = product > 0
    half = jnp.where(positive, product / jnp.where(positive, low + high, 1.0), 0.0)
    flux = speeds[0] * (field + half) + speeds[1] * up(field - half, axis)
    return flux - down(flux, axis)


def push(pressure, density, speed, axis, courant):
    compress = jnp.minimum(up(speed, axis) - down(speed, axis), 0.0)
    total = pressure + VISCOSITY_COEF * density * compress * compress
    work = total * speed
    scale = -0.5 * courant
    return scale * (up(total, axis) - down(total, axis)), scale * (up(work, axis) - down(work, axis))


def shifted(window, shift_left, rows, longest):
    bits = longest.bit_length()
    x = window
    for bit in reversed(range(bits)):
        stride = 1 << bit
        left = stride - 1
        if stride >= TILE:
            keep = -(-(rows + left) // TILE) * TILE
            chosen = min(keep, x.shape[0] - stride)
            mask = (jnp.broadcast_to(shift_left, (chosen, shift_left.shape[1])) & stride) != 0
            y = jnp.where(mask, x[stride : stride + chosen], x[:chosen])
            x = y if chosen == keep else jnp.concatenate([y, x[chosen:keep]], axis=0)
        else:
            mask = (jnp.broadcast_to(shift_left, x.shape) & stride) != 0
            x = jnp.where(mask, pltpu.roll(x, x.shape[0] - stride, 0), x)
    return x[:rows]


def kernel(n_az, n_rad, x_in, shifts, out, *scratch):
    (x, load_sem, A, W0, W1, O0, O1, L0, R0, L1, R1, L2, R2, state_send, state_recv, gather_send, gather_recv,
     side_send, side_recv) = scratch
    fields, depth, width, lanes = x.shape
    behind = SMAX + EDGE
    whole = behind // width
    tail = behind % width
    tail_rows = -(-tail // TILE) * TILE
    group = whole + 1
    base = group * width
    first_row = width - tail_rows
    me = lax.axis_index("az")
    place = lax.rem(me, group)
    position = lax.axis_index("rad")

    def az(by):
        return {"az": lax.rem(me + by + n_az, n_az)}

    def member(by):
        return {"az": me - place + lax.rem(place + by + group, group)}

    def rad(by):
        return {"rad": position + by}

    barrier = pltpu.get_barrier_semaphore()
    MESH = pl.DeviceIdType.MESH
    load = pltpu.make_async_copy(x_in, x, load_sem)
    load.start()
    for by in (1, -1, -group):
        pl.semaphore_signal(barrier, inc=1, device_id=az(by), device_id_type=MESH)
    for h in range(1, group):
        pl.semaphore_signal(barrier, inc=1, device_id=member(h), device_id_type=MESH)

    has_left = position > 0
    has_right = position < n_rad - 1

    @pl.when(has_left)
    def _():
        pl.semaphore_signal(barrier, inc=1, device_id=rad(-1), device_id_type=MESH)

    @pl.when(has_right)
    def _():
        pl.semaphore_signal(barrier, inc=1, device_id=rad(1), device_id_type=MESH)

    load.wait()
    A[:, :, TILE : TILE + width, :] = x[...]
    beside_me = (position + n_rad - 1) // n_rad + (2 * n_rad - 2 - position) // n_rad
    pl.semaphore_wait(barrier, group + 2 + beside_me)

    def remote(src, dst, send, recv, where):
        return pltpu.make_async_remote_copy(
            src_ref=src, dst_ref=dst, send_sem=send, recv_sem=recv, device_id=where, device_id_type=MESH
        )

    def ring_copies(z):
        return [
            remote(x.at[:, z, width - TILE : width], A.at[:, z, 0:TILE],
                   state_send.at[0, z], state_recv.at[0, z], az(1)),
            remote(x.at[:, z, 0:TILE], A.at[:, z, TILE + width : 2 * TILE + width],
                   state_send.at[1, z], state_recv.at[1, z], az(-1)),
        ]

    def side_copies(phase, src, left_dst, right_dst, z):
        to_right = remote(src.at[:, z], left_dst.at[:, z], side_send.at[phase, 0, z],
                          side_recv.at[phase, 0, z], rad(1))
        to_left = remote(src.at[:, z], right_dst.at[:, z], side_send.at[phase, 1, z],
                         side_recv.at[phase, 1, z], rad(-1))
        return to_right, to_left

    def start_side(*args):
        to_right, to_left = side_copies(*args)

        @pl.when(has_right)
        def _():
            to_right.start()

        @pl.when(has_left)
        def _():
            to_left.start()

    def await_side(*args):
        to_right, to_left = side_copies(*args)

        @pl.when(has_left)
        def _():
            to_right.wait_recv()

        @pl.when(has_right)
        def _():
            to_left.wait_recv()

    def end_side(*args):
        to_right, to_left = side_copies(*args)

        @pl.when(has_right)
        def _():
            to_right.wait_send()

        @pl.when(has_left)
        def _():
            to_left.wait_send()

    windows = (W0, W1)
    rotated = (O0, O1)
    sides = ((x, L0, R0), (O0, L1, R1), (O1, L2, R2))

    def gather_copies(step, f, z):
        W = windows[step]
        own, back = W.at[f, z, base : base + width], W.at[f, z, 0:width]
        sems = lambda h: (gather_send.at[step, h, f, z], gather_recv.at[step, h, f, z])
        onward = remote(own, back, *sems(0), az(group))
        inside = []
        for h in range(1, group):
            dst = W.at[f, z, base - h * width : base - (h - 1) * width]
            inside.append([remote(src, dst, *sems(h), member(h)) for src in (own, back)])
        return onward, inside

    def send_own(step, f, z):
        onward, inside = gather_copies(step, f, z)
        onward.start()
        for h in range(1, group):

            @pl.when(place + h < group)
            def _():
                inside[h - 1][0].start()

    def pass_on(step, f, z):
        onward, inside = gather_copies(step, f, z)
        onward.wait_recv()
        for h in range(1, group):

            @pl.when(place + h >= group)
            def _():
                inside[h - 1][1].start()

    def edges(own, left, right):
        rows = own.shape[0]
        lane = lax.broadcasted_iota(jnp.int32, (rows, lanes), 1)
        at = jnp.full((rows, lanes), position, jnp.int32)
        left = jnp.where(at == 0, jnp.broadcast_to(own[:, 0:1], own.shape), left)
        right = jnp.where(at == n_rad - 1, jnp.broadcast_to(own[:, lanes - 1 : lanes], own.shape), right)
        return jnp.where(lane < lanes // 2, right, left)

    def wide(own, beside):
        return jnp.concatenate([own, beside], axis=1)

    def hydro(step, z, strip, beside):
        rows = slice(TILE, TILE + width)
        tall = [strip(f) for f in range(fields)]
        az_speeds = face_speeds(tall[2] / tall[0], 0, COURANT_AZIMUTH)
        broad = [wide(tall[f][rows], beside(f, tall[f][rows])) for f in range(fields)]
        rad_speeds = face_speeds(broad[1] / broad[0], 1, COURANT_RADIAL)
        for f in range(fields):
            along = advect(tall[f], az_speeds, 0)[rows]
            across = advect(broad[f], rad_speeds, 1)[:, :lanes]
            windows[step][f, z, base : base + width, :] = tall[f][rows] - along - across
            send_own(step, f, z)

    def viscous(z, state, extended):
        rho, mr, mp, mz, energy = state
        own = slice(None) if extended else slice(0, lanes)
        inverse = 1.0 / rho
        pressure = (GAMMA_GAS - 1.0) * (energy - 0.5 * (mr * mr + mp * mp + mz * mz) * inverse)
        az_m, az_e = push(pressure[:, own], rho[:, own], (mp * inverse)[:, own], 0, COURANT_AZIMUTH)
        rad_m, rad_e = push(pressure, rho, mr * inverse, 1, COURANT_RADIAL)
        return [
            rho[:, own],
            mr[:, own] + rad_m[:, own],
            mp[:, own] + az_m,
            mz[:, own],
            energy[:, own] + az_e + rad_e[:, own],
        ]

    count = width + 2 * EDGE

    for z in range(depth):
        for copy in ring_copies(z):
            copy.start()
    for z in range(depth):
        start_side(0, *sides[0], z)
    for z in range(depth):
        for copy in ring_copies(z):
            copy.wait_recv()
        await_side(0, *sides[0], z)
        hydro(0, z, lambda f: A[f, z], lambda f, own: edges(own, L0[f, z], R0[f, z]))

    for step in range(STEPS):
        for z in range(depth):
            for f in range(fields):
                pass_on(step, f, z)
        O, L, R = sides[step + 1]
        for z in range(depth):
            for f in range(fields):
                for copies in gather_copies(step, f, z)[1]:
                    copies[0].wait_recv()
                start = base - first_row - EDGE
                O[f, z] = shifted(windows[step][f, z, first_row:], start - shifts[...], count, start - SMIN)
            start_side(step + 1, O, L, R, z)
        for z in range(depth):
            await_side(step + 1, O, L, R, z)
            state = [wide(O[f, z], edges(O[f, z], L[f, z], R[f, z])) for f in range(fields)]
            if step == STEPS - 1:
                new = viscous(z, state, False)
                for f in range(fields):
                    out[f, z] = new[f][EDGE : EDGE + width]
            else:
                new = viscous(z, state, True)
                A_rows = slice(TILE - EDGE, TILE - EDGE + count)
                for f in range(fields):
                    A[f, z, A_rows, :] = new[f][:, :lanes]
                hydro(
                    step + 1,
                    z,
                    lambda f: A[f, z],
                    lambda f, own: edges(own, *[new[f][EDGE : EDGE + width, lanes:]] * 2),
                )

    for z in range(depth):
        for copy in ring_copies(z):
            copy.wait_send()
        for phase in range(STEPS + 1):
            end_side(phase, *sides[phase], z)
        for step in range(STEPS):
            for f in range(fields):
                onward, inside = gather_copies(step, f, z)
                onward.wait_send()
                for copies in inside:
                    copies[0].wait_send()


def body(mesh, state, shifts):
    n_az, n_rad = mesh.shape["az"], mesh.shape["rad"]
    fields, depth, width, lanes = state.shape
    behind = SMAX + EDGE
    group = behind // width + 1
    window = (group + 1) * width
    count = width + 2 * EDGE
    vmem = lambda rows: pltpu.VMEM((fields, depth, rows, lanes), jnp.float32)
    dma = pltpu.SemaphoreType.DMA
    return pl.pallas_call(
        functools.partial(kernel, n_az, n_rad),
        out_shape=pltpu.VMEM(state.shape, state.dtype),
        in_specs=[pl.BlockSpec(memory_space=pl.ANY), pl.BlockSpec(memory_space=pltpu.VMEM)],
        out_specs=pl.BlockSpec(memory_space=pltpu.VMEM),
        scratch_shapes=[
            vmem(width),
            dma(()),
            vmem(width + 2 * TILE),
            vmem(window),
            vmem(window),
            vmem(count),
            vmem(count),
            vmem(width),
            vmem(width),
            vmem(count),
            vmem(count),
            vmem(count),
            vmem(count),
            dma((2, depth)),
            dma((2, depth)),
            dma((STEPS, group, fields, depth)),
            dma((STEPS, group, fields, depth)),
            dma((STEPS + 1, 2, depth)),
            dma((STEPS + 1, 2, depth)),
        ],
        compiler_params=pltpu.CompilerParams(collective_id=0, has_side_effects=True),
    )(state, shifts.reshape(1, -1))


GROUPS = 4


def lane_rows(x, shift):
    return pltpu.roll(x, shift % x.shape[1], 1)


def exchange(parts, lane):
    n = len(parts)
    out = [parts[-g % n] for g in range(n)]
    for bit in range(n.bit_length() - 1):
        far = (lane & (TILE << bit)) != 0
        out = [jnp.where(far, out[(g - (1 << bit)) % n], out[g]) for g in range(n)]
    return out


def fold(x, lane, row):
    half = x.shape[1] // 2
    stay = (lane < half) == (row < TILE // 2)
    return jnp.where(stay, x, lane_rows(pltpu.roll(x, TILE // 2, 0), half))


def line(tiles):
    return jnp.concatenate(tiles, axis=0)


def tiles_of(x):
    return [x[g * TILE : (g + 1) * TILE] for g in range(GROUPS)]


def next_of(x, axis):
    first = x[:TILE]
    return jnp.concatenate([x[TILE:], pltpu.roll(first, first.shape[axis] - 1, axis)], axis=0)


def last_of(x, axis):
    last = x[-TILE:]
    return jnp.concatenate([pltpu.roll(last, 1, axis), x[:-TILE]], axis=0)


def along(field, w):
    return line([field[u][w] for u in range(GROUPS)])


def across(field, u):
    return line(field[u])


def line_speeds(velocity, axis, courant):
    face = (0.5 * courant) * (velocity + next_of(velocity, axis))
    return jnp.maximum(face, 0.0), jnp.minimum(face, 0.0)


def line_advect(field, speeds, axis):
    low = field - last_of(field, axis)
    high = next_of(low, axis)
    product = low * high
    half = jnp.where(product > 0, product / (low + high), 0.0)
    flux = speeds[0] * (field + half) + speeds[1] * next_of(field - half, axis)
    return flux - last_of(flux, axis)


def line_push(pressure, density, speed, axis):
    compress = jnp.minimum(next_of(speed, axis) - last_of(speed, axis), 0.0)
    total = pressure + density * compress * compress
    work = total * speed
    return next_of(total, axis) - last_of(total, axis), next_of(work, axis) - last_of(work, axis)


def advect_all(state):
    rho, mr, mp = state[:3]
    az_speeds, rad_speeds = [], []
    inverse = [tiles_of(1.0 / across(rho, u)) for u in range(GROUPS)]
    for g in range(GROUPS):
        az_speeds.append(line_speeds(along(mp, g) * along(inverse, g), 1, COURANT_AZIMUTH))
        rad_speeds.append(line_speeds(across(mr, g) * across(inverse, g), 0, COURANT_RADIAL))

    def step(field):
        turned = [along(field, w) for w in range(GROUPS)]
        turned = [tiles_of(turned[w] - line_advect(turned[w], az_speeds[w], 1)) for w in range(GROUPS)]
        out = []
        for u in range(GROUPS):
            rest = line([turned[w][u] for w in range(GROUPS)])
            out.append(tiles_of(rest - line_advect(across(field, u), rad_speeds[u], 0)))
        return out

    return step


def push_all(state):
    scale = -0.5 * COURANT_AZIMUTH
    assert COURANT_RADIAL == COURANT_AZIMUTH
    rho, mr, mp, mz, energy = state
    inverse, pressure, density, new_mr, rest = [], [], [], [], []
    for u in range(GROUPS):
        r, a, b, c, e = (across(f, u) for f in state)
        inv = 1.0 / r
        p = (scale * (GAMMA_GAS - 1.0)) * (e - 0.5 * (a * a + b * b + c * c) * inv)
        d = (scale * VISCOSITY_COEF) * r
        rad_m, rad_e = line_push(p, d, a * inv, 0)
        inverse.append(tiles_of(inv))
        pressure.append(tiles_of(p))
        density.append(tiles_of(d))
        new_mr.append(tiles_of(a + rad_m))
        rest.append(tiles_of(e + rad_e))
    new_mp = [[None] * GROUPS for _ in range(GROUPS)]
    new_energy = [[None] * GROUPS for _ in range(GROUPS)]
    for w in range(GROUPS):
        b = along(mp, w)
        az_m, az_e = line_push(along(pressure, w), along(density, w), b * along(inverse, w), 1)
        for u, (m, e) in enumerate(zip(tiles_of(b + az_m), tiles_of(along(rest, w) + az_e))):
            new_mp[u][w], new_energy[u][w] = m, e
    return new_mr, new_mp, new_energy


def turned_kernel(n_az, n_rad, x_in, shifts_in, out, *scratch):
    (x, T4, EP, M, W, shifts, other, SC, AM, F, G, B, R, load_sem, table_sem, shift_sem, swap_sem, out_send, out_recv, pass_send, pass_recv,
     back_send, back_recv) = scratch
    fields, depth, width, lanes = x.shape
    blocks = n_az // (depth * n_rad)
    tiles = lanes // TILE
    rows = 4 * TILE
    MESH = pl.DeviceIdType.MESH
    me = lax.axis_index("az")
    core = lax.axis_index("rad")
    half = lax.rem(me // 2, 2)
    layer = lax.rem(me, 2)
    block = me // 4
    place = (half * blocks + block) * 2 + core
    partner = {"rad": 1 - core}
    here = half == core

    def remote(src, dst, send, recv, where):
        return pltpu.make_async_remote_copy(
            src_ref=src, dst_ref=dst, send_sem=send, recv_sem=recv, device_id=where, device_id_type=MESH
        )

    loads = [pltpu.make_async_copy(x_in.at[:, l], x.at[:, l], load_sem.at[l]) for l in range(depth)]
    for load in loads:
        load.start()
    table = pltpu.make_async_copy(shifts_in, shifts, table_sem)
    table.start()
    barrier = pltpu.get_barrier_semaphore()
    for k in range(n_az - 1):
        pl.semaphore_signal(
            barrier, inc=1, device_id={"az": k + (me <= k).astype(jnp.int32), "rad": half}, device_id_type=MESH
        )
    pl.semaphore_signal(barrier, inc=1, device_id=partner, device_id_type=MESH)

    lane = lax.broadcasted_iota(jnp.int32, (TILE, lanes), 1)
    row = lax.broadcasted_iota(jnp.int32, (TILE, lanes), 0)
    group = lane // width

    spin = me * TILE

    def rows_of(f, l):
        return [x[f, l, pl.ds(u, width // GROUPS, stride=GROUPS), :] for u in range(GROUPS)]

    for l in range(depth):
        loads[l].wait()
        cells = jnp.concatenate([part for f in range(GROUPS) for part in rows_of(f, l)], axis=0)
        T4[l, 1 : tiles + 1] = pltpu.roll(cells.T, spin, 1).reshape(tiles, TILE, lanes)
    energy = [part for l in range(depth) for part in rows_of(4, l)]
    turned = jnp.concatenate(energy * (lanes // (depth * width)), axis=0).T.reshape(tiles, TILE, lanes)
    for l in range(depth):
        for m in range(tiles // GROUPS):
            packed = turned[GROUPS * m] if l == 0 else lane_rows(turned[GROUPS * m], -width * l)
            for g in range(1, GROUPS):
                packed = jnp.where(group == g, lane_rows(turned[GROUPS * m + g], width * (g - l)), packed)
            EP[l, 1 + m] = packed

    @pl.when(core == 0)
    def _():
        for l in range(depth):
            T4[l, 0] = jnp.broadcast_to(T4[l, 1, 0:1], (TILE, lanes))
            EP[l, 0] = jnp.broadcast_to(lane_rows(EP[l, 1], -width)[0:1], (TILE, lanes))

    @pl.when(core == 1)
    def _():
        for l in range(depth):
            T4[l, tiles + 1] = jnp.broadcast_to(T4[l, tiles, TILE - 1 : TILE], (TILE, lanes))
            EP[l, blocks + 1] = jnp.broadcast_to(lane_rows(EP[l, blocks], width)[TILE - 1 : TILE], (TILE, lanes))

    def stage(l, s, c):
        own = EP[l, 1 + s]
        if c == 0:
            M[l, s, c, 0] = pltpu.roll(jnp.where(group == GROUPS - 1, EP[l, s], own), lax.rem(spin + width, lanes), 1)
            M[l, s, c, 1:3] = T4[l, GROUPS * s : GROUPS * s + 2]
        else:
            M[l, s, c, 1:3] = T4[l, GROUPS * s + 4 : GROUPS * s + 6]
            M[l, s, c, 3] = pltpu.roll(jnp.where(group == 0, EP[l, s + 2], own), lax.rem(spin + lanes - width, lanes), 1)

    late = ((0, 0), (blocks - 1, 1))
    for l in range(depth):
        for s in range(blocks):
            for c in range(2):
                M[l, s, c, 3 - 3 * c] = T4[l, GROUPS * s + 2 + c]
                if (s, c) not in late:
                    stage(l, s, c)

    table.wait()
    senders = jnp.where(here, 2 * (n_az // n_rad - 1) + 1, 2 * (n_az // n_rad) + 1)
    pl.semaphore_wait(barrier, senders)

    whole = behind // width
    tail = behind % width
    tail_rows = -(-tail // TILE) * TILE
    group = whole + 1
    base = group * width
    first_row = width - tail_rows
    me = lax.axis_index("az")
    place = lax.rem(me, group)
    position = lax.axis_index("rad")

    def az(by):
        return {"az": lax.rem(me + by + n_az, n_az)}

    def member(by):
        return {"az": me - place + lax.rem(place + by + group, group)}

    def rad(by):
        return {"rad": position + by}

    barrier = pltpu.get_barrier_semaphore()
    MESH = pl.DeviceIdType.MESH
    load = pltpu.make_async_copy(x_in, x, load_sem)
    load.start()
    for by in (1, -1, -group):
        pl.semaphore_signal(barrier, inc=1, device_id=az(by), device_id_type=MESH)
    for h in range(1, group):
        pl.semaphore_signal(barrier, inc=1, device_id=member(h), device_id_type=MESH)

    has_left = position > 0
    has_right = position < n_rad - 1

    @pl.when(has_left)
    def _():
        pl.semaphore_signal(barrier, inc=1, device_id=rad(-1), device_id_type=MESH)

    @pl.when(has_right)
    def _():
        pl.semaphore_signal(barrier, inc=1, device_id=rad(1), device_id_type=MESH)

    load.wait()
    A[:, :, TILE : TILE + width, :] = x[...]
    beside_me = (position + n_rad - 1) // n_rad + (2 * n_rad - 2 - position) // n_rad
    pl.semaphore_wait(barrier, group + 2 + beside_me)

    def remote(src, dst, send, recv, where):
        return pltpu.make_async_remote_copy(
            src_ref=src, dst_ref=dst, send_sem=send, recv_sem=recv, device_id=where, device_id_type=MESH
        )

    def ring_copies(z):
        return [
            remote(x.at[:, z, width - TILE : width], A.at[:, z, 0:TILE],
                   state_send.at[0, z], state_recv.at[0, z], az(1)),
            remote(x.at[:, z, 0:TILE], A.at[:, z, TILE + width : 2 * TILE + width],
                   state_send.at[1, z], state_recv.at[1, z], az(-1)),
        ]

    def side_copies(phase, src, left_dst, right_dst, z):
        to_right = remote(src.at[:, z], left_dst.at[:, z], side_send.at[phase, 0, z],
                          side_recv.at[phase, 0, z], rad(1))
        to_left = remote(src.at[:, z], right_dst.at[:, z], side_send.at[phase, 1, z],
                         side_recv.at[phase, 1, z], rad(-1))
        return to_right, to_left

    def start_side(*args):
        to_right, to_left = side_copies(*args)

        @pl.when(has_right)
        def _():
            to_right.start()

        @pl.when(has_left)
        def _():
            to_left.start()

    def await_side(*args):
        to_right, to_left = side_copies(*args)

        @pl.when(has_left)
        def _():
            to_right.wait_recv()

        @pl.when(has_right)
        def _():
            to_left.wait_recv()

    def end_side(*args):
        to_right, to_left = side_copies(*args)

        @pl.when(has_right)
        def _():
            to_right.wait_send()

        @pl.when(has_left)
        def _():
            to_left.wait_send()

    windows = (W0, W1)
    rotated = (O0, O1)
    sides = ((x, L0, R0), (O0, L1, R1), (O1, L2, R2))

    def gather_copies(step, f, z):
        W = windows[step]
        own, back = W.at[f, z, base : base + width], W.at[f, z, 0:width]
        sems = lambda h: (gather_send.at[step, h, f, z], gather_recv.at[step, h, f, z])
        onward = remote(own, back, *sems(0), az(group))
        inside = []
        for h in range(1, group):
            dst = W.at[f, z, base - h * width : base - (h - 1) * width]
            inside.append([remote(src, dst, *sems(h), member(h)) for src in (own, back)])
        return onward, inside

    def send_own(step, f, z):
        onward, inside = gather_copies(step, f, z)
        onward.start()
        for h in range(1, group):

            @pl.when(place + h < group)
            def _():
                inside[h - 1][0].start()

    def pass_on(step, f, z):
        onward, inside = gather_copies(step, f, z)
        onward.wait_recv()
        for h in range(1, group):

            @pl.when(place + h >= group)
            def _():
                inside[h - 1][1].start()

    def edges(own, left, right):
        rows = own.shape[0]
        lane = lax.broadcasted_iota(jnp.int32, (rows, lanes), 1)
        at = jnp.full((rows, lanes), position, jnp.int32)
        left = jnp.where(at == 0, jnp.broadcast_to(own[:, 0:1], own.shape), left)
        right = jnp.where(at == n_rad - 1, jnp.broadcast_to(own[:, lanes - 1 : lanes], own.shape), right)
        return jnp.where(lane < lanes // 2, right, left)

    def wide(own, beside):
        return jnp.concatenate([own, beside], axis=1)

    def hydro(step, z, strip, beside):
        rows = slice(TILE, TILE + width)
        tall = [strip(f) for f in range(fields)]
        az_speeds = face_speeds(tall[2] / tall[0], 0, COURANT_AZIMUTH)
        broad = [wide(tall[f][rows], beside(f, tall[f][rows])) for f in range(fields)]
        rad_speeds = face_speeds(broad[1] / broad[0], 1, COURANT_RADIAL)
        for f in range(fields):
            along = advect(tall[f], az_speeds, 0)[rows]
            across = advect(broad[f], rad_speeds, 1)[:, :lanes]
            windows[step][f, z, base : base + width, :] = tall[f][rows] - along - across
            send_own(step, f, z)

    def viscous(z, state, extended):
        rho, mr, mp, mz, energy = state
        own = slice(None) if extended else slice(0, lanes)
        inverse = 1.0 / rho
        pressure = (GAMMA_GAS - 1.0) * (energy - 0.5 * (mr * mr + mp * mp + mz * mz) * inverse)
        az_m, az_e = push(pressure[:, own], rho[:, own], (mp * inverse)[:, own], 0, COURANT_AZIMUTH)
        rad_m, rad_e = push(pressure, rho, mr * inverse, 1, COURANT_RADIAL)
        return [
            rho[:, own],
            mr[:, own] + rad_m[:, own],
            mp[:, own] + az_m,
            mz[:, own],
            energy[:, own] + az_e + rad_e[:, own],
        ]

    count = width + 2 * EDGE

    for z in range(depth):
        for copy in ring_copies(z):
            copy.start()
    for z in range(depth):
        start_side(0, *sides[0], z)
    for z in range(depth):
        for copy in ring_copies(z):
            copy.wait_recv()
        await_side(0, *sides[0], z)
        hydro(0, z, lambda f: A[f, z], lambda f, own: edges(own, L0[f, z], R0[f, z]))

    for step in range(STEPS):
        for z in range(depth):
            for f in range(fields):
                pass_on(step, f, z)
        O, L, R = sides[step + 1]
        for z in range(depth):
            for f in range(fields):
                for copies in gather_copies(step, f, z)[1]:
                    copies[0].wait_recv()
                start = base - first_row - EDGE
                O[f, z] = shifted(windows[step][f, z, first_row:], start - shifts[...], count, start - SMIN)
            start_side(step + 1, O, L, R, z)
        for z in range(depth):
            await_side(step + 1, O, L, R, z)
            state = [wide(O[f, z], edges(O[f, z], L[f, z], R[f, z])) for f in range(fields)]
            if step == STEPS - 1:
                new = viscous(z, state, False)
                for f in range(fields):
                    out[f, z] = new[f][EDGE : EDGE + width]
            else:
                new = viscous(z, state, True)
                A_rows = slice(TILE - EDGE, TILE - EDGE + count)
                for f in range(fields):
                    A[f, z, A_rows, :] = new[f][:, :lanes]
                hydro(
                    step + 1,
                    z,
                    lambda f: A[f, z],
                    lambda f, own: edges(own, *[new[f][EDGE : EDGE + width, lanes:]] * 2),
                )

    for z in range(depth):
        for copy in ring_copies(z):
            copy.wait_send()
        for phase in range(STEPS + 1):
            end_side(phase, *sides[phase], z)
        for step in range(STEPS):
            for f in range(fields):
                onward, inside = gather_copies(step, f, z)
                onward.wait_send()
                for copies in inside:
                    copies[0].wait_send()


def body(mesh, state, shifts):
    n_az, n_rad = mesh.shape["az"], mesh.shape["rad"]
    fields, depth, width, lanes = state.shape
    behind = SMAX + EDGE
    group = behind // width + 1
    window = (group + 1) * width
    count = width + 2 * EDGE
    vmem = lambda rows: pltpu.VMEM((fields, depth, rows, lanes), jnp.float32)
    dma = pltpu.SemaphoreType.DMA
    return pl.pallas_call(
        functools.partial(kernel, n_az, n_rad),
        out_shape=pltpu.VMEM(state.shape, state.dtype),
        in_specs=[pl.BlockSpec(memory_space=pl.ANY), pl.BlockSpec(memory_space=pltpu.VMEM)],
        out_specs=pl.BlockSpec(memory_space=pltpu.VMEM),
        scratch_shapes=[
            vmem(width),
            dma(()),
            vmem(width + 2 * TILE),
            vmem(window),
            vmem(window),
            vmem(count),
            vmem(count),
            vmem(width),
            vmem(width),
            vmem(count),
            vmem(count),
            vmem(count),
            vmem(count),
            dma((2, depth)),
            dma((2, depth)),
            dma((STEPS, group, fields, depth)),
            dma((STEPS, group, fields, depth)),
            dma((STEPS + 1, 2, depth)),
            dma((STEPS + 1, 2, depth)),
        ],
        compiler_params=pltpu.CompilerParams(collective_id=0, has_side_effects=True),
    )(state, shifts.reshape(1, -1))


GROUPS = 4


def lane_rows(x, shift):
    return pltpu.roll(x, shift % x.shape[1], 1)


def exchange(parts, lane):
    n = len(parts)
    out = [parts[-g % n] for g in range(n)]
    for bit in range(n.bit_length() - 1):
        far = (lane & (TILE << bit)) != 0
        out = [jnp.where(far, out[(g - (1 << bit)) % n], out[g]) for g in range(n)]
    return out


def fold(x, lane, row):
    half = x.shape[1] // 2
    stay = (lane < half) == (row < TILE // 2)
    return jnp.where(stay, x, lane_rows(pltpu.roll(x, TILE // 2, 0), half))


def line(tiles):
    return jnp.concatenate(tiles, axis=0)


def tiles_of(x):
    return [x[g * TILE : (g + 1) * TILE] for g in range(GROUPS)]


def next_of(x, axis):
    first = x[:TILE]
    return jnp.concatenate([x[TILE:], pltpu.roll(first, first.shape[axis] - 1, axis)], axis=0)


def last_of(x, axis):
    last = x[-TILE:]
    return jnp.concatenate([pltpu.roll(last, 1, axis), x[:-TILE]], axis=0)


def along(field, w):
    return line([field[u][w] for u in range(GROUPS)])


def across(field, u):
    return line(field[u])


def line_speeds(velocity, axis, courant):
    face = (0.5 * courant) * (velocity + next_of(velocity, axis))
    return jnp.maximum(face, 0.0), jnp.minimum(face, 0.0)


def line_advect(field, speeds, axis):
    low = field - last_of(field, axis)
    high = next_of(low, axis)
    product = low * high
    half = jnp.where(product > 0, product / (low + high), 0.0)
    flux = speeds[0] * (field + half) + speeds[1] * next_of(field - half, axis)
    return flux - last_of(flux, axis)


def line_push(pressure, density, speed, axis):
    compress = jnp.minimum(next_of(speed, axis) - last_of(speed, axis), 0.0)
    total = pressure + density * compress * compress
    work = total * speed
    return next_of(total, axis) - last_of(total, axis), next_of(work, axis) - last_of(work, axis)


def advect_all(state):
    rho, mr, mp = state[:3]
    az_speeds, rad_speeds = [], []
    inverse = [tiles_of(1.0 / across(rho, u)) for u in range(GROUPS)]
    for g in range(GROUPS):
        az_speeds.append(line_speeds(along(mp, g) * along(inverse, g), 1, COURANT_AZIMUTH))
        rad_speeds.append(line_speeds(across(mr, g) * across(inverse, g), 0, COURANT_RADIAL))

    def step(field):
        turned = [along(field, w) for w in range(GROUPS)]
        turned = [tiles_of(turned[w] - line_advect(turned[w], az_speeds[w], 1)) for w in range(GROUPS)]
        out = []
        for u in range(GROUPS):
            rest = line([turned[w][u] for w in range(GROUPS)])
            out.append(tiles_of(rest - line_advect(across(field, u), rad_speeds[u], 0)))
        return out

    return step


def push_all(state):
    scale = -0.5 * COURANT_AZIMUTH
    assert COURANT_RADIAL == COURANT_AZIMUTH
    rho, mr, mp, mz, energy = state
    inverse, pressure, density, new_mr, rest = [], [], [], [], []
    for u in range(GROUPS):
        r, a, b, c, e = (across(f, u) for f in state)
        inv = 1.0 / r
        p = (scale * (GAMMA_GAS - 1.0)) * (e - 0.5 * (a * a + b * b + c * c) * inv)
        d = (scale * VISCOSITY_COEF) * r
        rad_m, rad_e = line_push(p, d, a * inv, 0)
        inverse.append(tiles_of(inv))
        pressure.append(tiles_of(p))
        density.append(tiles_of(d))
        new_mr.append(tiles_of(a + rad_m))
        rest.append(tiles_of(e + rad_e))
    new_mp = [[None] * GROUPS for _ in range(GROUPS)]
    new_energy = [[None] * GROUPS for _ in range(GROUPS)]
    for w in range(GROUPS):
        b = along(mp, w)
        az_m, az_e = line_push(along(pressure, w), along(density, w), b * along(inverse, w), 1)
        for u, (m, e) in enumerate(zip(tiles_of(b + az_m), tiles_of(along(rest, w) + az_e))):
            new_mp[u][w], new_energy[u][w] = m, e
    return new_mr, new_mp, new_energy


def turned_kernel(n_az, n_rad, x_in, shifts_in, out, *scratch):
    (x, T4, EP, M, W, shifts, other, SC, AM, F, G, B, R, load_sem, table_sem, shift_sem, swap_sem, out_send, out_recv, pass_send, pass_recv,
     back_send, back_recv) = scratch
    fields, depth, width, lanes = x.shape
    blocks = n_az // (depth * n_rad)
    tiles = lanes // TILE
    rows = 4 * TILE
    MESH = pl.DeviceIdType.MESH
    me = lax.axis_index("az")
    core = lax.axis_index("rad")
    half = lax.rem(me // 2, 2)
    layer = lax.rem(me, 2)
    block = me // 4
    place = (half * blocks + block) * 2 + core
    partner = {"rad": 1 - core}
    here = half == core

    def remote(src, dst, send, recv, where):
        return pltpu.make_async_remote_copy(
            src_ref=src, dst_ref=dst, send_sem=send, recv_sem=recv, device_id=where, device_id_type=MESH
        )

    loads = [pltpu.make_async_copy(x_in.at[:, l], x.at[:, l], load_sem.at[l]) for l in range(depth)]
    for load in loads:
        load.start()
    table = pltpu.make_async_copy(shifts_in, shifts, table_sem)
    table.start()
    barrier = pltpu.get_barrier_semaphore()
    for k in range(n_az - 1):
        pl.semaphore_signal(
            barrier, inc=1, device_id={"az": k + (me <= k).astype(jnp.int32), "rad": half}, device_id_type=MESH
        )
    pl.semaphore_signal(barrier, inc=1, device_id=partner, device_id_type=MESH)

    lane = lax.broadcasted_iota(jnp.int32, (TILE, lanes), 1)
    row = lax.broadcasted_iota(jnp.int32, (TILE, lanes), 0)
    group = lane // width

    spin = me * TILE

    def rows_of(f, l):
        return [x[f, l, pl.ds(u, width // GROUPS, stride=GROUPS), :] for u in range(GROUPS)]

    for l in range(depth):
        loads[l].wait()
        cells = jnp.concatenate([part for f in range(GROUPS) for part in rows_of(f, l)], axis=0)
        T4[l, 1 : tiles + 1] = pltpu.roll(cells.T, spin, 1).reshape(tiles, TILE, lanes)
    energy = [part for l in range(depth) for part in rows_of(4, l)]
    turned = jnp.concatenate(energy * (lanes // (depth * width)), axis=0).T.reshape(tiles, TILE, lanes)
    for l in range(depth):
        for m in range(tiles // GROUPS):
            packed = turned[GROUPS * m] if l == 0 else lane_rows(turned[GROUPS * m], -width * l)
            for g in range(1, GROUPS):
                packed = jnp.where(group == g, lane_rows(turned[GROUPS * m + g], width * (g - l)), packed)
            EP[l, 1 + m] = packed

    @pl.when(core == 0)
    def _():
        for l in range(depth):
            T4[l, 0] = jnp.broadcast_to(T4[l, 1, 0:1], (TILE, lanes))
            EP[l, 0] = jnp.broadcast_to(lane_rows(EP[l, 1], -width)[0:1], (TILE, lanes))

    @pl.when(core == 1)
    def _():
        for l in range(depth):
            T4[l, tiles + 1] = jnp.broadcast_to(T4[l, tiles, TILE - 1 : TILE], (TILE, lanes))
            EP[l, blocks + 1] = jnp.broadcast_to(lane_rows(EP[l, blocks], width)[TILE - 1 : TILE], (TILE, lanes))

    def stage(l, s, c):
        own = EP[l, 1 + s]
        if c == 0:
            M[l, s, c, 0] = pltpu.roll(jnp.where(group == GROUPS - 1, EP[l, s], own), lax.rem(spin + width, lanes), 1)
            M[l, s, c, 1:3] = T4[l, GROUPS * s : GROUPS * s + 2]
        else:
            M[l, s, c, 1:3] = T4[l, GROUPS * s + 4 : GROUPS * s + 6]
            M[l, s, c, 3] = pltpu.roll(jnp.where(group == 0, EP[l, s + 2], own), lax.rem(spin + lanes - width, lanes), 1)

    late = ((0, 0), (blocks - 1, 1))
    for l in range(depth):
        for s in range(blocks):
            for c in range(2):
                M[l, s, c, 3 - 3 * c] = T4[l, GROUPS * s + 2 + c]
                if (s, c) not in late:
                    stage(l, s, c)

    table.wait()
    senders = jnp.where(here, 2 * (n_az // n_rad - 1) + 1, 2 * (n_az // n_rad) + 1)
    pl.semaphore_wait(barrier, senders)

    swap_shift = remote(shifts, other, shift_sem.at[0], shift_sem.at[1], partner)
    swap_shift.start()

    def swaps(l, up):
        src = (tiles, blocks) if up else (1, 1)
        dst = (0, 0) if up else (tiles + 1, blocks + 1)
        return [
            remote(T4.at[l, src[0]], T4.at[l, dst[0]], swap_sem.at[0, l], swap_sem.at[1, l], partner),
            remote(EP.at[l, src[1]], EP.at[l, dst[1]], swap_sem.at[2, l], swap_sem.at[3, l], partner),
        ]

    @pl.when(core == 0)
    def _():
        for l in range(depth):
            for copy in swaps(l, True):
                copy.start()

    @pl.when(core == 1)
    def _():
        for l in range(depth):
            for copy in swaps(l, False):
                copy.start()

    whole = ()
    split = (2, 1, 3, 0)
    targets = [(ks, kl, kc) for ks in (*whole, *split) for kl in (1, 0) for kc in (0, 1)]

    def send(index, first):
        ks, kl, kc = targets[index]
        s = lax.rem(block + ks, blocks)
        l = lax.rem(layer + kl, depth)
        c = lax.rem(core + kc, 2)
        if first:
            src, dst = M.at[l, s, c, 3 - 3 * c], W.at[me, 3 - 2 * c]
            sems = out_send.at[0, index], out_recv.at[0, me]
        else:
            if ks in split:
                src, dst = M.at[l, s, c, pl.ds(c, 3)], W.at[me, pl.ds(2 * c, 3)]
            else:
                src, dst = M.at[l, s, c], W.at[me, pl.ds(c, 4)]
            sems = out_send.at[1, index], out_recv.at[1, me]
        sent = remote(src, dst, *sems, {"az": s * 4 + core * 2 + l, "rad": c})
        is_late = s == c * (blocks - 1)
        return sent, None if ks or kl or kc else pltpu.make_async_copy(src, dst, sems[1]), is_late

    messages = [(index, True) for index, t in enumerate(targets) if t[0] in split]
    messages += [(index, False) for index in range(len(targets))]

    def start(first, when=None):
        for index, part in messages:
            if part != first:
                continue
            sent, within, is_late = send(index, first)
            if within is None and when is None:
                sent.start()
                continue
            now = True if when is None else when(is_late)
            for copy, also in ((sent, None),) if within is None else ((within, here), (sent, jnp.logical_not(here))):

                @pl.when(now if also is None else jnp.logical_and(now, also))
                def _():
                    copy.start()

    start(True)
    start(False, jnp.logical_not)
    for l in range(depth):
        for copy in swaps(l, True):
            copy.wait_recv()
    for l in range(depth):
        for s, c in late:
            stage(l, s, c)
    start(False, lambda is_late: is_late)

    swap_shift.wait_recv()
    lower = jnp.full((1, lanes), core, jnp.int32) == 0
    mine, theirs = shifts[...], other[...]
    for c in range(2):
        part = jnp.where(lower, mine if c == 0 else theirs, theirs if c == 0 else mine)
        table = jnp.broadcast_to(part.astype(jnp.float32), (lanes, lanes)).T.astype(jnp.int32)
        SC[TILE + c * lanes : TILE + (c + 1) * lanes] = table
    SC[0:TILE] = jnp.zeros((TILE, lanes), jnp.int32)
    SC[TILE + 2 * lanes :] = jnp.zeros((TILE, lanes), jnp.int32)
    AM[...] = SC[pl.ds(pl.multiple_of(place * 2 * TILE, TILE), rows)]
    amounts = [AM[pl.ds(w, TILE, stride=GROUPS), :] for w in range(GROUPS)]
    coarse = [amount // GROUPS for amount in amounts]
    odd = [(amount & 1) != 0 for amount in amounts]
    two = [(amount & 2) != 0 for amount in amounts]
    source = [
        [(lane - coarse[w] - jnp.where(u < (amounts[w] & (GROUPS - 1)), 1, 0)) & (lanes - 1) for w in range(GROUPS)]
        for u in range(GROUPS)
    ]

    plane = n_az // GROUPS

    def sender(ks):
        return lax.rem(block + blocks - ks, blocks)

    def passes(ks):
        ahead = pl.ds(sender(ks) * plane, plane)
        return remote(
            W.at[ahead, 3 - 2 * core], W.at[ahead, 4 * core], pass_send.at[ks], pass_recv.at[sender(ks)], partner
        )

    def passed(q):
        return remote(
            W.at[pl.ds(q * plane, plane), 3 - 2 * core], W.at[pl.ds(q * plane, plane), 4 - 4 * core],
            pass_send.at[q], pass_recv.at[q], partner
        )

    def arrived(dst, recv):
        return pltpu.make_async_copy(dst, dst, recv)

    def await_senders(ks, first):
        for j in range(plane):
            i = sender(ks) * plane + lax.rem(me + j, plane)
            if first:
                arrived(W.at[i, 3 - 2 * core], out_recv.at[0, i]).wait()
            elif ks in split:
                arrived(W.at[i, pl.ds(2 * core, 3)], out_recv.at[1, i]).wait()
            else:
                arrived(W.at[i, pl.ds(core, 4)], out_recv.at[1, i]).wait()

    for ks in split:
        await_senders(ks, True)
        passes(ks).start()
    for ks in whole:
        await_senders(ks, False)
        passes(ks).start()

    def rotate(field):
        out = [[None] * GROUPS for _ in range(GROUPS)]
        for w in range(GROUPS):
            near_by = [jnp.where(odd[w], field[u - 1][w], field[u][w]) for u in range(GROUPS)]
            for u in range(GROUPS):
                chosen = jnp.where(two[w], near_by[u - 2], near_by[u])
                out[u][w] = jnp.take_along_axis(chosen, source[u][w], axis=1)
        return out

    at = jnp.full((TILE, lanes), place, jnp.int32)
    lowest = jnp.logical_and(at == 0, row < 2)
    highest = jnp.logical_and(at == 2 * blocks * n_rad - 1, row >= TILE - 2)

    def edged(field):
        out = []
        for u in range(GROUPS):
            low = jnp.broadcast_to(field[u][0][2:3], (TILE, lanes))
            high = jnp.broadcast_to(field[u][3][TILE - 3 : TILE - 2], (TILE, lanes))
            out.append(
                [jnp.where(highest, high, field[u][w]) for w in range(2)]
                + [jnp.where(lowest, low, field[u][w]) for w in range(2, GROUPS)]
            )
        return out

    def unpack(parts):
        return [lane_rows(part, -TILE * g) for g, part in enumerate(exchange(parts, lane_of[parts[0].shape[0]]))]

    lane_of = {n * TILE: lax.broadcasted_iota(jnp.int32, (n * TILE, lanes), 1) for n in (1, 2, 3)}

    def settle(slot, at_row):
        for g, part in enumerate(unpack([W[i, pl.ds(slot, 2)].reshape(2 * TILE, lanes) for i in range(n_az)])):
            F[g, pl.ds(pl.multiple_of(at_row, TILE), 2 * TILE)] = part

    for q in range(GROUPS):
        passed(q).wait_recv()
    settle(3 - 3 * core, 2 * TILE * (1 - core))
    for ks in split:
        await_senders(ks, False)
    settle(1 + core, 2 * TILE * core)
    for g, part in enumerate(unpack([W[i, 4 * core] for i in range(n_az)])):
        w, u = g // GROUPS, g % GROUPS
        F[GROUPS * GROUPS + u, w * TILE : (w + 1) * TILE] = part

    state = [
        [[F[GROUPS * f + u, pl.ds(w, TILE, stride=GROUPS), :] for w in range(GROUPS)] for u in range(GROUPS)]
        for f in range(fields)
    ]
    step = advect_all(state)
    state = [edged(rotate(step(field))) for field in state]
    mr, mp, en = push_all(state)
    state = [edged(field) for field in (state[0], mr, mp, state[3], en)]
    step = advect_all(state)
    state = [edged(rotate(step(field))) for field in state]
    mr, mp, en = push_all(state)
    for f, field in enumerate((state[0], mr, mp, state[3], en)):
        for u in range(GROUPS):
            for w in range(GROUPS):
                G[GROUPS * f + u, pl.ds(w, TILE, stride=GROUPS), :] = field[u][w]

    order = [(k, j) for k in (2, 1, 3, 0) for j in [*range(1, plane), 0]]

    def back(index):
        k, j = order[index]
        n = order.index((k, j))
        if n == 0:
            i = 0
        elif n < 4:
            i = 1 + lax.rem(me + n - 1, 3)
        elif n < 8:
            i = 4 + lax.rem(me + n + 1, 4)
        else:
            i = 8 + lax.rem(me + n + 1, 8)
        src, dst = B.at[i], R.at[layer, block, core]
        sems = back_send.at[index], back_recv.at[(layer * blocks + block) * 2 + core]
        sent = remote(src, dst, *sems, {"az": i, "rad": half})
        return sent, None if n not in (0, 3, 7, 15) else pltpu.make_async_copy(src, dst, sems[1]), i == me

    own = [lane_rows(G[g, TILE : 3 * TILE], TILE * g) for g in range(GROUPS * GROUPS)]
    for i, part in enumerate(exchange(own, lane_of[2 * TILE])):
        B[i, : 2 * TILE] = part
    own = [
        lane_rows(G[GROUPS * GROUPS + u, (1 + t) * TILE : (2 + t) * TILE], TILE * (GROUPS * t + u))
        for t in range(2)
        for u in range(GROUPS)
    ]
    for i, part in enumerate(exchange(own, lane)):
        folded = fold(lane_rows(part, -TILE * i), lane, row)
        B[i, 2 * TILE :] = folded[: TILE // 2]
        B[i + n_az // 2, 2 * TILE :] = folded[TILE // 2 :]
    for index in range(len(order)):
        sent, within, same = back(index)
        if within is None:
            sent.start()
        else:

            @pl.when(jnp.logical_and(here, same))
            def _():
                within.start()

            @pl.when(jnp.logical_not(jnp.logical_and(here, same)))
            def _():
                sent.start()

    for l in range(depth):
        for s in range(blocks):
            for c in range(2):
                arrived(R.at[l, s, c], back_recv.at[(l * blocks + s) * 2 + c]).wait()
        pieces = [R[l, s, c, : 2 * TILE] for s in range(blocks) for c in range(2)]
        cells = pltpu.roll(jnp.concatenate(pieces, axis=0), lax.rem(lanes - spin, lanes), 1).T
        for f in range(GROUPS):
            for u in range(GROUPS):
                g = GROUPS * f + u
                out[f, l, pl.ds(u, TILE, stride=GROUPS), :] = cells[g * TILE : (g + 1) * TILE]
    pieces = []
    for s in range(blocks):
        both = [fold(jnp.concatenate([R[l, s, c, 2 * TILE :] for c in range(2)], axis=0), lane, row) for l in range(depth)]
        for g in range(GROUPS):
            piece = lane_rows(both[0], -width * g)
            for l in range(1, depth):
                piece = jnp.where(group == l, lane_rows(both[l], width * (l - g)), piece)
            pieces.append(piece)
    cells = jnp.concatenate(pieces, axis=0).T
    for l in range(depth):
        for u in range(GROUPS):
            g = GROUPS * l + u
            out[4, l, pl.ds(u, TILE, stride=GROUPS), :] = cells[g * TILE : (g + 1) * TILE]

    swap_shift.wait_send()
    for l in range(depth):
        for copy in swaps(l, True):
            copy.wait_send()
    for index, first in messages:
        sent, within, _ = send(index, first)
        if within is None:
            sent.wait_send()
        else:

            @pl.when(jnp.logical_not(here))
            def _():
                sent.wait_send()

    for k in range(GROUPS):
        passes(k).wait_send()
    for index in range(len(order)):
        sent, within, same = back(index)
        if within is None:
            sent.wait_send()
        else:

            @pl.when(jnp.logical_not(jnp.logical_and(here, same)))
            def _():
                sent.wait_send()


def turned_body(mesh, state, shifts):
    n_az, n_rad = mesh.shape["az"], mesh.shape["rad"]
    fields, depth, width, lanes = state.shape
    blocks = n_az // (depth * n_rad)
    tiles = lanes // TILE
    vmem = lambda *shape: pltpu.VMEM(shape, jnp.float32)
    dma = pltpu.SemaphoreType.DMA
    tile = (TILE, lanes)
    return pl.pallas_call(
        functools.partial(turned_kernel, n_az, n_rad),
        out_shape=pltpu.VMEM(state.shape, state.dtype),
        in_specs=[pl.BlockSpec(memory_space=pl.ANY)] * 2,
        out_specs=pl.BlockSpec(memory_space=pltpu.VMEM),
        scratch_shapes=[
            vmem(fields, depth, width, lanes),
            vmem(depth, tiles + 2, *tile),
            vmem(depth, blocks + 2, *tile),
            vmem(depth, blocks, 2, 4, *tile),
            vmem(n_az, 5, *tile),
            pltpu.VMEM((1, lanes), jnp.int32),
            pltpu.VMEM((1, lanes), jnp.int32),
            pltpu.VMEM((2 * lanes + 2 * TILE, lanes), jnp.int32),
            pltpu.VMEM((4 * TILE, lanes), jnp.int32),
            vmem(GROUPS * fields, 4 * TILE, lanes),
            vmem(GROUPS * fields, 4 * TILE, lanes),
            vmem(n_az, 2 * TILE + TILE // 2, lanes),
            vmem(depth, blocks, 2, 2 * TILE + TILE // 2, lanes),
            dma((depth,)),
            dma(()),
            dma((2,)),
            dma((4, depth)),
            dma((2, n_az)),
            dma((2, n_az)),
            dma((GROUPS,)),
            dma((GROUPS,)),
            dma((n_az,)),
            dma((n_az,)),
        ],
        compiler_params=pltpu.CompilerParams(collective_id=0, has_side_effects=True),
    )(state, shifts.reshape(1, -1))


def turns(mesh, state):
    n_az, n_rad = mesh.shape["az"], mesh.shape["rad"]
    fields, depth, width, lanes = state.shape
    tiles = lanes // TILE
    return (
        n_rad == 2
        and fields == GROUPS + 1
        and width * GROUPS == lanes
        and n_az == GROUPS * GROUPS
        and width == GROUPS * TILE
        and lanes == n_az * TILE
        and n_az % (depth * n_rad) == 0
        and tiles == GROUPS * (n_az // (depth * n_rad))
        and depth * width <= lanes
        and SMAX <= lanes
    )


def choose(mesh, state, shifts):
    return (turned_body if turns(mesh, state) else body)(mesh, state, shifts)


def solution(mesh):
    in_specs = (P(None, None, "az", "rad"), P("rad"))
    out_specs = P(None, None, "az", "rad")
    return jax.shard_map(
        functools.partial(choose, mesh), mesh=mesh, in_specs=in_specs, out_specs=out_specs, check_vma=False
    )
```

```python
import functools

import jax
import jax.numpy as jnp
from jax import lax
from jax.experimental import pallas as pl
from jax.experimental.pallas import tpu as pltpu
from jax.sharding import PartitionSpec as P

STEPS = 2
SMIN = 4
SMAX = 96
EDGE = 4
TILE = 8

GAMMA_GAS = 1.4
COURANT_RADIAL = 0.15
COURANT_AZIMUTH = 0.15
VISCOSITY_COEF = 1.0


def up(x, axis):
    return pltpu.roll(x, x.shape[axis] - 1, axis)


def down(x, axis):
    return pltpu.roll(x, 1, axis)


def face_speeds(velocity, axis, courant):
    face = (0.5 * courant) * (velocity + up(velocity, axis))
    return jnp.maximum(face, 0.0), jnp.minimum(face, 0.0)


def advect(field, speeds, axis):
    low = field - down(field, axis)
    high = up(low, axis)
    product = low * high
    positive = product > 0
    half = jnp.where(positive, product / jnp.where(positive, low + high, 1.0), 0.0)
    flux = speeds[0] * (field + half) + speeds[1] * up(field - half, axis)
    return flux - down(flux, axis)


def push(pressure, density, speed, axis, courant):
    compress = jnp.minimum(up(speed, axis) - down(speed, axis), 0.0)
    total = pressure + VISCOSITY_COEF * density * compress * compress
    work = total * speed
    scale = -0.5 * courant
    return scale * (up(total, axis) - down(total, axis)), scale * (up(work, axis) - down(work, axis))


def shifted(window, shift_left, rows, longest):
    bits = longest.bit_length()
    x = window
    for bit in reversed(range(bits)):
        stride = 1 << bit
        left = stride - 1
        if stride >= TILE:
            keep = -(-(rows + left) // TILE) * TILE
            chosen = min(keep, x.shape[0] - stride)
            mask = (jnp.broadcast_to(shift_left, (chosen, shift_left.shape[1])) & stride) != 0
            y = jnp.where(mask, x[stride : stride + chosen], x[:chosen])
            x = y if chosen == keep else jnp.concatenate([y, x[chosen:keep]], axis=0)
        else:
            mask = (jnp.broadcast_to(shift_left, x.shape) & stride) != 0
            x = jnp.where(mask, pltpu.roll(x, x.shape[0] - stride, 0), x)
    return x[:rows]


def kernel(n_az, n_rad, x_in, shifts, out, *scratch):
    (x, load_sem, A, W0, W1, O0, O1, L0, R0, L1, R1, L2, R2, state_send, state_recv, gather_send, gather_recv,
     side_send, side_recv) = scratch
    fields, depth, width, lanes = x.shape
    behind = SMAX + EDGE
    whole = behind // width
    tail = behind % width
    tail_rows = -(-tail // TILE) * TILE
    group = whole + 1
    base = group * width
    first_row = width - tail_rows
    me = lax.axis_index("az")
    place = lax.rem(me, group)
    position = lax.axis_index("rad")

    def az(by):
        return {"az": lax.rem(me + by + n_az, n_az)}

    def member(by):
        return {"az": me - place + lax.rem(place + by + group, group)}

    def rad(by):
        return {"rad": position + by}

    barrier = pltpu.get_barrier_semaphore()
    MESH = pl.DeviceIdType.MESH
    load = pltpu.make_async_copy(x_in, x, load_sem)
    load.start()
    for by in (1, -1, -group):
        pl.semaphore_signal(barrier, inc=1, device_id=az(by), device_id_type=MESH)
    for h in range(1, group):
        pl.semaphore_signal(barrier, inc=1, device_id=member(h), device_id_type=MESH)

    has_left = position > 0
    has_right = position < n_rad - 1

    @pl.when(has_left)
    def _():
        pl.semaphore_signal(barrier, inc=1, device_id=rad(-1), device_id_type=MESH)

    @pl.when(has_right)
    def _():
        pl.semaphore_signal(barrier, inc=1, device_id=rad(1), device_id_type=MESH)

    load.wait()
    A[:, :, TILE : TILE + width, :] = x[...]
    beside_me = (position + n_rad - 1) // n_rad + (2 * n_rad - 2 - position) // n_rad
    pl.semaphore_wait(barrier, group + 2 + beside_me)

    def remote(src, dst, send, recv, where):
        return pltpu.make_async_remote_copy(
            src_ref=src, dst_ref=dst, send_sem=send, recv_sem=recv, device_id=where, device_id_type=MESH
        )

    def ring_copies(z):
        return [
            remote(x.at[:, z, width - TILE : width], A.at[:, z, 0:TILE],
                   state_send.at[0, z], state_recv.at[0, z], az(1)),
            remote(x.at[:, z, 0:TILE], A.at[:, z, TILE + width : 2 * TILE + width],
                   state_send.at[1, z], state_recv.at[1, z], az(-1)),
        ]

    def side_copies(phase, src, left_dst, right_dst, z):
        to_right = remote(src.at[:, z], left_dst.at[:, z], side_send.at[phase, 0, z],
                          side_recv.at[phase, 0, z], rad(1))
        to_left = remote(src.at[:, z], right_dst.at[:, z], side_send.at[phase, 1, z],
                         side_recv.at[phase, 1, z], rad(-1))
        return to_right, to_left

    def start_side(*args):
        to_right, to_left = side_copies(*args)

        @pl.when(has_right)
        def _():
            to_right.start()

        @pl.when(has_left)
        def _():
            to_left.start()

    def await_side(*args):
        to_right, to_left = side_copies(*args)

        @pl.when(has_left)
        def _():
            to_right.wait_recv()

        @pl.when(has_right)
        def _():
            to_left.wait_recv()

    def end_side(*args):
        to_right, to_left = side_copies(*args)

        @pl.when(has_right)
        def _():
            to_right.wait_send()

        @pl.when(has_left)
        def _():
            to_left.wait_send()

    windows = (W0, W1)
    rotated = (O0, O1)
    sides = ((x, L0, R0), (O0, L1, R1), (O1, L2, R2))

    def gather_copies(step, f, z):
        W = windows[step]
        own, back = W.at[f, z, base : base + width], W.at[f, z, 0:width]
        sems = lambda h: (gather_send.at[step, h, f, z], gather_recv.at[step, h, f, z])
        onward = remote(own, back, *sems(0), az(group))
        inside = []
        for h in range(1, group):
            dst = W.at[f, z, base - h * width : base - (h - 1) * width]
            inside.append([remote(src, dst, *sems(h), member(h)) for src in (own, back)])
        return onward, inside

    def send_own(step, f, z):
        onward, inside = gather_copies(step, f, z)
        onward.start()
        for h in range(1, group):

            @pl.when(place + h < group)
            def _():
                inside[h - 1][0].start()

    def pass_on(step, f, z):
        onward, inside = gather_copies(step, f, z)
        onward.wait_recv()
        for h in range(1, group):

            @pl.when(place + h >= group)
            def _():
                inside[h - 1][1].start()

    def edges(own, left, right):
        rows = own.shape[0]
        lane = lax.broadcasted_iota(jnp.int32, (rows, lanes), 1)
        at = jnp.full((rows, lanes), position, jnp.int32)
        left = jnp.where(at == 0, jnp.broadcast_to(own[:, 0:1], own.shape), left)
        right = jnp.where(at == n_rad - 1, jnp.broadcast_to(own[:, lanes - 1 : lanes], own.shape), right)
        return jnp.where(lane < lanes // 2, right, left)

    def wide(own, beside):
        return jnp.concatenate([own, beside], axis=1)

    def hydro(step, z, strip, beside):
        rows = slice(TILE, TILE + width)
        tall = [strip(f) for f in range(fields)]
        az_speeds = face_speeds(tall[2] / tall[0], 0, COURANT_AZIMUTH)
        broad = [wide(tall[f][rows], beside(f, tall[f][rows])) for f in range(fields)]
        rad_speeds = face_speeds(broad[1] / broad[0], 1, COURANT_RADIAL)
        for f in range(fields):
            along = advect(tall[f], az_speeds, 0)[rows]
            across = advect(broad[f], rad_speeds, 1)[:, :lanes]
            windows[step][f, z, base : base + width, :] = tall[f][rows] - along - across
            send_own(step, f, z)

    def viscous(z, state, extended):
        rho, mr, mp, mz, energy = state
        own = slice(None) if extended else slice(0, lanes)
        inverse = 1.0 / rho
        pressure = (GAMMA_GAS - 1.0) * (energy - 0.5 * (mr * mr + mp * mp + mz * mz) * inverse)
        az_m, az_e = push(pressure[:, own], rho[:, own], (mp * inverse)[:, own], 0, COURANT_AZIMUTH)
        rad_m, rad_e = push(pressure, rho, mr * inverse, 1, COURANT_RADIAL)
        return [
            rho[:, own],
            mr[:, own] + rad_m[:, own],
            mp[:, own] + az_m,
            mz[:, own],
            energy[:, own] + az_e + rad_e[:, own],
        ]

    count = width + 2 * EDGE

    for z in range(depth):
        for copy in ring_copies(z):
            copy.start()
    for z in range(depth):
        start_side(0, *sides[0], z)
    for z in range(depth):
        for copy in ring_copies(z):
            copy.wait_recv()
        await_side(0, *sides[0], z)
        hydro(0, z, lambda f: A[f, z], lambda f, own: edges(own, L0[f, z], R0[f, z]))

    for step in range(STEPS):
        for z in range(depth):
            for f in range(fields):
                pass_on(step, f, z)
        O, L, R = sides[step + 1]
        for z in range(depth):
            for f in range(fields):
                for copies in gather_copies(step, f, z)[1]:
                    copies[0].wait_recv()
                start = base - first_row - EDGE
                O[f, z] = shifted(windows[step][f, z, first_row:], start - shifts[...], count, start - SMIN)
            start_side(step + 1, O, L, R, z)
        for z in range(depth):
            await_side(step + 1, O, L, R, z)
            state = [wide(O[f, z], edges(O[f, z], L[f, z], R[f, z])) for f in range(fields)]
            if step == STEPS - 1:
                new = viscous(z, state, False)
                for f in range(fields):
                    out[f, z] = new[f][EDGE : EDGE + width]
            else:
                new = viscous(z, state, True)
                A_rows = slice(TILE - EDGE, TILE - EDGE + count)
                for f in range(fields):
                    A[f, z, A_rows, :] = new[f][:, :lanes]
                hydro(
                    step + 1,
                    z,
                    lambda f: A[f, z],
                    lambda f, own: edges(own, *[new[f][EDGE : EDGE + width, lanes:]] * 2),
                )

    for z in range(depth):
        for copy in ring_copies(z):
            copy.wait_send()
        for phase in range(STEPS + 1):
            end_side(phase, *sides[phase], z)
        for step in range(STEPS):
            for f in range(fields):
                onward, inside = gather_copies(step, f, z)
                onward.wait_send()
                for copies in inside:
                    copies[0].wait_send()


def body(mesh, state, shifts):
    n_az, n_rad = mesh.shape["az"], mesh.shape["rad"]
    fields, depth, width, lanes = state.shape
    behind = SMAX + EDGE
    group = behind // width + 1
    window = (group + 1) * width
    count = width + 2 * EDGE
    vmem = lambda rows: pltpu.VMEM((fields, depth, rows, lanes), jnp.float32)
    dma = pltpu.SemaphoreType.DMA
    return pl.pallas_call(
        functools.partial(kernel, n_az, n_rad),
        out_shape=pltpu.VMEM(state.shape, state.dtype),
        in_specs=[pl.BlockSpec(memory_space=pl.ANY), pl.BlockSpec(memory_space=pltpu.VMEM)],
        out_specs=pl.BlockSpec(memory_space=pltpu.VMEM),
        scratch_shapes=[
            vmem(width),
            dma(()),
            vmem(width + 2 * TILE),
            vmem(window),
            vmem(window),
            vmem(count),
            vmem(count),
            vmem(width),
            vmem(width),
            vmem(count),
            vmem(count),
            vmem(count),
            vmem(count),
            dma((2, depth)),
            dma((2, depth)),
            dma((STEPS, group, fields, depth)),
            dma((STEPS, group, fields, depth)),
            dma((STEPS + 1, 2, depth)),
            dma((STEPS + 1, 2, depth)),
        ],
        compiler_params=pltpu.CompilerParams(collective_id=0, has_side_effects=True),
    )(state, shifts.reshape(1, -1))


GROUPS = 4


def lane_rows(x, shift):
    return pltpu.roll(x, shift % x.shape[1], 1)


def exchange(parts, lane):
    n = len(parts)
    out = [parts[-g % n] for g in range(n)]
    for bit in range(n.bit_length() - 1):
        far = (lane & (TILE << bit)) != 0
        out = [jnp.where(far, out[(g - (1 << bit)) % n], out[g]) for g in range(n)]
    return out


def fold(x, lane, row):
    half = x.shape[1] // 2
    stay = (lane < half) == (row < TILE // 2)
    return jnp.where(stay, x, lane_rows(pltpu.roll(x, TILE // 2, 0), half))


def line(tiles):
    return jnp.concatenate(tiles, axis=0)


def tiles_of(x):
    return [x[g : g + TILE] for g in range(0, x.shape[0], TILE)]


def next_of(x, axis):
    first = x[:TILE]
    return jnp.concatenate([x[TILE:], pltpu.roll(first, first.shape[axis] - 1, axis)], axis=0)


def last_of(x, axis):
    last = x[-TILE:]
    return jnp.concatenate([pltpu.roll(last, 1, axis), x[:-TILE]], axis=0)


def along(field, w):
    return line([field[u][w] for u in range(GROUPS)])


def across(field, u):
    return line(field[u])


def line_speeds(velocity, axis, courant):
    face = (0.5 * courant) * (velocity + next_of(velocity, axis))
    return jnp.maximum(face, 0.0), jnp.minimum(face, 0.0)


def line_advect(field, speeds, axis):
    low = field - last_of(field, axis)
    high = next_of(low, axis)
    product = low * high
    half = jnp.where(product > 0, product / (low + high), 0.0)
    flux = speeds[0] * (field + half) + speeds[1] * next_of(field - half, axis)
    return flux - last_of(flux, axis)


def line_push(pressure, density, speed, axis):
    compress = jnp.minimum(next_of(speed, axis) - last_of(speed, axis), 0.0)
    total = pressure + density * compress * compress
    work = total * speed
    return next_of(total, axis) - last_of(total, axis), next_of(work, axis) - last_of(work, axis)


def advect_all(state):
    rho, mr, mp = state[:3]
    span = len(rho[0])
    inverse = [tiles_of(1.0 / across(rho, u)) for u in range(GROUPS)]
    az_speeds = [line_speeds(along(mp, w) * along(inverse, w), 1, COURANT_AZIMUTH) for w in range(span)]
    rad_speeds = [line_speeds(across(mr, u) * across(inverse, u), 0, COURANT_RADIAL) for u in range(GROUPS)]

    def step(field):
        turned = [along(field, w) for w in range(span)]
        turned = [tiles_of(turned[w] - line_advect(turned[w], az_speeds[w], 1)) for w in range(span)]
        out = []
        for u in range(GROUPS):
            rest = line([turned[w][u] for w in range(span)])
            out.append(tiles_of(rest - line_advect(across(field, u), rad_speeds[u], 0)))
        return out

    return step


def push_all(state):
    scale = -0.5 * COURANT_AZIMUTH
    assert COURANT_RADIAL == COURANT_AZIMUTH
    rho, mr, mp, mz, energy = state
    inverse, pressure, density, new_mr, rest = [], [], [], [], []
    for u in range(GROUPS):
        r, a, b, c, e = (across(f, u) for f in state)
        inv = 1.0 / r
        p = (scale * (GAMMA_GAS - 1.0)) * (e - 0.5 * (a * a + b * b + c * c) * inv)
        d = (scale * VISCOSITY_COEF) * r
        rad_m, rad_e = line_push(p, d, a * inv, 0)
        inverse.append(tiles_of(inv))
        pressure.append(tiles_of(p))
        density.append(tiles_of(d))
        new_mr.append(tiles_of(a + rad_m))
        rest.append(tiles_of(e + rad_e))
    span = len(rho[0])
    new_mp = [[None] * span for _ in range(GROUPS)]
    new_energy = [[None] * span for _ in range(GROUPS)]
    for w in range(span):
        b = along(mp, w)
        az_m, az_e = line_push(along(pressure, w), along(density, w), b * along(inverse, w), 1)
        for u, (m, e) in enumerate(zip(tiles_of(b + az_m), tiles_of(along(rest, w) + az_e))):
            new_mp[u][w], new_energy[u][w] = m, e
    return new_mr, new_mp, new_energy


def turned_kernel(n_az, n_rad, x_in, shifts_in, out, *scratch):
    (x, T4, EP, M, W, shifts, other, SC, AM, F, G, B, R, load_sem, table_sem, shift_sem, swap_sem, out_send, out_recv,
     pass_send, pass_recv, back_send, back_recv) = scratch
    fields, depth, width, lanes = x.shape
    plane = n_az // GROUPS
    workers = n_az // 2
    blocks = workers // (depth * n_rad)
    tiles = lanes // TILE
    quads = tiles // GROUPS
    own = tiles // (2 * blocks)
    span = own + 2
    parts = span + 1
    rows = span * TILE
    MESH = pl.DeviceIdType.MESH
    me = lax.axis_index("az")
    core = lax.axis_index("rad")
    half = lax.rem(me // depth, n_rad)
    layer = lax.rem(me, depth)
    block = me // plane - 1
    works = jnp.logical_and(block >= 0, block < blocks)
    place = (half * blocks + block) * 2 + core
    partner = {"rad": 1 - core}
    here = half == core
    stays = jnp.logical_and(works, here)

    def remote(src, dst, send, recv, where):
        return pltpu.make_async_remote_copy(
            src_ref=src, dst_ref=dst, send_sem=send, recv_sem=recv, device_id=where, device_id_type=MESH
        )

    def arrived(dst, recv):
        return pltpu.make_async_copy(dst, dst, recv)

    barrier = pltpu.get_barrier_semaphore()

    @pl.when(works)
    def _():
        for k in range(n_az - 1):
            pl.semaphore_signal(
                barrier, inc=1, device_id={"az": k + (me <= k).astype(jnp.int32), "rad": half}, device_id_type=MESH
            )

    pl.semaphore_signal(barrier, inc=1, device_id=partner, device_id_type=MESH)
    loads = [pltpu.make_async_copy(x_in.at[:, l], x.at[:, l], load_sem.at[l]) for l in range(depth)]
    for load in loads:
        load.start()
    table = pltpu.make_async_copy(shifts_in, shifts, table_sem)
    table.start()

    lane = lax.broadcasted_iota(jnp.int32, (TILE, lanes), 1)
    row = lax.broadcasted_iota(jnp.int32, (TILE, lanes), 0)
    lane_of = {n * TILE: lax.broadcasted_iota(jnp.int32, (n * TILE, lanes), 1) for n in (1, 2, own)}
    group = lane // width
    spin = me * TILE
    unspin = lax.rem(lanes - spin, lanes)

    def rows_of(f, l):
        return [x[f, l, pl.ds(u, width // GROUPS, stride=GROUPS), :] for u in range(GROUPS)]

    for l in range(depth):
        loads[l].wait()
        cells = jnp.concatenate([part for f in range(GROUPS) for part in rows_of(f, l)], axis=0)
        T4[l, 1 : tiles + 1] = pltpu.roll(cells.T, spin, 1).reshape(tiles, TILE, lanes)
    energy = [part for l in range(depth) for part in rows_of(4, l)]
    turned = jnp.concatenate(energy * (lanes // (depth * width)), axis=0).T.reshape(tiles, TILE, lanes)
    for l in range(depth):
        for m in range(quads):
            packed = turned[GROUPS * m] if l == 0 else lane_rows(turned[GROUPS * m], -width * l)
            for g in range(1, GROUPS):
                packed = jnp.where(group == g, lane_rows(turned[GROUPS * m + g], width * (g - l)), packed)
            EP[l, 1 + m] = packed

    @pl.when(core == 0)
    def _():
        for l in range(depth):
            T4[l, 0] = jnp.broadcast_to(T4[l, 1, 0:1], (TILE, lanes))
            EP[l, 0] = jnp.broadcast_to(lane_rows(EP[l, 1], -width)[0:1], (TILE, lanes))

    @pl.when(core == 1)
    def _():
        for l in range(depth):
            T4[l, tiles + 1] = jnp.broadcast_to(T4[l, tiles, TILE - 1 : TILE], (TILE, lanes))
            EP[l, quads + 1] = jnp.broadcast_to(lane_rows(EP[l, quads], width)[TILE - 1 : TILE], (TILE, lanes))

    def energy_of(l, m):
        joined = jnp.where(group == GROUPS - 1, EP[l, m], EP[l, m + 1])
        return pltpu.roll(joined, lax.rem(spin + width, lanes), 1)

    def stage(l, s, c):
        first = 2 * own * s + c * (own + 1)
        if c == 0:
            M[l, s, c, 0], M[l, s, c, 1] = energy_of(l, 2 * s), energy_of(l, 2 * s + 1)
            M[l, s, c, 2 : own + 2] = T4[l, first : first + own]
        else:
            M[l, s, c, 1 : own + 1] = T4[l, first + 1 : first + own + 1]
            M[l, s, c, own + 1], M[l, s, c, own + 2] = energy_of(l, 2 * s + 1), energy_of(l, 2 * s + 2)

    late = ((0, 0), (blocks - 1, 1))
    for l in range(depth):
        for s in range(blocks):
            for c in range(2):
                M[l, s, c, (parts - 1) * (1 - c)] = T4[l, 2 * own * s + own + c]
                if (s, c) not in late:
                    stage(l, s, c)

    table.wait()
    pl.semaphore_wait(barrier, jnp.where(stays, 2 * (workers // n_rad) - 1, 2 * (workers // n_rad) + 1))

    targets = [(ks, kl, kc) for ks in (1, 0) for kl in (1, 0) for kc in (0, 1)]

    def send(index, first):
        ks, kl, kc = targets[index]
        s = lax.rem(me // plane + 1 + ks, blocks)
        l = lax.rem(layer + kl, depth)
        c = lax.rem(core + kc, 2)
        if first:
            src, dst = M.at[l, s, c, (parts - 1) * (1 - c)], W.at[me, (parts - 1) - (parts - 2) * c]
            sems = out_send.at[0, index], out_recv.at[0, me]
        else:
            src, dst = M.at[l, s, c, pl.ds(c, parts - 1)], W.at[me, pl.ds(2 * c, parts - 1)]
            sems = out_send.at[1, index], out_recv.at[1, me]
        sent = remote(src, dst, *sems, {"az": (1 + s) * plane + core * depth + l, "rad": c})
        is_late = s == c * (blocks - 1)
        return sent, None if ks or kl or kc else pltpu.make_async_copy(src, dst, sems[1]), is_late

    def start(first, when=None):
        for index in range(len(targets)):
            sent, within, is_late = send(index, first)
            if within is None and when is None:
                sent.start()
                continue
            now = True if when is None else when(is_late)
            for copy, also in ((sent, None),) if within is None else ((within, stays), (sent, jnp.logical_not(stays))):

                @pl.when(now if also is None else jnp.logical_and(now, also))
                def _():
                    copy.start()

    start(True)

    swap_shift = remote(shifts, other, shift_sem.at[0], shift_sem.at[1], partner)
    swap_shift.start()

    def swaps(l, up):
        src = (tiles, quads) if up else (1, 1)
        dst = (0, 0) if up else (tiles + 1, quads + 1)
        return [
            remote(T4.at[l, src[0]], T4.at[l, dst[0]], swap_sem.at[0, l], swap_sem.at[1, l], partner),
            remote(EP.at[l, src[1]], EP.at[l, dst[1]], swap_sem.at[2, l], swap_sem.at[3, l], partner),
        ]

    @pl.when(core == 0)
    def _():
        for l in range(depth):
            for copy in swaps(l, True):
                copy.start()

    @pl.when(core == 1)
    def _():
        for l in range(depth):
            for copy in swaps(l, False):
                copy.start()

    start(False, jnp.logical_not)
    for l in range(depth):
        for copy in swaps(l, True):
            copy.wait_recv()
    for l in range(depth):
        for s, c in late:
            stage(l, s, c)
    start(False, lambda is_late: is_late)
    swap_shift.wait_recv()

    def passes(k):
        q = lax.rem(me // plane + k, GROUPS)
        ahead = pl.ds(q * plane, plane)
        src, dst = W.at[ahead, (parts - 1) - (parts - 2) * core], W.at[ahead, parts * core]
        return remote(src, dst, pass_send.at[k], pass_recv.at[q], partner)

    def passed(q):
        return arrived(W.at[pl.ds(q * plane, plane), parts * (1 - core)], pass_recv.at[q])

    order = range(n_az)

    def back(n):
        if n == 0:
            i = 0
        elif n < plane:
            i = 1 + lax.rem(me + n - 1, plane - 1)
        elif n < 2 * plane:
            i = plane + lax.rem(me + n + 1, plane)
        else:
            i = 2 * plane + lax.rem(me + n + 1, 2 * plane)
        src, dst = B.at[i], R.at[layer, block, core]
        sems = back_send.at[n], back_recv.at[(layer * blocks + block) * 2 + core]
        sent = remote(src, dst, *sems, {"az": i, "rad": half})
        return sent, pltpu.make_async_copy(src, dst, sems[1]) if n in (2 * plane - 1, n_az - 1) else None, me == i

    @pl.when(works)
    def _():
        lower = jnp.full((1, lanes), core, jnp.int32) == 0
        mine, theirs = shifts[...], other[...]
        for c in range(2):
            part = jnp.where(lower, mine if c == 0 else theirs, theirs if c == 0 else mine)
            along_lanes = jnp.broadcast_to(part.astype(jnp.float32), (lanes, lanes)).T.astype(jnp.int32)
            SC[TILE + c * lanes : TILE + (c + 1) * lanes] = along_lanes
        SC[0:TILE] = jnp.zeros((TILE, lanes), jnp.int32)
        SC[TILE + 2 * lanes :] = jnp.zeros((TILE, lanes), jnp.int32)
        AM[...] = SC[pl.ds(pl.multiple_of(place * own * TILE, TILE), rows)]
        amounts = [AM[pl.ds(w, TILE, stride=span), :] for w in range(span)]
        coarse = [amount // GROUPS for amount in amounts]
        odd = [(amount & 1) != 0 for amount in amounts]
        two = [(amount & 2) != 0 for amount in amounts]
        source = [
            [
                (lane - coarse[w] - jnp.where(u < (amounts[w] & (GROUPS - 1)), 1, 0)) & (lanes - 1)
                for w in range(span)
            ]
            for u in range(GROUPS)
        ]

        for k in (0, 1, 3, 2):
            for j in range(plane):
                i = lax.rem(me // plane + k, GROUPS) * plane + lax.rem(me + j, plane)
                arrived(W.at[i, (parts - 1) - (parts - 2) * core], out_recv.at[0, i]).wait()
            passes(k).start()

        def rotate(field):
            done = [[None] * span for _ in range(GROUPS)]
            for w in range(span):
                near_by = [jnp.where(odd[w], field[u - 1][w], field[u][w]) for u in range(GROUPS)]
                for u in range(GROUPS):
                    chosen = jnp.where(two[w], near_by[u - 2], near_by[u])
                    done[u][w] = jnp.take_along_axis(chosen, source[u][w], axis=1)
            return done

        at = jnp.full((TILE, lanes), place, jnp.int32)
        is_low = at == 0
        is_high = at == 2 * blocks * n_rad - 1
        end_low, end_high = TILE, TILE * (1 + own) - 1

        def replaced(field, at_row, by_row, where):
            w, sub = by_row % span, by_row // span
            mask = jnp.logical_and(where, row == at_row // span)
            for u in range(GROUPS):
                end = jnp.broadcast_to(field[u][w][sub : sub + 1], (TILE, lanes))
                field[u][at_row % span] = jnp.where(mask, end, field[u][at_row % span])

        def edged(field):
            field = [list(tiles_u) for tiles_u in field]
            for k in (1, 2):
                replaced(field, end_low - k, end_low, is_low)
                replaced(field, end_high + k, end_high, is_high)
            return field

        def unpack(pieces):
            return [lane_rows(p, -TILE * g) for g, p in enumerate(exchange(pieces, lane_of[pieces[0].shape[0]]))]

        def settle(slot, count, at_row):
            pieces = [W[i, pl.ds(slot, count)].reshape(count * TILE, lanes) for i in range(n_az)]
            for g, piece in enumerate(unpack(pieces)):
                F[g, pl.ds(pl.multiple_of(at_row, TILE), count * TILE)] = piece

        for q in range(GROUPS):
            passed(q).wait()
        settle((parts - 1) * (1 - core), 2, own * TILE * (1 - core))
        for k in (0, 1, 3, 2):
            for j in range(plane):
                i = lax.rem(me // plane + k, GROUPS) * plane + lax.rem(me + j, plane)
                arrived(W.at[i, pl.ds(2 * core, parts - 1)], out_recv.at[1, i]).wait()
        settle(2, own, 2 * TILE * core)
        pieces = [W[i, pl.ds((parts - 1) * core, 2)].reshape(2 * TILE, lanes) for i in range(n_az)]
        for g, piece in enumerate(unpack(pieces)):
            for t in range(2):
                w, u = GROUPS * t + g // GROUPS, g % GROUPS
                if w < span:
                    F[GROUPS * GROUPS + u, w * TILE : (w + 1) * TILE] = piece[t * TILE : (t + 1) * TILE]

        state = [
            [[F[GROUPS * f + u, pl.ds(w, TILE, stride=span), :] for w in range(span)] for u in range(GROUPS)]
            for f in range(fields)
        ]
        step = advect_all(state)
        state = [edged(rotate(step(field))) for field in state]
        mr, mp, en = push_all(state)
        state = [edged(field) for field in (state[0], mr, mp, state[3], en)]
        step = advect_all(state)
        state = [edged(rotate(step(field))) for field in state]
        mr, mp, en = push_all(state)
        for f, field in enumerate((state[0], mr, mp, state[3], en)):
            for u in range(GROUPS):
                for w in range(span):
                    G[GROUPS * f + u, pl.ds(w, TILE, stride=span), :] = field[u][w]

        mine = slice(TILE, (1 + own) * TILE)
        kept = [lane_rows(G[g, mine], TILE * g) for g in range(GROUPS * GROUPS)]
        for i, piece in enumerate(exchange(kept, lane_of[own * TILE])):
            B[i, : own * TILE] = piece
        kept = [
            lane_rows(G[GROUPS * GROUPS + u, (1 + t) * TILE : (2 + t) * TILE], TILE * (GROUPS * t + u))
            for t in range(own)
            for u in range(GROUPS)
        ]
        for i, piece in enumerate(exchange(kept, lane)):
            B[i, own * TILE :] = piece

        for n in order:
            sent, within, mine = back(n)
            if within is None:
                sent.start()
                continue

            @pl.when(jnp.logical_and(here, mine))
            def _():
                within.start()

            @pl.when(jnp.logical_not(jnp.logical_and(here, mine)))
            def _():
                sent.start()

    for l in range(depth):
        for s in range(blocks):
            for c in range(2):
                arrived(R.at[l, s, c], back_recv.at[(l * blocks + s) * 2 + c]).wait()
        pieces = [R[l, s, c, : own * TILE] for s in range(blocks) for c in range(2)]
        cells = pltpu.roll(jnp.concatenate(pieces, axis=0), unspin, 1).T
        for f in range(GROUPS):
            for u in range(GROUPS):
                g = GROUPS * f + u
                out[f, l, pl.ds(u, TILE, stride=GROUPS), :] = cells[g * TILE : (g + 1) * TILE]
    pieces = []
    for s in range(blocks):
        for c in range(2):
            both = [pltpu.roll(R[l, s, c, own * TILE :], unspin, 1) for l in range(depth)]
            for g in range(GROUPS):
                piece = lane_rows(both[0], -width * g)
                for l in range(1, depth):
                    piece = jnp.where(group == l, lane_rows(both[l], width * (l - g)), piece)
                pieces.append(piece)
    cells = jnp.concatenate(pieces, axis=0).T
    for l in range(depth):
        for u in range(GROUPS):
            g = GROUPS * l + u
            out[4, l, pl.ds(u, TILE, stride=GROUPS), :] = cells[g * TILE : (g + 1) * TILE]

    swap_shift.wait_send()
    for l in range(depth):
        for copy in swaps(l, True):
            copy.wait_send()
    for first in (True, False):
        for index in range(len(targets)):
            sent, within, _ = send(index, first)
            if within is None:
                sent.wait_send()
            else:

                @pl.when(jnp.logical_not(stays))
                def _():
                    sent.wait_send()

    @pl.when(works)
    def _():
        for k in range(GROUPS):
            passes(k).wait_send()
        for n in order:
            sent, within, mine = back(n)
            if within is None:
                sent.wait_send()
                continue

            @pl.when(jnp.logical_not(jnp.logical_and(here, mine)))
            def _():
                sent.wait_send()


def turned_body(mesh, state, shifts):
    n_az, n_rad = mesh.shape["az"], mesh.shape["rad"]
    fields, depth, width, lanes = state.shape
    blocks = n_az // 2 // (depth * n_rad)
    tiles = lanes // TILE
    own = tiles // (2 * blocks)
    vmem = lambda *shape: pltpu.VMEM(shape, jnp.float32)
    dma = pltpu.SemaphoreType.DMA
    tile = (TILE, lanes)
    return pl.pallas_call(
        functools.partial(turned_kernel, n_az, n_rad),
        out_shape=pltpu.VMEM(state.shape, state.dtype),
        in_specs=[pl.BlockSpec(memory_space=pl.ANY)] * 2,
        out_specs=pl.BlockSpec(memory_space=pltpu.VMEM),
        scratch_shapes=[
            vmem(fields, depth, width, lanes),
            vmem(depth, tiles + 2, *tile),
            vmem(depth, tiles // GROUPS + 2, *tile),
            vmem(depth, blocks, 2, own + 3, *tile),
            vmem(n_az, own + 4, *tile),
            pltpu.VMEM((1, lanes), jnp.int32),
            pltpu.VMEM((1, lanes), jnp.int32),
            pltpu.VMEM((2 * lanes + 2 * TILE, lanes), jnp.int32),
            pltpu.VMEM(((own + 2) * TILE, lanes), jnp.int32),
            vmem(GROUPS * fields, (own + 2) * TILE, lanes),
            vmem(GROUPS * fields, (own + 2) * TILE, lanes),
            vmem(n_az, (own + 1) * TILE, lanes),
            vmem(depth, blocks, 2, (own + 1) * TILE, lanes),
            dma((depth,)),
            dma(()),
            dma((2,)),
            dma((4, depth)),
            dma((2, n_az)),
            dma((2, n_az)),
            dma((GROUPS,)),
            dma((GROUPS,)),
            dma((n_az,)),
            dma((n_az,)),
        ],
        compiler_params=pltpu.CompilerParams(collective_id=0, has_side_effects=True),
    )(state, shifts.reshape(1, -1))


def turns(mesh, state):
    n_az, n_rad = mesh.shape["az"], mesh.shape["rad"]
    fields, depth, width, lanes = state.shape
    tiles = lanes // TILE
    return (
        n_rad == 2
        and depth == 2
        and fields == GROUPS + 1
        and width == GROUPS * TILE
        and lanes == n_az * TILE
        and n_az == GROUPS * GROUPS
        and tiles == n_az
        and SMAX <= lanes
    )


def choose(mesh, state, shifts):
    return (turned_body if turns(mesh, state) else body)(mesh, state, shifts)


def solution(mesh):
    in_specs = (P(None, None, "az", "rad"), P("rad"))
    out_specs = P(None, None, "az", "rad")
    return jax.shard_map(
        functools.partial(choose, mesh), mesh=mesh, in_specs=in_specs, out_specs=out_specs, check_vma=False
    )
```

```python
import functools

import jax
import jax.numpy as jnp
from jax import lax
from jax.experimental import pallas as pl
from jax.experimental.pallas import tpu as pltpu
from jax.sharding import PartitionSpec as P

STEPS = 2
SMIN = 4
SMAX = 96
EDGE = 4
TILE = 8

GAMMA_GAS = 1.4
COURANT_RADIAL = 0.15
COURANT_AZIMUTH = 0.15
VISCOSITY_COEF = 1.0


def up(x, axis):
    return pltpu.roll(x, x.shape[axis] - 1, axis)


def down(x, axis):
    return pltpu.roll(x, 1, axis)


def face_speeds(velocity, axis, courant):
    face = (0.5 * courant) * (velocity + up(velocity, axis))
    return jnp.maximum(face, 0.0), jnp.minimum(face, 0.0)


def advect(field, speeds, axis):
    low = field - down(field, axis)
    high = up(low, axis)
    product = low * high
    positive = product > 0
    half = jnp.where(positive, product / jnp.where(positive, low + high, 1.0), 0.0)
    flux = speeds[0] * (field + half) + speeds[1] * up(field - half, axis)
    return flux - down(flux, axis)


def push(pressure, density, speed, axis, courant):
    compress = jnp.minimum(up(speed, axis) - down(speed, axis), 0.0)
    total = pressure + VISCOSITY_COEF * density * compress * compress
    work = total * speed
    scale = -0.5 * courant
    return scale * (up(total, axis) - down(total, axis)), scale * (up(work, axis) - down(work, axis))


def shifted(window, shift_left, rows, longest):
    bits = longest.bit_length()
    x = window
    for bit in reversed(range(bits)):
        stride = 1 << bit
        left = stride - 1
        if stride >= TILE:
            keep = -(-(rows + left) // TILE) * TILE
            chosen = min(keep, x.shape[0] - stride)
            mask = (jnp.broadcast_to(shift_left, (chosen, shift_left.shape[1])) & stride) != 0
            y = jnp.where(mask, x[stride : stride + chosen], x[:chosen])
            x = y if chosen == keep else jnp.concatenate([y, x[chosen:keep]], axis=0)
        else:
            mask = (jnp.broadcast_to(shift_left, x.shape) & stride) != 0
            x = jnp.where(mask, pltpu.roll(x, x.shape[0] - stride, 0), x)
    return x[:rows]


def kernel(n_az, n_rad, x_in, shifts, out, *scratch):
    (x, load_sem, A, W0, W1, O0, O1, L0, R0, L1, R1, L2, R2, state_send, state_recv, gather_send, gather_recv,
     side_send, side_recv) = scratch
    fields, depth, width, lanes = x.shape
    behind = SMAX + EDGE
    whole = behind // width
    tail = behind % width
    tail_rows = -(-tail // TILE) * TILE
    group = whole + 1
    base = group * width
    first_row = width - tail_rows
    me = lax.axis_index("az")
    place = lax.rem(me, group)
    position = lax.axis_index("rad")

    def az(by):
        return {"az": lax.rem(me + by + n_az, n_az)}

    def member(by):
        return {"az": me - place + lax.rem(place + by + group, group)}

    def rad(by):
        return {"rad": position + by}

    barrier = pltpu.get_barrier_semaphore()
    MESH = pl.DeviceIdType.MESH
    load = pltpu.make_async_copy(x_in, x, load_sem)
    load.start()
    for by in (1, -1, -group):
        pl.semaphore_signal(barrier, inc=1, device_id=az(by), device_id_type=MESH)
    for h in range(1, group):
        pl.semaphore_signal(barrier, inc=1, device_id=member(h), device_id_type=MESH)

    has_left = position > 0
    has_right = position < n_rad - 1

    @pl.when(has_left)
    def _():
        pl.semaphore_signal(barrier, inc=1, device_id=rad(-1), device_id_type=MESH)

    @pl.when(has_right)
    def _():
        pl.semaphore_signal(barrier, inc=1, device_id=rad(1), device_id_type=MESH)

    load.wait()
    A[:, :, TILE : TILE + width, :] = x[...]
    beside_me = (position + n_rad - 1) // n_rad + (2 * n_rad - 2 - position) // n_rad
    pl.semaphore_wait(barrier, group + 2 + beside_me)

    def remote(src, dst, send, recv, where):
        return pltpu.make_async_remote_copy(
            src_ref=src, dst_ref=dst, send_sem=send, recv_sem=recv, device_id=where, device_id_type=MESH
        )

    def ring_copies(z):
        return [
            remote(x.at[:, z, width - TILE : width], A.at[:, z, 0:TILE],
                   state_send.at[0, z], state_recv.at[0, z], az(1)),
            remote(x.at[:, z, 0:TILE], A.at[:, z, TILE + width : 2 * TILE + width],
                   state_send.at[1, z], state_recv.at[1, z], az(-1)),
        ]

    def side_copies(phase, src, left_dst, right_dst, z):
        to_right = remote(src.at[:, z], left_dst.at[:, z], side_send.at[phase, 0, z],
                          side_recv.at[phase, 0, z], rad(1))
        to_left = remote(src.at[:, z], right_dst.at[:, z], side_send.at[phase, 1, z],
                         side_recv.at[phase, 1, z], rad(-1))
        return to_right, to_left

    def start_side(*args):
        to_right, to_left = side_copies(*args)

        @pl.when(has_right)
        def _():
            to_right.start()

        @pl.when(has_left)
        def _():
            to_left.start()

    def await_side(*args):
        to_right, to_left = side_copies(*args)

        @pl.when(has_left)
        def _():
            to_right.wait_recv()

        @pl.when(has_right)
        def _():
            to_left.wait_recv()

    def end_side(*args):
        to_right, to_left = side_copies(*args)

        @pl.when(has_right)
        def _():
            to_right.wait_send()

        @pl.when(has_left)
        def _():
            to_left.wait_send()

    windows = (W0, W1)
    rotated = (O0, O1)
    sides = ((x, L0, R0), (O0, L1, R1), (O1, L2, R2))

    def gather_copies(step, f, z):
        W = windows[step]
        own, back = W.at[f, z, base : base + width], W.at[f, z, 0:width]
        sems = lambda h: (gather_send.at[step, h, f, z], gather_recv.at[step, h, f, z])
        onward = remote(own, back, *sems(0), az(group))
        inside = []
        for h in range(1, group):
            dst = W.at[f, z, base - h * width : base - (h - 1) * width]
            inside.append([remote(src, dst, *sems(h), member(h)) for src in (own, back)])
        return onward, inside

    def send_own(step, f, z):
        onward, inside = gather_copies(step, f, z)
        onward.start()
        for h in range(1, group):

            @pl.when(place + h < group)
            def _():
                inside[h - 1][0].start()

    def pass_on(step, f, z):
        onward, inside = gather_copies(step, f, z)
        onward.wait_recv()
        for h in range(1, group):

            @pl.when(place + h >= group)
            def _():
                inside[h - 1][1].start()

    def edges(own, left, right):
        rows = own.shape[0]
        lane = lax.broadcasted_iota(jnp.int32, (rows, lanes), 1)
        at = jnp.full((rows, lanes), position, jnp.int32)
        left = jnp.where(at == 0, jnp.broadcast_to(own[:, 0:1], own.shape), left)
        right = jnp.where(at == n_rad - 1, jnp.broadcast_to(own[:, lanes - 1 : lanes], own.shape), right)
        return jnp.where(lane < lanes // 2, right, left)

    def wide(own, beside):
        return jnp.concatenate([own, beside], axis=1)

    def hydro(step, z, strip, beside):
        rows = slice(TILE, TILE + width)
        tall = [strip(f) for f in range(fields)]
        az_speeds = face_speeds(tall[2] / tall[0], 0, COURANT_AZIMUTH)
        broad = [wide(tall[f][rows], beside(f, tall[f][rows])) for f in range(fields)]
        rad_speeds = face_speeds(broad[1] / broad[0], 1, COURANT_RADIAL)
        for f in range(fields):
            along = advect(tall[f], az_speeds, 0)[rows]
            across = advect(broad[f], rad_speeds, 1)[:, :lanes]
            windows[step][f, z, base : base + width, :] = tall[f][rows] - along - across
            send_own(step, f, z)

    def viscous(z, state, extended):
        rho, mr, mp, mz, energy = state
        own = slice(None) if extended else slice(0, lanes)
        inverse = 1.0 / rho
        pressure = (GAMMA_GAS - 1.0) * (energy - 0.5 * (mr * mr + mp * mp + mz * mz) * inverse)
        az_m, az_e = push(pressure[:, own], rho[:, own], (mp * inverse)[:, own], 0, COURANT_AZIMUTH)
        rad_m, rad_e = push(pressure, rho, mr * inverse, 1, COURANT_RADIAL)
        return [
            rho[:, own],
            mr[:, own] + rad_m[:, own],
            mp[:, own] + az_m,
            mz[:, own],
            energy[:, own] + az_e + rad_e[:, own],
        ]

    count = width + 2 * EDGE

    for z in range(depth):
        for copy in ring_copies(z):
            copy.start()
    for z in range(depth):
        start_side(0, *sides[0], z)
    for z in range(depth):
        for copy in ring_copies(z):
            copy.wait_recv()
        await_side(0, *sides[0], z)
        hydro(0, z, lambda f: A[f, z], lambda f, own: edges(own, L0[f, z], R0[f, z]))

    for step in range(STEPS):
        for z in range(depth):
            for f in range(fields):
                pass_on(step, f, z)
        O, L, R = sides[step + 1]
        for z in range(depth):
            for f in range(fields):
                for copies in gather_copies(step, f, z)[1]:
                    copies[0].wait_recv()
                start = base - first_row - EDGE
                O[f, z] = shifted(windows[step][f, z, first_row:], start - shifts[...], count, start - SMIN)
            start_side(step + 1, O, L, R, z)
        for z in range(depth):
            await_side(step + 1, O, L, R, z)
            state = [wide(O[f, z], edges(O[f, z], L[f, z], R[f, z])) for f in range(fields)]
            if step == STEPS - 1:
                new = viscous(z, state, False)
                for f in range(fields):
                    out[f, z] = new[f][EDGE : EDGE + width]
            else:
                new = viscous(z, state, True)
                A_rows = slice(TILE - EDGE, TILE - EDGE + count)
                for f in range(fields):
                    A[f, z, A_rows, :] = new[f][:, :lanes]
                hydro(
                    step + 1,
                    z,
                    lambda f: A[f, z],
                    lambda f, own: edges(own, *[new[f][EDGE : EDGE + width, lanes:]] * 2),
                )

    for z in range(depth):
        for copy in ring_copies(z):
            copy.wait_send()
        for phase in range(STEPS + 1):
            end_side(phase, *sides[phase], z)
        for step in range(STEPS):
            for f in range(fields):
                onward, inside = gather_copies(step, f, z)
                onward.wait_send()
                for copies in inside:
                    copies[0].wait_send()


def body(mesh, state, shifts):
    n_az, n_rad = mesh.shape["az"], mesh.shape["rad"]
    fields, depth, width, lanes = state.shape
    behind = SMAX + EDGE
    group = behind // width + 1
    window = (group + 1) * width
    count = width + 2 * EDGE
    vmem = lambda rows: pltpu.VMEM((fields, depth, rows, lanes), jnp.float32)
    dma = pltpu.SemaphoreType.DMA
    return pl.pallas_call(
        functools.partial(kernel, n_az, n_rad),
        out_shape=pltpu.VMEM(state.shape, state.dtype),
        in_specs=[pl.BlockSpec(memory_space=pl.ANY), pl.BlockSpec(memory_space=pltpu.VMEM)],
        out_specs=pl.BlockSpec(memory_space=pltpu.VMEM),
        scratch_shapes=[
            vmem(width),
            dma(()),
            vmem(width + 2 * TILE),
            vmem(window),
            vmem(window),
            vmem(count),
            vmem(count),
            vmem(width),
            vmem(width),
            vmem(count),
            vmem(count),
            vmem(count),
            vmem(count),
            dma((2, depth)),
            dma((2, depth)),
            dma((STEPS, group, fields, depth)),
            dma((STEPS, group, fields, depth)),
            dma((STEPS + 1, 2, depth)),
            dma((STEPS + 1, 2, depth)),
        ],
        compiler_params=pltpu.CompilerParams(collective_id=0, has_side_effects=True),
    )(state, shifts.reshape(1, -1))


GROUPS = 4


def lane_rows(x, shift):
    return pltpu.roll(x, shift % x.shape[1], 1)


def exchange(parts, lane):
    n = len(parts)
    out = [parts[-g % n] for g in range(n)]
    for bit in range(n.bit_length() - 1):
        far = (lane & (TILE << bit)) != 0
        out = [jnp.where(far, out[(g - (1 << bit)) % n], out[g]) for g in range(n)]
    return out


def fold(x, lane, row):
    half = x.shape[1] // 2
    stay = (lane < half) == (row < TILE // 2)
    return jnp.where(stay, x, lane_rows(pltpu.roll(x, TILE // 2, 0), half))


def line(tiles):
    return jnp.concatenate(tiles, axis=0)


def tiles_of(x):
    return [x[g : g + TILE] for g in range(0, x.shape[0], TILE)]


def next_of(x, axis):
    first = x[:TILE]
    return jnp.concatenate([x[TILE:], pltpu.roll(first, first.shape[axis] - 1, axis)], axis=0)


def last_of(x, axis):
    last = x[-TILE:]
    return jnp.concatenate([pltpu.roll(last, 1, axis), x[:-TILE]], axis=0)


def along(field, w):
    return line([field[u][w] for u in range(GROUPS)])


def across(field, u):
    return line(field[u])


def line_speeds(velocity, axis, courant):
    face = (0.5 * courant) * (velocity + next_of(velocity, axis))
    return jnp.maximum(face, 0.0), jnp.minimum(face, 0.0)


def line_advect(field, speeds, axis):
    low = field - last_of(field, axis)
    high = next_of(low, axis)
    product = low * high
    half = jnp.where(product > 0, product / (low + high), 0.0)
    flux = speeds[0] * (field + half) + speeds[1] * next_of(field - half, axis)
    return flux - last_of(flux, axis)


def line_push(pressure, density, speed, axis):
    compress = jnp.minimum(next_of(speed, axis) - last_of(speed, axis), 0.0)
    total = pressure + density * compress * compress
    work = total * speed
    return next_of(total, axis) - last_of(total, axis), next_of(work, axis) - last_of(work, axis)


def advect_all(state):
    rho, mr, mp = state[:3]
    span = len(rho[0])
    inverse = [tiles_of(1.0 / across(rho, u)) for u in range(GROUPS)]
    az_speeds = [line_speeds(along(mp, w) * along(inverse, w), 1, COURANT_AZIMUTH) for w in range(span)]
    rad_speeds = [line_speeds(across(mr, u) * across(inverse, u), 0, COURANT_RADIAL) for u in range(GROUPS)]

    def step(field):
        turned = [along(field, w) for w in range(span)]
        turned = [tiles_of(turned[w] - line_advect(turned[w], az_speeds[w], 1)) for w in range(span)]
        out = []
        for u in range(GROUPS):
            rest = line([turned[w][u] for w in range(span)])
            out.append(tiles_of(rest - line_advect(across(field, u), rad_speeds[u], 0)))
        return out

    return step


def push_all(state):
    scale = -0.5 * COURANT_AZIMUTH
    assert COURANT_RADIAL == COURANT_AZIMUTH
    rho, mr, mp, mz, energy = state
    inverse, pressure, density, new_mr, rest = [], [], [], [], []
    for u in range(GROUPS):
        r, a, b, c, e = (across(f, u) for f in state)
        inv = 1.0 / r
        p = (scale * (GAMMA_GAS - 1.0)) * (e - 0.5 * (a * a + b * b + c * c) * inv)
        d = (scale * VISCOSITY_COEF) * r
        rad_m, rad_e = line_push(p, d, a * inv, 0)
        inverse.append(tiles_of(inv))
        pressure.append(tiles_of(p))
        density.append(tiles_of(d))
        new_mr.append(tiles_of(a + rad_m))
        rest.append(tiles_of(e + rad_e))
    span = len(rho[0])
    new_mp = [[None] * span for _ in range(GROUPS)]
    new_energy = [[None] * span for _ in range(GROUPS)]
    for w in range(span):
        b = along(mp, w)
        az_m, az_e = line_push(along(pressure, w), along(density, w), b * along(inverse, w), 1)
        for u, (m, e) in enumerate(zip(tiles_of(b + az_m), tiles_of(along(rest, w) + az_e))):
            new_mp[u][w], new_energy[u][w] = m, e
    return new_mr, new_mp, new_energy


def turned_kernel(n_az, n_rad, x_in, shifts_in, out, *scratch):
    (x, T4, EP, M, W, shifts, other, SC, AM, F, FE, K, G, B, R, load_sem, table_sem, shift_sem, swap_sem, out_send, out_recv,
     pass_send, pass_recv, back_send, back_recv) = scratch
    fields, depth, width, lanes = x.shape
    plane = n_az // GROUPS
    workers = n_az // 2
    blocks = workers // (depth * n_rad)
    tiles = lanes // TILE
    quads = tiles // GROUPS
    own = tiles // (2 * blocks)
    span = own + 2
    parts = span + 1
    rows = span * TILE
    MESH = pl.DeviceIdType.MESH
    me = lax.axis_index("az")
    core = lax.axis_index("rad")
    half = lax.rem(me // depth, n_rad)
    layer = lax.rem(me, depth)
    block = me // plane - 1
    works = jnp.logical_and(block >= 0, block < blocks)
    place = (half * blocks + block) * 2 + core
    partner = {"rad": 1 - core}
    here = half == core
    stays = jnp.logical_and(works, here)

    def remote(src, dst, send, recv, where):
        return pltpu.make_async_remote_copy(
            src_ref=src, dst_ref=dst, send_sem=send, recv_sem=recv, device_id=where, device_id_type=MESH
        )

    def arrived(dst, recv):
        return pltpu.make_async_copy(dst, dst, recv)

    barrier = pltpu.get_barrier_semaphore()

    @pl.when(works)
    def _():
        for k in range(n_az - 1):
            pl.semaphore_signal(
                barrier, inc=1, device_id={"az": k + (me <= k).astype(jnp.int32), "rad": half}, device_id_type=MESH
            )

    pl.semaphore_signal(barrier, inc=1, device_id=partner, device_id_type=MESH)
    loads = [pltpu.make_async_copy(x_in.at[:, l], x.at[:, l], load_sem.at[l]) for l in range(depth)]
    for load in loads:
        load.start()
    table = pltpu.make_async_copy(shifts_in, shifts, table_sem)
    table.start()

    lane = lax.broadcasted_iota(jnp.int32, (TILE, lanes), 1)
    row = lax.broadcasted_iota(jnp.int32, (TILE, lanes), 0)
    lane_of = {n * TILE: lax.broadcasted_iota(jnp.int32, (n * TILE, lanes), 1) for n in (1, 2, own)}
    group = lane // width
    spin = me * TILE
    unspin = lax.rem(lanes - spin, lanes)

    def rows_of(f, l):
        return [x[f, l, pl.ds(u, width // GROUPS, stride=GROUPS), :] for u in range(GROUPS)]

    for l in range(depth):
        loads[l].wait()
        cells = jnp.concatenate([part for f in range(GROUPS) for part in rows_of(f, l)], axis=0)
        T4[l, 1 : tiles + 1] = pltpu.roll(cells.T, spin, 1).reshape(tiles, TILE, lanes)
    energy = [part for l in range(depth) for part in rows_of(4, l)]
    turned = jnp.concatenate(energy * (lanes // (depth * width)), axis=0).T.reshape(tiles, TILE, lanes)
    for l in range(depth):
        for m in range(quads):
            packed = turned[GROUPS * m] if l == 0 else lane_rows(turned[GROUPS * m], -width * l)
            for g in range(1, GROUPS):
                packed = jnp.where(group == g, lane_rows(turned[GROUPS * m + g], width * (g - l)), packed)
            EP[l, 1 + m] = packed

    @pl.when(core == 0)
    def _():
        for l in range(depth):
            T4[l, 0] = jnp.broadcast_to(T4[l, 1, 0:1], (TILE, lanes))
            EP[l, 0] = jnp.broadcast_to(lane_rows(EP[l, 1], -width)[0:1], (TILE, lanes))

    @pl.when(core == 1)
    def _():
        for l in range(depth):
            T4[l, tiles + 1] = jnp.broadcast_to(T4[l, tiles, TILE - 1 : TILE], (TILE, lanes))
            EP[l, quads + 1] = jnp.broadcast_to(lane_rows(EP[l, quads], width)[TILE - 1 : TILE], (TILE, lanes))

    def energy_of(l, m):
        joined = jnp.where(group == GROUPS - 1, EP[l, m], EP[l, m + 1])
        return pltpu.roll(joined, lax.rem(spin + width, lanes), 1)

    def stage(l, s, c):
        first = 2 * own * s + c * (own + 1)
        if c == 0:
            M[l, s, c, 0], M[l, s, c, 1] = energy_of(l, 2 * s), energy_of(l, 2 * s + 1)
            M[l, s, c, 2 : own + 2] = T4[l, first : first + own]
        else:
            M[l, s, c, 1 : own + 1] = T4[l, first + 1 : first + own + 1]
            M[l, s, c, own + 1], M[l, s, c, own + 2] = energy_of(l, 2 * s + 1), energy_of(l, 2 * s + 2)

    late = ((0, 0), (blocks - 1, 1))
    for l in range(depth):
        for s in range(blocks):
            for c in range(2):
                M[l, s, c, (parts - 1) * (1 - c)] = T4[l, 2 * own * s + own + c]
                if (s, c) not in late:
                    stage(l, s, c)

    table.wait()
    pl.semaphore_wait(barrier, jnp.where(stays, 2 * (workers // n_rad) - 1, 2 * (workers // n_rad) + 1))

    targets = [(ks, kl, kc) for ks in (0, 1) for kl in (1, 0) for kc in (0, 1)]

    def send(index, first):
        ks, kl, kc = targets[index]
        s = lax.rem(me // plane + 1 + ks, blocks)
        l = lax.rem(layer + kl, depth)
        c = lax.rem(core + kc, 2)
        if first:
            src, dst = M.at[l, s, c, (parts - 1) * (1 - c)], W.at[me, (parts - 1) - (parts - 2) * c]
            sems = out_send.at[0, index], out_recv.at[0, me]
        else:
            src, dst = M.at[l, s, c, pl.ds(c, parts - 1)], W.at[me, pl.ds(2 * c, parts - 1)]
            sems = out_send.at[1, index], out_recv.at[1, me]
        sent = remote(src, dst, *sems, {"az": (1 + s) * plane + core * depth + l, "rad": c})
        is_late = s == c * (blocks - 1)
        return sent, None if ks or kl or kc else pltpu.make_async_copy(src, dst, sems[1]), is_late

    def start(first, when=None):
        for index in range(len(targets)):
            sent, within, is_late = send(index, first)
            if within is None and when is None:
                sent.start()
                continue
            now = True if when is None else when(is_late)
            for copy, also in ((sent, None),) if within is None else ((within, stays), (sent, jnp.logical_not(stays))):

                @pl.when(now if also is None else jnp.logical_and(now, also))
                def _():
                    copy.start()

    start(True)

    swap_shift = remote(shifts, other, shift_sem.at[0], shift_sem.at[1], partner)
    swap_shift.start()

    def swaps(l, up):
        src = (tiles, quads) if up else (1, 1)
        dst = (0, 0) if up else (tiles + 1, quads + 1)
        return [
            remote(T4.at[l, src[0]], T4.at[l, dst[0]], swap_sem.at[0, l], swap_sem.at[1, l], partner),
            remote(EP.at[l, src[1]], EP.at[l, dst[1]], swap_sem.at[2, l], swap_sem.at[3, l], partner),
        ]

    @pl.when(core == 0)
    def _():
        for l in range(depth):
            for copy in swaps(l, True):
                copy.start()

    @pl.when(core == 1)
    def _():
        for l in range(depth):
            for copy in swaps(l, False):
                copy.start()

    start(False, jnp.logical_not)
    for l in range(depth):
        for copy in swaps(l, True):
            copy.wait_recv()
    for l in range(depth):
        for s, c in late:
            stage(l, s, c)
    start(False, lambda is_late: is_late)
    swap_shift.wait_recv()

    def passes(k):
        q = lax.rem(me // plane + k, GROUPS)
        ahead = pl.ds(q * plane, plane)
        src, dst = W.at[ahead, (parts - 1) - (parts - 2) * core], W.at[ahead, parts * core]
        return remote(src, dst, pass_send.at[k], pass_recv.at[q], partner)

    def passed(q):
        return arrived(W.at[pl.ds(q * plane, plane), parts * (1 - core)], pass_recv.at[q])

    order = range(n_az)

    def back(n):
        if n == 0:
            i = 0
        elif n < plane:
            i = 1 + lax.rem(me + n - 1, plane - 1)
        elif n < 2 * plane:
            i = plane + lax.rem(me + n + 1, plane)
        else:
            i = 2 * plane + lax.rem(me + n + 1, 2 * plane)
        src, dst = B.at[i], R.at[layer, block, core]
        sems = back_send.at[n], back_recv.at[(layer * blocks + block) * 2 + core]
        sent = remote(src, dst, *sems, {"az": i, "rad": half})
        return sent, pltpu.make_async_copy(src, dst, sems[1]) if n in (2 * plane - 1, n_az - 1) else None, me == i

    @pl.when(works)
    def _():
        lower = jnp.full((1, lanes), core, jnp.int32) == 0
        mine, theirs = shifts[...], other[...]
        for c in range(2):
            part = jnp.where(lower, mine if c == 0 else theirs, theirs if c == 0 else mine)
            along_lanes = jnp.broadcast_to(part.astype(jnp.float32), (lanes, lanes)).T.astype(jnp.int32)
            SC[TILE + c * lanes : TILE + (c + 1) * lanes] = along_lanes
        SC[0:TILE] = jnp.zeros((TILE, lanes), jnp.int32)
        SC[TILE + 2 * lanes :] = jnp.zeros((TILE, lanes), jnp.int32)
        AM[...] = SC[pl.ds(pl.multiple_of(place * own * TILE, TILE), rows)]
        at = jnp.full((TILE, lanes), place, jnp.int32)
        is_low = at == 0
        is_high = at == 2 * blocks * n_rad - 1

        def tools_of(span, start):
            amounts = [AM[pl.ds(start + w, TILE, stride=span), :] for w in range(span)]
            odd = [(amount & 1) != 0 for amount in amounts]
            two = [(amount & 2) != 0 for amount in amounts]
            source = [
                [
                    (lane - amounts[w] // GROUPS - jnp.where(u < (amounts[w] & (GROUPS - 1)), 1, 0)) & (lanes - 1)
                    for w in range(span)
                ]
                for u in range(GROUPS)
            ]

            def rotate(field):
                done = [[None] * span for _ in range(GROUPS)]
                for w in range(span):
                    near_by = [jnp.where(odd[w], field[u - 1][w], field[u][w]) for u in range(GROUPS)]
                    for u in range(GROUPS):
                        chosen = jnp.where(two[w], near_by[u - 2], near_by[u])
                        done[u][w] = jnp.take_along_axis(chosen, source[u][w], axis=1)
                return done

            end_low, end_high = TILE - start, TILE * (1 + own) - 1 - start

            def replaced(field, at_row, by_row, where):
                w, sub = by_row % span, by_row // span
                mask = jnp.logical_and(where, row == at_row // span)
                for u in range(GROUPS):
                    end = jnp.broadcast_to(field[u][w][sub : sub + 1], (TILE, lanes))
                    field[u][at_row % span] = jnp.where(mask, end, field[u][at_row % span])

            def edged(field):
                field = [list(tiles_u) for tiles_u in field]
                for k in (1, 2):
                    replaced(field, end_low - k, end_low, is_low)
                    replaced(field, end_high + k, end_high, is_high)
                return field

            return rotate, edged

        rotate, edged = tools_of(span, 0)
        rotate_core, edged_core = tools_of(span - 1, GROUPS)

        for k in (0, 1, 3, 2):
            for j in range(plane):
                i = lax.rem(me // plane + k, GROUPS) * plane + lax.rem(me + j, plane)
                arrived(W.at[i, (parts - 1) - (parts - 2) * core], out_recv.at[0, i]).wait()
            passes(k).start()

        def unpack(pieces):
            return [lane_rows(p, -TILE * g) for g, p in enumerate(exchange(pieces, lane_of[pieces[0].shape[0]]))]

        def settle(slot, count, at_row):
            pieces = [W[i, pl.ds(slot, count)].reshape(count * TILE, lanes) for i in range(n_az)]
            for g, piece in enumerate(unpack(pieces)):
                F[g, pl.ds(pl.multiple_of(at_row, TILE), count * TILE)] = piece

        for q in range(GROUPS):
            passed(q).wait()
        settle((parts - 1) * (1 - core), 2, own * TILE * (1 - core))
        for k in (0, 1, 3, 2):
            for j in range(plane):
                i = lax.rem(me // plane + k, GROUPS) * plane + lax.rem(me + j, plane)
                arrived(W.at[i, pl.ds(2 * core, parts - 1)], out_recv.at[1, i]).wait()
        settle(2, own, 2 * TILE * core)
        pieces = [W[i, pl.ds((parts - 1) * core, 2)].reshape(2 * TILE, lanes) for i in range(n_az)]
        for g, piece in enumerate(unpack(pieces)):
            for t in range(2):
                w, u = GROUPS * t + g // GROUPS, g % GROUPS
                if w < span:
                    FE[u, w * TILE : (w + 1) * TILE] = piece[t * TILE : (t + 1) * TILE]

        def source_of(f, u):
            return FE.at[u] if f == GROUPS else F.at[GROUPS * f + u]

        state = [
            [[source_of(f, u)[pl.ds(w, TILE, stride=span), :] for w in range(span)] for u in range(GROUPS)]
            for f in range(fields)
        ]
        step = advect_all(state)
        state = [edged(rotate(step(field))) for field in state]
        mr, mp, en = push_all(state)
        for f, field in enumerate((state[0], mr, mp, state[3], en)):
            for u in range(GROUPS):
                for w in range(span):
                    K[GROUPS * f + u, pl.ds(w, TILE, stride=span), :] = field[u][w]

        inner = range(span - 1)
        state = [
            edged_core(
                [
                    [K[GROUPS * f + u, pl.ds(GROUPS + w, TILE, stride=span - 1), :] for w in inner]
                    for u in range(GROUPS)
                ]
            )
            for f in range(fields)
        ]
        step = advect_all(state)
        state = [edged_core(rotate_core(step(field))) for field in state]
        mr, mp, en = push_all(state)
        for f, field in enumerate((state[0], mr, mp, state[3], en)):
            for u in range(GROUPS):
                for w in inner:
                    G[GROUPS * f + u, pl.ds(GROUPS + w, TILE, stride=span - 1), :] = field[u][w]

        mine = slice(TILE, (1 + own) * TILE)
        kept = [lane_rows(G[g, mine], TILE * g) for g in range(GROUPS * GROUPS)]
        for i, piece in enumerate(exchange(kept, lane_of[own * TILE])):
            B[i, : own * TILE] = piece
        kept = [
            lane_rows(G[GROUPS * GROUPS + u, (1 + t) * TILE : (2 + t) * TILE], TILE * (GROUPS * t + u))
            for t in range(own)
            for u in range(GROUPS)
        ]
        for i, piece in enumerate(exchange(kept, lane)):
            B[i, own * TILE :] = piece

        for n in order:
            sent, within, mine = back(n)
            if within is None:
                sent.start()
                continue

            @pl.when(jnp.logical_and(here, mine))
            def _():
                within.start()

            @pl.when(jnp.logical_not(jnp.logical_and(here, mine)))
            def _():
                sent.start()

    for l in range(depth):
        for s in range(blocks):
            for c in range(2):
                arrived(R.at[l, s, c], back_recv.at[(l * blocks + s) * 2 + c]).wait()
        pieces = [R[l, s, c, : own * TILE] for s in range(blocks) for c in range(2)]
        cells = pltpu.roll(jnp.concatenate(pieces, axis=0), unspin, 1).T
        for f in range(GROUPS):
            for u in range(GROUPS):
                g = GROUPS * f + u
                out[f, l, pl.ds(u, TILE, stride=GROUPS), :] = cells[g * TILE : (g + 1) * TILE]
    pieces = []
    for s in range(blocks):
        for c in range(2):
            both = [pltpu.roll(R[l, s, c, own * TILE :], unspin, 1) for l in range(depth)]
            for g in range(GROUPS):
                piece = lane_rows(both[0], -width * g)
                for l in range(1, depth):
                    piece = jnp.where(group == l, lane_rows(both[l], width * (l - g)), piece)
                pieces.append(piece)
    cells = jnp.concatenate(pieces, axis=0).T
    for l in range(depth):
        for u in range(GROUPS):
            g = GROUPS * l + u
            out[4, l, pl.ds(u, TILE, stride=GROUPS), :] = cells[g * TILE : (g + 1) * TILE]

    swap_shift.wait_send()
    for l in range(depth):
        for copy in swaps(l, True):
            copy.wait_send()
    for first in (True, False):
        for index in range(len(targets)):
            sent, within, _ = send(index, first)
            if within is None:
                sent.wait_send()
            else:

                @pl.when(jnp.logical_not(stays))
                def _():
                    sent.wait_send()

    @pl.when(works)
    def _():
        for k in range(GROUPS):
            passes(k).wait_send()
        for n in order:
            sent, within, mine = back(n)
            if within is None:
                sent.wait_send()
                continue

            @pl.when(jnp.logical_not(jnp.logical_and(here, mine)))
            def _():
                sent.wait_send()


def turned_body(mesh, state, shifts):
    n_az, n_rad = mesh.shape["az"], mesh.shape["rad"]
    fields, depth, width, lanes = state.shape
    blocks = n_az // 2 // (depth * n_rad)
    tiles = lanes // TILE
    own = tiles // (2 * blocks)
    vmem = lambda *shape: pltpu.VMEM(shape, jnp.float32)
    dma = pltpu.SemaphoreType.DMA
    tile = (TILE, lanes)
    return pl.pallas_call(
        functools.partial(turned_kernel, n_az, n_rad),
        out_shape=pltpu.VMEM(state.shape, state.dtype),
        in_specs=[pl.BlockSpec(memory_space=pl.ANY)] * 2,
        out_specs=pl.BlockSpec(memory_space=pltpu.VMEM),
        scratch_shapes=[
            vmem(fields, depth, width, lanes),
            vmem(depth, tiles + 2, *tile),
            vmem(depth, tiles // GROUPS + 2, *tile),
            vmem(depth, blocks, 2, own + 3, *tile),
            vmem(n_az, own + 4, *tile),
            pltpu.VMEM((1, lanes), jnp.int32),
            pltpu.VMEM((1, lanes), jnp.int32),
            pltpu.VMEM((2 * lanes + 2 * TILE, lanes), jnp.int32),
            pltpu.VMEM(((own + 2) * TILE, lanes), jnp.int32),
            vmem(GROUPS * GROUPS, (own + 2) * TILE, lanes),
            vmem(GROUPS, (own + 2) * TILE, lanes),
            vmem(GROUPS * fields, (own + 2) * TILE, lanes),
            vmem(GROUPS * fields, (own + 2) * TILE, lanes),
            vmem(n_az, (own + 1) * TILE, lanes),
            vmem(depth, blocks, 2, (own + 1) * TILE, lanes),
            dma((depth,)),
            dma(()),
            dma((2,)),
            dma((4, depth)),
            dma((2, n_az)),
            dma((2, n_az)),
            dma((GROUPS,)),
            dma((GROUPS,)),
            dma((n_az,)),
            dma((n_az,)),
        ],
        compiler_params=pltpu.CompilerParams(collective_id=0, has_side_effects=True),
    )(state, shifts.reshape(1, -1))


def turns(mesh, state):
    n_az, n_rad = mesh.shape["az"], mesh.shape["rad"]
    fields, depth, width, lanes = state.shape
    tiles = lanes // TILE
    return (
        n_rad == 2
        and depth == 2
        and fields == GROUPS + 1
        and width == GROUPS * TILE
        and lanes == n_az * TILE
        and n_az == GROUPS * GROUPS
        and tiles == n_az
        and SMAX <= lanes
    )


def choose(mesh, state, shifts):
    return (turned_body if turns(mesh, state) else body)(mesh, state, shifts)


def solution(mesh):
    in_specs = (P(None, None, "az", "rad"), P("rad"))
    out_specs = P(None, None, "az", "rad")
    return jax.shard_map(
        functools.partial(choose, mesh), mesh=mesh, in_specs=in_specs, out_specs=out_specs, check_vma=False
    )
```

```python
import functools

import jax
import jax.numpy as jnp
from jax import lax
from jax.experimental import pallas as pl
from jax.experimental.pallas import tpu as pltpu
from jax.sharding import PartitionSpec as P

STEPS = 2
SMIN = 4
SMAX = 96
EDGE = 4
TILE = 8

GAMMA_GAS = 1.4
COURANT_RADIAL = 0.15
COURANT_AZIMUTH = 0.15
VISCOSITY_COEF = 1.0


def up(x, axis):
    return pltpu.roll(x, x.shape[axis] - 1, axis)


def down(x, axis):
    return pltpu.roll(x, 1, axis)


def face_speeds(velocity, axis, courant):
    face = (0.5 * courant) * (velocity + up(velocity, axis))
    return jnp.maximum(face, 0.0), jnp.minimum(face, 0.0)


def advect(field, speeds, axis):
    low = field - down(field, axis)
    high = up(low, axis)
    product = low * high
    positive = product > 0
    half = jnp.where(positive, product / jnp.where(positive, low + high, 1.0), 0.0)
    flux = speeds[0] * (field + half) + speeds[1] * up(field - half, axis)
    return flux - down(flux, axis)


def push(pressure, density, speed, axis, courant):
    compress = jnp.minimum(up(speed, axis) - down(speed, axis), 0.0)
    total = pressure + VISCOSITY_COEF * density * compress * compress
    work = total * speed
    scale = -0.5 * courant
    return scale * (up(total, axis) - down(total, axis)), scale * (up(work, axis) - down(work, axis))


def shifted(window, shift_left, rows, longest):
    bits = longest.bit_length()
    x = window
    for bit in reversed(range(bits)):
        stride = 1 << bit
        left = stride - 1
        if stride >= TILE:
            keep = -(-(rows + left) // TILE) * TILE
            chosen = min(keep, x.shape[0] - stride)
            mask = (jnp.broadcast_to(shift_left, (chosen, shift_left.shape[1])) & stride) != 0
            y = jnp.where(mask, x[stride : stride + chosen], x[:chosen])
            x = y if chosen == keep else jnp.concatenate([y, x[chosen:keep]], axis=0)
        else:
            mask = (jnp.broadcast_to(shift_left, x.shape) & stride) != 0
            x = jnp.where(mask, pltpu.roll(x, x.shape[0] - stride, 0), x)
    return x[:rows]


def kernel(n_az, n_rad, x_in, shifts, out, *scratch):
    (x, load_sem, A, W0, W1, O0, O1, L0, R0, L1, R1, L2, R2, state_send, state_recv, gather_send, gather_recv,
     side_send, side_recv) = scratch
    fields, depth, width, lanes = x.shape
    behind = SMAX + EDGE
    whole = behind // width
    tail = behind % width
    tail_rows = -(-tail // TILE) * TILE
    group = whole + 1
    base = group * width
    first_row = width - tail_rows
    me = lax.axis_index("az")
    place = lax.rem(me, group)
    position = lax.axis_index("rad")

    def az(by):
        return {"az": lax.rem(me + by + n_az, n_az)}

    def member(by):
        return {"az": me - place + lax.rem(place + by + group, group)}

    def rad(by):
        return {"rad": position + by}

    barrier = pltpu.get_barrier_semaphore()
    MESH = pl.DeviceIdType.MESH
    load = pltpu.make_async_copy(x_in, x, load_sem)
    load.start()
    for by in (1, -1, -group):
        pl.semaphore_signal(barrier, inc=1, device_id=az(by), device_id_type=MESH)
    for h in range(1, group):
        pl.semaphore_signal(barrier, inc=1, device_id=member(h), device_id_type=MESH)

    has_left = position > 0
    has_right = position < n_rad - 1

    @pl.when(has_left)
    def _():
        pl.semaphore_signal(barrier, inc=1, device_id=rad(-1), device_id_type=MESH)

    @pl.when(has_right)
    def _():
        pl.semaphore_signal(barrier, inc=1, device_id=rad(1), device_id_type=MESH)

    load.wait()
    A[:, :, TILE : TILE + width, :] = x[...]
    beside_me = (position + n_rad - 1) // n_rad + (2 * n_rad - 2 - position) // n_rad
    pl.semaphore_wait(barrier, group + 2 + beside_me)

    def remote(src, dst, send, recv, where):
        return pltpu.make_async_remote_copy(
            src_ref=src, dst_ref=dst, send_sem=send, recv_sem=recv, device_id=where, device_id_type=MESH
        )

    def ring_copies(z):
        return [
            remote(x.at[:, z, width - TILE : width], A.at[:, z, 0:TILE],
                   state_send.at[0, z], state_recv.at[0, z], az(1)),
            remote(x.at[:, z, 0:TILE], A.at[:, z, TILE + width : 2 * TILE + width],
                   state_send.at[1, z], state_recv.at[1, z], az(-1)),
        ]

    def side_copies(phase, src, left_dst, right_dst, z):
        to_right = remote(src.at[:, z], left_dst.at[:, z], side_send.at[phase, 0, z],
                          side_recv.at[phase, 0, z], rad(1))
        to_left = remote(src.at[:, z], right_dst.at[:, z], side_send.at[phase, 1, z],
                         side_recv.at[phase, 1, z], rad(-1))
        return to_right, to_left

    def start_side(*args):
        to_right, to_left = side_copies(*args)

        @pl.when(has_right)
        def _():
            to_right.start()

        @pl.when(has_left)
        def _():
            to_left.start()

    def await_side(*args):
        to_right, to_left = side_copies(*args)

        @pl.when(has_left)
        def _():
            to_right.wait_recv()

        @pl.when(has_right)
        def _():
            to_left.wait_recv()

    def end_side(*args):
        to_right, to_left = side_copies(*args)

        @pl.when(has_right)
        def _():
            to_right.wait_send()

        @pl.when(has_left)
        def _():
            to_left.wait_send()

    windows = (W0, W1)
    rotated = (O0, O1)
    sides = ((x, L0, R0), (O0, L1, R1), (O1, L2, R2))

    def gather_copies(step, f, z):
        W = windows[step]
        own, back = W.at[f, z, base : base + width], W.at[f, z, 0:width]
        sems = lambda h: (gather_send.at[step, h, f, z], gather_recv.at[step, h, f, z])
        onward = remote(own, back, *sems(0), az(group))
        inside = []
        for h in range(1, group):
            dst = W.at[f, z, base - h * width : base - (h - 1) * width]
            inside.append([remote(src, dst, *sems(h), member(h)) for src in (own, back)])
        return onward, inside

    def send_own(step, f, z):
        onward, inside = gather_copies(step, f, z)
        onward.start()
        for h in range(1, group):

            @pl.when(place + h < group)
            def _():
                inside[h - 1][0].start()

    def pass_on(step, f, z):
        onward, inside = gather_copies(step, f, z)
        onward.wait_recv()
        for h in range(1, group):

            @pl.when(place + h >= group)
            def _():
                inside[h - 1][1].start()

    def edges(own, left, right):
        rows = own.shape[0]
        lane = lax.broadcasted_iota(jnp.int32, (rows, lanes), 1)
        at = jnp.full((rows, lanes), position, jnp.int32)
        left = jnp.where(at == 0, jnp.broadcast_to(own[:, 0:1], own.shape), left)
        right = jnp.where(at == n_rad - 1, jnp.broadcast_to(own[:, lanes - 1 : lanes], own.shape), right)
        return jnp.where(lane < lanes // 2, right, left)

    def wide(own, beside):
        return jnp.concatenate([own, beside], axis=1)

    def hydro(step, z, strip, beside):
        rows = slice(TILE, TILE + width)
        tall = [strip(f) for f in range(fields)]
        az_speeds = face_speeds(tall[2] / tall[0], 0, COURANT_AZIMUTH)
        broad = [wide(tall[f][rows], beside(f, tall[f][rows])) for f in range(fields)]
        rad_speeds = face_speeds(broad[1] / broad[0], 1, COURANT_RADIAL)
        for f in range(fields):
            along = advect(tall[f], az_speeds, 0)[rows]
            across = advect(broad[f], rad_speeds, 1)[:, :lanes]
            windows[step][f, z, base : base + width, :] = tall[f][rows] - along - across
            send_own(step, f, z)

    def viscous(z, state, extended):
        rho, mr, mp, mz, energy = state
        own = slice(None) if extended else slice(0, lanes)
        inverse = 1.0 / rho
        pressure = (GAMMA_GAS - 1.0) * (energy - 0.5 * (mr * mr + mp * mp + mz * mz) * inverse)
        az_m, az_e = push(pressure[:, own], rho[:, own], (mp * inverse)[:, own], 0, COURANT_AZIMUTH)
        rad_m, rad_e = push(pressure, rho, mr * inverse, 1, COURANT_RADIAL)
        return [
            rho[:, own],
            mr[:, own] + rad_m[:, own],
            mp[:, own] + az_m,
            mz[:, own],
            energy[:, own] + az_e + rad_e[:, own],
        ]

    count = width + 2 * EDGE

    for z in range(depth):
        for copy in ring_copies(z):
            copy.start()
    for z in range(depth):
        start_side(0, *sides[0], z)
    for z in range(depth):
        for copy in ring_copies(z):
            copy.wait_recv()
        await_side(0, *sides[0], z)
        hydro(0, z, lambda f: A[f, z], lambda f, own: edges(own, L0[f, z], R0[f, z]))

    for step in range(STEPS):
        for z in range(depth):
            for f in range(fields):
                pass_on(step, f, z)
        O, L, R = sides[step + 1]
        for z in range(depth):
            for f in range(fields):
                for copies in gather_copies(step, f, z)[1]:
                    copies[0].wait_recv()
                start = base - first_row - EDGE
                O[f, z] = shifted(windows[step][f, z, first_row:], start - shifts[...], count, start - SMIN)
            start_side(step + 1, O, L, R, z)
        for z in range(depth):
            await_side(step + 1, O, L, R, z)
            state = [wide(O[f, z], edges(O[f, z], L[f, z], R[f, z])) for f in range(fields)]
            if step == STEPS - 1:
                new = viscous(z, state, False)
                for f in range(fields):
                    out[f, z] = new[f][EDGE : EDGE + width]
            else:
                new = viscous(z, state, True)
                A_rows = slice(TILE - EDGE, TILE - EDGE + count)
                for f in range(fields):
                    A[f, z, A_rows, :] = new[f][:, :lanes]
                hydro(
                    step + 1,
                    z,
                    lambda f: A[f, z],
                    lambda f, own: edges(own, *[new[f][EDGE : EDGE + width, lanes:]] * 2),
                )

    for z in range(depth):
        for copy in ring_copies(z):
            copy.wait_send()
        for phase in range(STEPS + 1):
            end_side(phase, *sides[phase], z)
        for step in range(STEPS):
            for f in range(fields):
                onward, inside = gather_copies(step, f, z)
                onward.wait_send()
                for copies in inside:
                    copies[0].wait_send()


def body(mesh, state, shifts):
    n_az, n_rad = mesh.shape["az"], mesh.shape["rad"]
    fields, depth, width, lanes = state.shape
    behind = SMAX + EDGE
    group = behind // width + 1
    window = (group + 1) * width
    count = width + 2 * EDGE
    vmem = lambda rows: pltpu.VMEM((fields, depth, rows, lanes), jnp.float32)
    dma = pltpu.SemaphoreType.DMA
    return pl.pallas_call(
        functools.partial(kernel, n_az, n_rad),
        out_shape=pltpu.VMEM(state.shape, state.dtype),
        in_specs=[pl.BlockSpec(memory_space=pl.ANY), pl.BlockSpec(memory_space=pltpu.VMEM)],
        out_specs=pl.BlockSpec(memory_space=pltpu.VMEM),
        scratch_shapes=[
            vmem(width),
            dma(()),
            vmem(width + 2 * TILE),
            vmem(window),
            vmem(window),
            vmem(count),
            vmem(count),
            vmem(width),
            vmem(width),
            vmem(count),
            vmem(count),
            vmem(count),
            vmem(count),
            dma((2, depth)),
            dma((2, depth)),
            dma((STEPS, group, fields, depth)),
            dma((STEPS, group, fields, depth)),
            dma((STEPS + 1, 2, depth)),
            dma((STEPS + 1, 2, depth)),
        ],
        compiler_params=pltpu.CompilerParams(collective_id=0, has_side_effects=True),
    )(state, shifts.reshape(1, -1))


GROUPS = 4


def lane_rows(x, shift):
    return pltpu.roll(x, shift % x.shape[1], 1)


def exchange(parts, lane):
    n = len(parts)
    out = [parts[-g % n] for g in range(n)]
    for bit in range(n.bit_length() - 1):
        far = (lane & (TILE << bit)) != 0
        out = [jnp.where(far, out[(g - (1 << bit)) % n], out[g]) for g in range(n)]
    return out


def fold(x, lane, row):
    half = x.shape[1] // 2
    stay = (lane < half) == (row < TILE // 2)
    return jnp.where(stay, x, lane_rows(pltpu.roll(x, TILE // 2, 0), half))


def line(tiles):
    return jnp.concatenate(tiles, axis=0)


def tiles_of(x):
    return [x[g : g + TILE] for g in range(0, x.shape[0], TILE)]


def next_of(x, axis):
    first = x[:TILE]
    return jnp.concatenate([x[TILE:], pltpu.roll(first, first.shape[axis] - 1, axis)], axis=0)


def last_of(x, axis):
    last = x[-TILE:]
    return jnp.concatenate([pltpu.roll(last, 1, axis), x[:-TILE]], axis=0)


def along(field, w):
    return line([field[u][w] for u in range(GROUPS)])


def across(field, u):
    return line(field[u])


def line_speeds(velocity, axis, courant):
    face = (0.5 * courant) * (velocity + next_of(velocity, axis))
    return face, face > 0


def line_advect(field, speeds, axis):
    low = field - last_of(field, axis)
    high = next_of(low, axis)
    product = low * high
    half = jnp.where(product > 0, product / (low + high), 0.0)
    flux = speeds[0] * jnp.where(speeds[1], field + half, next_of(field - half, axis))
    return flux - last_of(flux, axis)


def line_push(pressure, density, speed, axis):
    compress = jnp.minimum(next_of(speed, axis) - last_of(speed, axis), 0.0)
    total = pressure + density * compress * compress
    work = total * speed
    return next_of(total, axis) - last_of(total, axis), next_of(work, axis) - last_of(work, axis)


def advect_all(state):
    rho, mr, mp = state[:3]
    span = len(rho[0])
    inverse = [tiles_of(1.0 / across(rho, u)) for u in range(GROUPS)]
    az_speeds = [line_speeds(along(mp, w) * along(inverse, w), 1, COURANT_AZIMUTH) for w in range(span)]
    rad_speeds = [line_speeds(across(mr, u) * across(inverse, u), 0, COURANT_RADIAL) for u in range(GROUPS)]

    def step(field):
        turned = [along(field, w) for w in range(span)]
        turned = [tiles_of(turned[w] - line_advect(turned[w], az_speeds[w], 1)) for w in range(span)]
        out = []
        for u in range(GROUPS):
            rest = line([turned[w][u] for w in range(span)])
            out.append(tiles_of(rest - line_advect(across(field, u), rad_speeds[u], 0)))
        return out

    return step


def push_all(state):
    scale = -0.5 * COURANT_AZIMUTH
    assert COURANT_RADIAL == COURANT_AZIMUTH
    rho, mr, mp, mz, energy = state
    inverse, pressure, density, new_mr, rest = [], [], [], [], []
    for u in range(GROUPS):
        r, a, b, c, e = (across(f, u) for f in state)
        inv = 1.0 / r
        p = (scale * (GAMMA_GAS - 1.0)) * (e - 0.5 * (a * a + b * b + c * c) * inv)
        d = (scale * VISCOSITY_COEF) * r
        rad_m, rad_e = line_push(p, d, a * inv, 0)
        inverse.append(tiles_of(inv))
        pressure.append(tiles_of(p))
        density.append(tiles_of(d))
        new_mr.append(tiles_of(a + rad_m))
        rest.append(tiles_of(e + rad_e))
    span = len(rho[0])
    new_mp = [[None] * span for _ in range(GROUPS)]
    new_energy = [[None] * span for _ in range(GROUPS)]
    for w in range(span):
        b = along(mp, w)
        az_m, az_e = line_push(along(pressure, w), along(density, w), b * along(inverse, w), 1)
        for u, (m, e) in enumerate(zip(tiles_of(b + az_m), tiles_of(along(rest, w) + az_e))):
            new_mp[u][w], new_energy[u][w] = m, e
    return new_mr, new_mp, new_energy


def turned_kernel(n_az, n_rad, x_in, shifts_in, out, *scratch):
    (x, T4, EP, M, W, shifts, other, SC, AM, F, FE, K, G, B, R, load_sem, table_sem, shift_sem, swap_sem, out_send, out_recv,
     pass_send, pass_recv, back_send, back_recv) = scratch
    fields, depth, width, lanes = x.shape
    plane = n_az // GROUPS
    workers = n_az // 2
    blocks = workers // (depth * n_rad)
    tiles = lanes // TILE
    quads = tiles // GROUPS
    own = tiles // (2 * blocks)
    span = own + 2
    parts = span + 1
    rows = span * TILE
    MESH = pl.DeviceIdType.MESH
    me = lax.axis_index("az")
    core = lax.axis_index("rad")
    half = lax.rem(me // depth, n_rad)
    layer = lax.rem(me, depth)
    block = me // plane - 1
    works = jnp.logical_and(block >= 0, block < blocks)
    place = (half * blocks + block) * 2 + core
    partner = {"rad": 1 - core}
    here = half == core
    stays = jnp.logical_and(works, here)

    def remote(src, dst, send, recv, where):
        return pltpu.make_async_remote_copy(
            src_ref=src, dst_ref=dst, send_sem=send, recv_sem=recv, device_id=where, device_id_type=MESH
        )

    def arrived(dst, recv):
        return pltpu.make_async_copy(dst, dst, recv)

    barrier = pltpu.get_barrier_semaphore()

    @pl.when(works)
    def _():
        for k in range(n_az - 1):
            pl.semaphore_signal(
                barrier, inc=1, device_id={"az": k + (me <= k).astype(jnp.int32), "rad": half}, device_id_type=MESH
            )

    pl.semaphore_signal(barrier, inc=1, device_id=partner, device_id_type=MESH)
    loads = [pltpu.make_async_copy(x_in.at[:, l], x.at[:, l], load_sem.at[l]) for l in range(depth)]
    for load in loads:
        load.start()
    table = pltpu.make_async_copy(shifts_in, shifts, table_sem)
    table.start()

    lane = lax.broadcasted_iota(jnp.int32, (TILE, lanes), 1)
    row = lax.broadcasted_iota(jnp.int32, (TILE, lanes), 0)
    lane_of = {n * TILE: lax.broadcasted_iota(jnp.int32, (n * TILE, lanes), 1) for n in (1, 2, own)}
    group = lane // width
    spin = me * TILE
    unspin = lax.rem(lanes - spin, lanes)

    def rows_of(f, l):
        return [x[f, l, pl.ds(u, width // GROUPS, stride=GROUPS), :] for u in range(GROUPS)]

    for l in range(depth):
        loads[l].wait()
        cells = jnp.concatenate([part for f in range(GROUPS) for part in rows_of(f, l)], axis=0)
        T4[l, 1 : tiles + 1] = pltpu.roll(cells.T, spin, 1).reshape(tiles, TILE, lanes)
    energy = [part for l in range(depth) for part in rows_of(4, l)]
    turned = jnp.concatenate(energy * (lanes // (depth * width)), axis=0).T.reshape(tiles, TILE, lanes)
    for l in range(depth):
        for m in range(quads):
            packed = turned[GROUPS * m] if l == 0 else lane_rows(turned[GROUPS * m], -width * l)
            for g in range(1, GROUPS):
                packed = jnp.where(group == g, lane_rows(turned[GROUPS * m + g], width * (g - l)), packed)
            EP[l, 1 + m] = packed

    @pl.when(core == 0)
    def _():
        for l in range(depth):
            T4[l, 0] = jnp.broadcast_to(T4[l, 1, 0:1], (TILE, lanes))
            EP[l, 0] = jnp.broadcast_to(lane_rows(EP[l, 1], -width)[0:1], (TILE, lanes))

    @pl.when(core == 1)
    def _():
        for l in range(depth):
            T4[l, tiles + 1] = jnp.broadcast_to(T4[l, tiles, TILE - 1 : TILE], (TILE, lanes))
            EP[l, quads + 1] = jnp.broadcast_to(lane_rows(EP[l, quads], width)[TILE - 1 : TILE], (TILE, lanes))

    def energy_of(l, m):
        joined = jnp.where(group == GROUPS - 1, EP[l, m], EP[l, m + 1])
        return pltpu.roll(joined, lax.rem(spin + width, lanes), 1)

    def stage(l, s, c):
        first = 2 * own * s + c * (own + 1)
        if c == 0:
            M[l, s, c, 0], M[l, s, c, 1] = energy_of(l, 2 * s), energy_of(l, 2 * s + 1)
            M[l, s, c, 2 : own + 2] = T4[l, first : first + own]
        else:
            M[l, s, c, 1 : own + 1] = T4[l, first + 1 : first + own + 1]
            M[l, s, c, own + 1], M[l, s, c, own + 2] = energy_of(l, 2 * s + 1), energy_of(l, 2 * s + 2)

    late = ((0, 0), (blocks - 1, 1))
    for l in range(depth):
        for s in range(blocks):
            for c in range(2):
                M[l, s, c, (parts - 1) * (1 - c)] = T4[l, 2 * own * s + own + c]
                if (s, c) not in late:
                    stage(l, s, c)

    table.wait()
    pl.semaphore_wait(barrier, jnp.where(stays, 2 * (workers // n_rad) - 1, 2 * (workers // n_rad) + 1))

    targets = [(ks, kl, kc) for ks in (0, 1) for kc in (1, 0) for kl in (1, 0)]

    def send(index, first):
        ks, kl, kc = targets[index]
        s = lax.rem(me // plane + 1 + ks, blocks)
        l = lax.rem(layer + kl, depth)
        c = lax.rem(core + kc, 2)
        if first:
            src, dst = M.at[l, s, c, (parts - 1) * (1 - c)], W.at[me, (parts - 1) - (parts - 2) * c]
            sems = out_send.at[0, index], out_recv.at[0, me]
        else:
            src, dst = M.at[l, s, c, pl.ds(c, parts - 1)], W.at[me, pl.ds(2 * c, parts - 1)]
            sems = out_send.at[1, index], out_recv.at[1, me]
        sent = remote(src, dst, *sems, {"az": (1 + s) * plane + core * depth + l, "rad": c})
        is_late = s == c * (blocks - 1)
        return sent, None if ks or kl or kc else pltpu.make_async_copy(src, dst, sems[1]), is_late

    def start(first, when=None):
        for index in range(len(targets)):
            sent, within, is_late = send(index, first)
            if within is None and when is None:
                sent.start()
                continue
            now = True if when is None else when(is_late)
            for copy, also in ((sent, None),) if within is None else ((within, stays), (sent, jnp.logical_not(stays))):

                @pl.when(now if also is None else jnp.logical_and(now, also))
                def _():
                    copy.start()

    start(True)

    swap_shift = remote(shifts, other, shift_sem.at[0], shift_sem.at[1], partner)
    swap_shift.start()

    def swaps(l, up):
        src = (tiles, quads) if up else (1, 1)
        dst = (0, 0) if up else (tiles + 1, quads + 1)
        return [
            remote(T4.at[l, src[0]], T4.at[l, dst[0]], swap_sem.at[0, l], swap_sem.at[1, l], partner),
            remote(EP.at[l, src[1]], EP.at[l, dst[1]], swap_sem.at[2, l], swap_sem.at[3, l], partner),
        ]

    @pl.when(core == 0)
    def _():
        for l in range(depth):
            for copy in swaps(l, True):
                copy.start()

    @pl.when(core == 1)
    def _():
        for l in range(depth):
            for copy in swaps(l, False):
                copy.start()

    start(False, jnp.logical_not)
    for l in range(depth):
        for copy in swaps(l, True):
            copy.wait_recv()
    for l in range(depth):
        for s, c in late:
            stage(l, s, c)
    start(False, lambda is_late: is_late)
    swap_shift.wait_recv()

    def passes(k):
        q = lax.rem(me // plane + k, GROUPS)
        ahead = pl.ds(q * plane, plane)
        src, dst = W.at[ahead, (parts - 1) - (parts - 2) * core], W.at[ahead, parts * core]
        return remote(src, dst, pass_send.at[k], pass_recv.at[q], partner)

    def passed(q):
        return arrived(W.at[pl.ds(q * plane, plane), parts * (1 - core)], pass_recv.at[q])

    order = range(n_az)

    def back(n):
        if n == 0:
            i = 0
        elif n < plane:
            i = 1 + lax.rem(me + n - 1, plane - 1)
        elif n < 2 * plane:
            i = plane + lax.rem(me + n + 1, plane)
        else:
            i = 2 * plane + lax.rem(me + n + 1, 2 * plane)
        src, dst = B.at[i], R.at[layer, block, core]
        sems = back_send.at[n], back_recv.at[(layer * blocks + block) * 2 + core]
        sent = remote(src, dst, *sems, {"az": i, "rad": half})
        return sent, pltpu.make_async_copy(src, dst, sems[1]) if n in (2 * plane - 1, n_az - 1) else None, me == i

    @pl.when(works)
    def _():
        lower = jnp.full((1, lanes), core, jnp.int32) == 0
        mine, theirs = shifts[...], other[...]
        for c in range(2):
            part = jnp.where(lower, mine if c == 0 else theirs, theirs if c == 0 else mine)
            along_lanes = jnp.broadcast_to(part.astype(jnp.float32), (lanes, lanes)).T.astype(jnp.int32)
            SC[TILE + c * lanes : TILE + (c + 1) * lanes] = along_lanes
        SC[0:TILE] = jnp.zeros((TILE, lanes), jnp.int32)
        SC[TILE + 2 * lanes :] = jnp.zeros((TILE, lanes), jnp.int32)
        AM[...] = SC[pl.ds(pl.multiple_of(place * own * TILE, TILE), rows)]
        at = jnp.full((TILE, lanes), place, jnp.int32)
        is_low = at == 0
        is_high = at == 2 * blocks * n_rad - 1

        def tools_of(span, start):
            amounts = [AM[pl.ds(start + w, TILE, stride=span), :] for w in range(span)]
            odd = [(amount & 1) != 0 for amount in amounts]
            two = [(amount & 2) != 0 for amount in amounts]
            source = [
                [
                    (lane - amounts[w] // GROUPS - jnp.where(u < (amounts[w] & (GROUPS - 1)), 1, 0)) & (lanes - 1)
                    for w in range(span)
                ]
                for u in range(GROUPS)
            ]

            def rotate(field):
                done = [[None] * span for _ in range(GROUPS)]
                for w in range(span):
                    near_by = [jnp.where(odd[w], field[u - 1][w], field[u][w]) for u in range(GROUPS)]
                    for u in range(GROUPS):
                        chosen = jnp.where(two[w], near_by[u - 2], near_by[u])
                        done[u][w] = jnp.take_along_axis(chosen, source[u][w], axis=1)
                return done

            end_low, end_high = TILE - start, TILE * (1 + own) - 1 - start

            def replaced(field, at_row, by_row, where):
                w, sub = by_row % span, by_row // span
                mask = jnp.logical_and(where, row == at_row // span)
                for u in range(GROUPS):
                    end = jnp.broadcast_to(field[u][w][sub : sub + 1], (TILE, lanes))
                    field[u][at_row % span] = jnp.where(mask, end, field[u][at_row % span])

            def edged(field):
                field = [list(tiles_u) for tiles_u in field]
                for k in (1, 2):
                    replaced(field, end_low - k, end_low, is_low)
                    replaced(field, end_high + k, end_high, is_high)
                return field

            return rotate, edged

        rotate, edged = tools_of(span, 0)
        rotate_core, edged_core = tools_of(span - 1, GROUPS)

        for k in (0, 1, 3, 2):
            for j in range(plane):
                i = lax.rem(me // plane + k, GROUPS) * plane + lax.rem(me + j, plane)
                arrived(W.at[i, (parts - 1) - (parts - 2) * core], out_recv.at[0, i]).wait()
            passes(k).start()

        def unpack(pieces):
            return [lane_rows(p, -TILE * g) for g, p in enumerate(exchange(pieces, lane_of[pieces[0].shape[0]]))]

        def settle(slot, count, at_row):
            pieces = [W[i, pl.ds(slot, count)].reshape(count * TILE, lanes) for i in range(n_az)]
            for g, piece in enumerate(unpack(pieces)):
                F[g, pl.ds(pl.multiple_of(at_row, TILE), count * TILE)] = piece

        for q in range(GROUPS):
            passed(q).wait()
        settle((parts - 1) * (1 - core), 2, own * TILE * (1 - core))
        for k in (0, 1, 3, 2):
            for j in range(plane):
                i = lax.rem(me // plane + k, GROUPS) * plane + lax.rem(me + j, plane)
                arrived(W.at[i, pl.ds(2 * core, parts - 1)], out_recv.at[1, i]).wait()
        settle(2, own, 2 * TILE * core)
        pieces = [W[i, pl.ds((parts - 1) * core, 2)].reshape(2 * TILE, lanes) for i in range(n_az)]
        for g, piece in enumerate(unpack(pieces)):
            for t in range(2):
                w, u = GROUPS * t + g // GROUPS, g % GROUPS
                if w < span:
                    FE[u, w * TILE : (w + 1) * TILE] = piece[t * TILE : (t + 1) * TILE]

        def source_of(f, u):
            return FE.at[u] if f == GROUPS else F.at[GROUPS * f + u]

        state = [
            [[source_of(f, u)[pl.ds(w, TILE, stride=span), :] for w in range(span)] for u in range(GROUPS)]
            for f in range(fields)
        ]
        step = advect_all(state)
        state = [edged(rotate(step(field))) for field in state]
        mr, mp, en = push_all(state)
        for f, field in enumerate((state[0], mr, mp, state[3], en)):
            for u in range(GROUPS):
                for w in range(span):
                    K[GROUPS * f + u, pl.ds(w, TILE, stride=span), :] = field[u][w]

        inner = range(span - 1)
        state = [
            edged_core(
                [
                    [K[GROUPS * f + u, pl.ds(GROUPS + w, TILE, stride=span - 1), :] for w in inner]
                    for u in range(GROUPS)
                ]
            )
            for f in range(fields)
        ]
        step = advect_all(state)
        state = [edged_core(rotate_core(step(field))) for field in state]
        mr, mp, en = push_all(state)
        for f, field in enumerate((state[0], mr, mp, state[3], en)):
            for u in range(GROUPS):
                for w in inner:
                    G[GROUPS * f + u, pl.ds(GROUPS + w, TILE, stride=span - 1), :] = field[u][w]

        mine = slice(TILE, (1 + own) * TILE)
        kept = [lane_rows(G[g, mine], TILE * g) for g in range(GROUPS * GROUPS)]
        for i, piece in enumerate(exchange(kept, lane_of[own * TILE])):
            B[i, : own * TILE] = piece
        kept = [
            lane_rows(G[GROUPS * GROUPS + u, (1 + t) * TILE : (2 + t) * TILE], TILE * (GROUPS * t + u))
            for t in range(own)
            for u in range(GROUPS)
        ]
        for i, piece in enumerate(exchange(kept, lane)):
            B[i, own * TILE :] = piece

        for n in order:
            sent, within, mine = back(n)
            if within is None:
                sent.start()
                continue

            @pl.when(jnp.logical_and(here, mine))
            def _():
                within.start()

            @pl.when(jnp.logical_not(jnp.logical_and(here, mine)))
            def _():
                sent.start()

    for l in range(depth):
        for s in range(blocks):
            for c in range(2):
                arrived(R.at[l, s, c], back_recv.at[(l * blocks + s) * 2 + c]).wait()
        pieces = [R[l, s, c, : own * TILE] for s in range(blocks) for c in range(2)]
        cells = pltpu.roll(jnp.concatenate(pieces, axis=0), unspin, 1).T
        for f in range(GROUPS):
            for u in range(GROUPS):
                g = GROUPS * f + u
                out[f, l, pl.ds(u, TILE, stride=GROUPS), :] = cells[g * TILE : (g + 1) * TILE]
    pieces = []
    for s in range(blocks):
        for c in range(2):
            both = [pltpu.roll(R[l, s, c, own * TILE :], unspin, 1) for l in range(depth)]
            for g in range(GROUPS):
                piece = lane_rows(both[0], -width * g)
                for l in range(1, depth):
                    piece = jnp.where(group == l, lane_rows(both[l], width * (l - g)), piece)
                pieces.append(piece)
    cells = jnp.concatenate(pieces, axis=0).T
    for l in range(depth):
        for u in range(GROUPS):
            g = GROUPS * l + u
            out[4, l, pl.ds(u, TILE, stride=GROUPS), :] = cells[g * TILE : (g + 1) * TILE]

    swap_shift.wait_send()
    for l in range(depth):
        for copy in swaps(l, True):
            copy.wait_send()
    for first in (True, False):
        for index in range(len(targets)):
            sent, within, _ = send(index, first)
            if within is None:
                sent.wait_send()
            else:

                @pl.when(jnp.logical_not(stays))
                def _():
                    sent.wait_send()

    @pl.when(works)
    def _():
        for k in range(GROUPS):
            passes(k).wait_send()
        for n in order:
            sent, within, mine = back(n)
            if within is None:
                sent.wait_send()
                continue

            @pl.when(jnp.logical_not(jnp.logical_and(here, mine)))
            def _():
                sent.wait_send()


def turned_body(mesh, state, shifts):
    n_az, n_rad = mesh.shape["az"], mesh.shape["rad"]
    fields, depth, width, lanes = state.shape
    blocks = n_az // 2 // (depth * n_rad)
    tiles = lanes // TILE
    own = tiles // (2 * blocks)
    vmem = lambda *shape: pltpu.VMEM(shape, jnp.float32)
    dma = pltpu.SemaphoreType.DMA
    tile = (TILE, lanes)
    return pl.pallas_call(
        functools.partial(turned_kernel, n_az, n_rad),
        out_shape=pltpu.VMEM(state.shape, state.dtype),
        in_specs=[pl.BlockSpec(memory_space=pl.ANY)] * 2,
        out_specs=pl.BlockSpec(memory_space=pltpu.VMEM),
        scratch_shapes=[
            vmem(fields, depth, width, lanes),
            vmem(depth, tiles + 2, *tile),
            vmem(depth, tiles // GROUPS + 2, *tile),
            vmem(depth, blocks, 2, own + 3, *tile),
            vmem(n_az, own + 4, *tile),
            pltpu.VMEM((1, lanes), jnp.int32),
            pltpu.VMEM((1, lanes), jnp.int32),
            pltpu.VMEM((2 * lanes + 2 * TILE, lanes), jnp.int32),
            pltpu.VMEM(((own + 2) * TILE, lanes), jnp.int32),
            vmem(GROUPS * GROUPS, (own + 2) * TILE, lanes),
            vmem(GROUPS, (own + 2) * TILE, lanes),
            vmem(GROUPS * fields, (own + 2) * TILE, lanes),
            vmem(GROUPS * fields, (own + 2) * TILE, lanes),
            vmem(n_az, (own + 1) * TILE, lanes),
            vmem(depth, blocks, 2, (own + 1) * TILE, lanes),
            dma((depth,)),
            dma(()),
            dma((2,)),
            dma((4, depth)),
            dma((2, n_az)),
            dma((2, n_az)),
            dma((GROUPS,)),
            dma((GROUPS,)),
            dma((n_az,)),
            dma((n_az,)),
        ],
        compiler_params=pltpu.CompilerParams(collective_id=0, has_side_effects=True),
    )(state, shifts.reshape(1, -1))


def turns(mesh, state):
    n_az, n_rad = mesh.shape["az"], mesh.shape["rad"]
    fields, depth, width, lanes = state.shape
    tiles = lanes // TILE
    return (
        n_rad == 2
        and depth == 2
        and fields == GROUPS + 1
        and width == GROUPS * TILE
        and lanes == n_az * TILE
        and n_az == GROUPS * GROUPS
        and tiles == n_az
        and SMAX <= lanes
    )


def choose(mesh, state, shifts):
    return (turned_body if turns(mesh, state) else body)(mesh, state, shifts)


def solution(mesh):
    in_specs = (P(None, None, "az", "rad"), P("rad"))
    out_specs = P(None, None, "az", "rad")
    return jax.shard_map(
        functools.partial(choose, mesh), mesh=mesh, in_specs=in_specs, out_specs=out_specs, check_vma=False
    )
```
